32 devices in a mesh: rows: 16 (over z, y, core), seq: 2 (over x).
Axes of the slice: x: 2, y: 2, z: 4, core: 2. Of those that a mesh axis runs over, the one named last changes fastest.
Arguments:
- block_input: bfloat16 [16, 2048, 1024], P('rows', 'seq'), may hold values from -6 to 6
- lengths: int32 [16, 4], P('rows'), may hold values from 1 to 1024, 2048 in all within a row
- norm_gain: bfloat16 [1024], P('rows'), may hold values from 0.099609375 to 1.8984375
- norm_bias: bfloat16 [1024], P('rows'), may hold values from -2 to 2
- w_qkv: bfloat16 [1024, 3072], P('rows'), may hold values from -0.1875 to 0.1875
- w_attn_out: bfloat16 [1024, 1024], P('rows'), may hold values from -0.75 to 0.75
- w_fc_in: bfloat16 [1024, 4096], P('rows'), may hold values from -0.1875 to 0.1875
- b_fc_in: bfloat16 [4096], P('rows'), may hold values from -3 to 3
- w_fc_out: bfloat16 [4096, 1024], P('rows'), may hold values from -0.09375 to 0.09375
- b_fc_out: bfloat16 [1024], P('rows'), may hold values from -2 to 2
- cotangent: bfloat16 [16, 2048, 1024], P('rows', 'seq'), may hold values from -15 to 15
Outputs:
- block_output: bfloat16 [16, 2048, 1024], P('rows', 'seq')
- grad_input: float32 [16, 2048, 1024], P('rows', 'seq')
- grad_norm_gain: float32 [1024], P('rows')
- grad_norm_bias: float32 [1024], P('rows')
- grad_w_qkv: float32 [1024, 3072], P('rows')
- grad_w_attn_out: float32 [1024, 1024], P('rows')
- grad_w_fc_in: float32 [1024, 4096], P('rows')
- grad_b_fc_in: float32 [4096], P('rows')
- grad_w_fc_out: float32 [4096, 1024], P('rows')
- grad_b_fc_out: float32 [1024], P('rows')
The draws below stay inside these ranges and needn't reach their ends.
Inputs may be any that keep to these rules, and one draw needn't show every extreme that they name: The 4 lengths of a row sum to 2048, and the longest protein of every row has exactly 1024 residues.
All inputs are finite; a program needn't handle non-finite values.
Results may differ from the reference program's by a relative error of at most 0.017.
Values may be sent and summed in bfloat16 or wider, within the bound.
A program may use at most 576 MiB of HBM per device.

```python
import math
import jax
import jax.numpy as jnp
import numpy as np
from jax import lax

D = 1024
HEADS = 16
HEAD = 64
ROT = 32
FF = 4096
MOST = 1024
ROWS = 16
ROW = 2048
SEGS = 4


def draw_cotangent(key, part):
    shape = (ROWS, ROW, D)
    base = jnp.clip(jax.random.normal(key, shape, jnp.float32), -5.0, 5.0)
    rising = 1.0 + 2.0 * jnp.arange(ROWS, dtype=jnp.float32) / (ROWS - 1)
    return (base * rising[:, None, None]).astype(jnp.bfloat16)


def block_scale(key, dims, split, least, top_value):
    loudness = 1.0
    for dim, parts in split:
        heights = jax.random.uniform(jax.random.fold_in(jax.random.fold_in(key, 6), dim), (parts,), jnp.float32, least / len(split), top_value / len(split))
        loudness = loudness * jnp.repeat(jnp.exp(heights), dims[dim] // parts).reshape((-1,) + (1,) * (len(dims) - 1 - dim))
    return loudness


def split_up(amount, total, most, lean):
    portions = [(1 << 20) // math.isqrt(rank ** lean) + 1 for rank in range(2, amount + 1)]
    rest, holding = total - most - (amount - 1), [1] * (amount - 1)
    while rest > 0:
        movable = [i for i in range(amount - 1) if holding[i] < most]
        whole, budget = sum([portions[i] for i in movable]), rest
        for i in movable:
            extra = min(most - holding[i], max(1, budget * portions[i] // whole), rest)
            holding[i] = holding[i] + extra
            rest = rest - extra
    return np.array([most] + holding)


def uneven_parts(key, count, total, most, skew):
    if count == 2:
        one = jax.random.randint(key, (), max(1, total - most), min(most, total - 1) + 1)
        return jnp.stack([one, total - one])
    tallies = jnp.asarray(split_up(count, total, most, skew), jnp.int32)
    couples = (count - 1) // 2
    giver, taker = tallies[1:1 + 2 * couples:2], tallies[2:2 + 2 * couples:2]
    room = jnp.minimum(giver - 1, most - taker)
    moved = jax.random.randint(jax.random.fold_in(key, 1), (couples,), 0, 1 << 20) % (room + 1)
    tallies = tallies.at[1:1 + 2 * couples:2].set(giver - moved).at[2:2 + 2 * couples:2].set(taker + moved)
    return tallies[jax.random.permutation(jax.random.fold_in(key, 2), count)]


def scatter_about(stream_key, shape, deviation, bound, split=(), kind=jnp.bfloat16):
    values = jax.random.normal(stream_key, shape, jnp.float32) * deviation
    if len(split) > 0:
        values = block_scale(stream_key, shape, split, -0.22, 0.18) * values
    return jnp.clip(values, min=-bound, max=bound).astype(kind)


def setup_inputs(seed: int = 0) -> dict:
    seeds = jax.random.split(jax.random.key(seed), 12)
    return {
        "block_input": scatter_about(seeds[0], (ROWS, ROW, D), 1.0, 6.0, ((0, 16), (1, 2))),
        "lengths": jax.vmap(lambda own: uneven_parts(own, SEGS, ROW, MOST, 1))(jax.random.split(seeds[1], ROWS)).reshape((ROWS, SEGS)).astype(jnp.int32),
        "norm_gain": jnp.clip(1.0 + 0.18 * jax.random.normal(seeds[2], (D,), jnp.float32), 0.099609375, 1.8984375).astype(jnp.bfloat16),
        "norm_bias": scatter_about(seeds[3], (D,), 0.3, 2.0, ((0, 16),)),
        "w_qkv": scatter_about(seeds[4], (D, 3 * D), D ** -0.5, 0.1875, ((0, 16),)),
        "w_attn_out": scatter_about(seeds[5], (D, D), (D // 16) ** -0.5, 0.75, ((0, 16),)),
        "w_fc_in": scatter_about(seeds[6], (D, FF), D ** -0.5, 0.1875, ((0, 16),)),
        "b_fc_in": scatter_about(seeds[7], (FF,), 0.5, 3.0, ((0, 16),)),
        "w_fc_out": scatter_about(seeds[8], (FF, D), FF ** -0.5, 0.09375, ((0, 16),)),
        "b_fc_out": scatter_about(seeds[9], (D,), 0.3, 2.0, ((0, 16),)),
        "cotangent": draw_cotangent(jax.random.fold_in(seeds[11], 71), 0),
    }


@jax.custom_vjp
def low(v):
    return lax.optimization_barrier(v.astype(jnp.bfloat16)).astype(jnp.float32)

@jax.custom_vjp
def low_back(v):
    return v

def low_keep(v):
    return (low(v), None)

def low_pass(kept, grad):
    return (grad,)

def back_keep(v):
    return (v, None)

def back_low(kept, grad):
    return (low(grad),)
low.defvjp(low_keep, low_pass)
low_back.defvjp(back_keep, back_low)
EPS = 1e-05
GELU_COEF = 0.7978845608028654
HIGHEST = lax.Precision.HIGHEST

def normalize(values, norm_gain, norm_bias):
    row_mean = lax.optimization_barrier(jnp.mean(values, axis=1, keepdims=True))
    centered = values - row_mean
    spread = lax.optimization_barrier(jnp.mean(centered * centered, axis=1, keepdims=True))
    return centered * lax.rsqrt(spread + EPS) * norm_gain + norm_bias

def gelu_tanh(values):
    return 0.5 * values * (1.0 + jnp.tanh(GELU_COEF * (values + 0.044715 * values * values * values)))

def layout(row_lengths, where_at):
    seg_ends = jnp.cumsum(row_lengths, dtype=jnp.int32)
    seg_starts = seg_ends - row_lengths
    segment = lax.optimization_barrier(jnp.sum((seg_ends[None, :] <= where_at[:, None]).astype(jnp.int32), axis=1, dtype=jnp.int32))
    chosen = segment[:, None] == jnp.arange(row_lengths.shape[0], dtype=jnp.int32)[None, :]
    seg_begin = lax.optimization_barrier(jnp.sum(jnp.where(chosen, seg_starts[None, :], 0), axis=1, dtype=jnp.int32))
    return (segment, (where_at - seg_begin).astype(jnp.int32))

def rotate(vectors, position):
    tokens = vectors.shape[0]
    head_count = vectors.shape[1]
    half_rot = ROT // 2
    freqs = 10000.0 ** (-2.0 * jnp.arange(half_rot, dtype=jnp.float32) / ROT)
    angles = position.astype(jnp.float32)[:, None] * freqs[None, :]
    cosine = jnp.cos(angles)[:, None, :]
    sine = jnp.sin(angles)[:, None, :]
    paired = vectors[:, :, :ROT].reshape(tokens, head_count, half_rot, 2)
    evens = paired[..., 0]
    odds = paired[..., 1]
    turned = jnp.stack([evens * cosine - odds * sine, odds * cosine + evens * sine], axis=-1)
    return jnp.concatenate([turned.reshape(tokens, head_count, ROT), vectors[:, :, ROT:]], axis=2)

def row_forward(values, norm_gain, norm_bias, w_qkv, w_attn_out, w_fc_in, b_fc_in, w_fc_out, b_fc_out, segment, position):
    tokens = values.shape[0]
    normed = low(normalize(values, norm_gain, norm_bias))
    mixed = low_back(jnp.dot(normed, w_qkv, precision=HIGHEST))
    queries = low(rotate(mixed[:, :D].reshape(tokens, HEADS, HEAD), position))
    keys_all = low(rotate(mixed[:, D:2 * D].reshape(tokens, HEADS, HEAD), position))
    values_all = low(mixed[:, 2 * D:].reshape(tokens, HEADS, HEAD))
    block_rows = min(512, tokens)
    index_all = jnp.arange(tokens, dtype=jnp.int32)
    score_scale = HEAD ** (-0.5)

    def attend(block_index):
        begin_row = block_index * block_rows
        query_block = lax.dynamic_slice_in_dim(queries, begin_row, block_rows, 0)
        query_index = lax.dynamic_slice_in_dim(index_all, begin_row, block_rows, 0)
        query_segment = lax.dynamic_slice_in_dim(segment, begin_row, block_rows, 0)
        allowed = (query_segment[:, None] == segment[None, :]) & (query_index[:, None] >= index_all[None, :])
        scores = low_back(jnp.einsum('qhd,khd->hqk', query_block, keys_all, precision=HIGHEST) * score_scale)
        scores = jnp.where(allowed[None], scores, -1e+30)
        row_max = lax.optimization_barrier(jnp.max(scores, axis=2, keepdims=True))
        exps = jnp.exp(scores - row_max)
        probs = exps / lax.optimization_barrier(jnp.sum(exps, axis=2, keepdims=True))
        return jnp.einsum('hqk,khd->qhd', low(probs), values_all, precision=HIGHEST)
    attended = lax.map(jax.checkpoint(attend), jnp.arange(tokens // block_rows, dtype=jnp.int32))
    attended = low(low_back(attended.reshape(tokens, D)))
    branch = jnp.dot(attended, w_attn_out, precision=HIGHEST)
    pre = low_back(jnp.dot(normed, w_fc_in, precision=HIGHEST) + b_fc_in)
    hidden = low(gelu_tanh(pre))
    return values + branch + jnp.dot(hidden, w_fc_out, precision=HIGHEST) + b_fc_out

def reference(block_input, lengths, norm_gain, norm_bias, w_qkv, w_attn_out, w_fc_in, b_fc_in, w_fc_out, b_fc_out, cotangent):
    weights = tuple((weight_arg.astype(jnp.float32) for weight_arg in (norm_gain, norm_bias, w_qkv, w_attn_out, w_fc_in, b_fc_in, w_fc_out, b_fc_out)))
    zeros = tuple((jnp.zeros(weight_arg.shape, jnp.float32) for weight_arg in weights))

    def one_row(totals, row_item):
        row_input, row_lengths, row_cot = row_item
        tokens = row_input.shape[0]
        segment, position = layout(row_lengths, jnp.arange(tokens, dtype=jnp.int32))

        def forward(values, *params):
            return row_forward(values, *params, segment, position)
        result, pullback = jax.vjp(forward, row_input.astype(jnp.float32), *weights)
        grads = pullback(row_cot.astype(jnp.float32))
        totals = tuple((a_sum + b_term for a_sum, b_term in zip(totals, grads[1:])))
        return (totals, (result.astype(jnp.bfloat16), grads[0]))
    totals, (outputs, grad_rows) = lax.scan(one_row, zeros, (block_input, lengths, cotangent))
    return (outputs, grad_rows) + totals
```

```python
import functools

import jax
import jax.numpy as jnp
import numpy as np
from jax import lax
from jax.experimental import pallas as pl
from jax.experimental.pallas import tpu as pltpu
from jax.sharding import PartitionSpec as P

HEADS = 16
HEAD = 64
ROT = 32
EPS = 1e-05
GELU_COEF = 0.7978845608028654

NEG = -1e30
BQ = 256

def dot_t(a, b):
    return lax.dot_general(a, b, (((1,), (1,)), ((), ())), preferred_element_type=jnp.float32)

def dot_n(a, b):
    return lax.dot_general(a, b, (((1,), (0,)), ((), ())), preferred_element_type=jnp.float32)

def dot_c(a, b):
    return lax.dot_general(a, b, (((0,), (0,)), ((), ())), preferred_element_type=jnp.float32)

def attention_kernel(pairs, tokens, lows, start_col, start_row, cos_ref, sin_ref, q_ref, k_ref, v_ref, do_ref,
                     out_ref, dq_ref, dk_ref, dv_ref, bias, bias_t, dk_acc, dv_acc, m_sc, l_sc, acc_sc, dq_sc):
    blocks = tokens // BQ
    span = blocks + 1
    lane = lax.broadcasted_iota(jnp.int32, (BQ, 128), 1)
    even = lane < 64

    @pl.when(pl.program_id(0) == 0)
    def _():
        for qb in range(blocks):
            start_c = start_col[qb * BQ:(qb + 1) * BQ, :]
            start_r = start_row[:, qb * BQ:(qb + 1) * BQ]
            q_c = tokens + qb * BQ + lax.broadcasted_iota(jnp.int32, (BQ, BQ), 0)
            q_r = tokens + qb * BQ + lax.broadcasted_iota(jnp.int32, (BQ, BQ), 1)

            def fill(kb, _):
                k_r = kb * BQ + lax.broadcasted_iota(jnp.int32, (BQ, BQ), 1)
                k_c = kb * BQ + lax.broadcasted_iota(jnp.int32, (BQ, BQ), 0)
                slot = qb * span + kb - qb
                bias[slot] = jnp.where((k_r >= start_c) & (k_r <= q_c), 0.0, NEG)
                bias_t[slot] = jnp.where((k_c >= start_r) & (k_c <= q_r), 0.0, NEG)
                return 0
            lax.fori_loop(lows[qb], blocks + qb + 1, fill, 0)

    dk_acc[...] = jnp.zeros_like(dk_acc)
    dv_acc[...] = jnp.zeros_like(dv_acc)
    heads = 2 * pairs

    def one_q(qb, _):
        q_rows = pl.ds(pl.multiple_of(qb * BQ, BQ), BQ)
        low = lows[qb]
        high = blocks + qb + 1
        q_h = []
        for p in range(pairs):
            q = q_ref[q_rows, p * 128:(p + 1) * 128]
            q_h += [jnp.where(even, q, 0), jnp.where(even, 0, q)]
        m_sc[...] = jnp.full_like(m_sc, NEG)
        l_sc[...] = jnp.zeros_like(l_sc)
        acc_sc[...] = jnp.zeros_like(acc_sc)

        def forward(kb, _):
            k_rows = pl.ds(pl.multiple_of(kb * BQ, BQ), BQ)
            b = bias[qb * span + kb - qb]
            for p in range(pairs):
                cols = slice(p * 128, (p + 1) * 128)
                k = k_ref[k_rows, cols]
                v = v_ref[k_rows, cols]
                outs, scales = [], []
                for h in (2 * p, 2 * p + 1):
                    s = dot_t(q_h[h], k) + b
                    m_old = m_sc[h]
                    m_new = jnp.maximum(m_old, jnp.max(s, axis=1, keepdims=True))
                    e = jnp.exp(s - m_new[:, :1])
                    a = jnp.exp(m_old - m_new)
                    l_sc[h] = a * l_sc[h] + jnp.sum(e, axis=1, keepdims=True)
                    m_sc[h] = m_new
                    outs.append(dot_n(e.astype(jnp.bfloat16), v))
                    scales.append(a)
                acc_sc[p] = acc_sc[p] * jnp.where(even, scales[0], scales[1]) + jnp.where(even, outs[0], outs[1])
            return 0
        lax.fori_loop(low, high, forward, 0)

        do_h, lse_r, delta_r = [], [], []
        for p in range(pairs):
            cols = slice(p * 128, (p + 1) * 128)
            o = acc_sc[p] / jnp.where(even, l_sc[2 * p], l_sc[2 * p + 1])
            out_ref[q_rows, cols] = o.astype(jnp.bfloat16)
            do = do_ref[q_rows, cols]
            prod = o * do.astype(jnp.float32)
            for h in (2 * p, 2 * p + 1):
                mine = even if h % 2 == 0 else ~even
                delta = jnp.sum(jnp.where(mine, prod, 0.0), axis=1, keepdims=True)
                lse = m_sc[h] + jnp.log(l_sc[h])
                both = jnp.where(even, lse, delta)
                turned = both.T
                lse_r.append(turned[0:1, :])
                delta_r.append(turned[64:65, :])
                do_h.append(jnp.where(mine, do, 0))
        dq_sc[...] = jnp.zeros_like(dq_sc)

        def backward(kb, _):
            k_rows = pl.ds(pl.multiple_of(kb * BQ, BQ), BQ)
            b = bias_t[qb * span + kb - qb]
            for p in range(pairs):
                cols = slice(p * 128, (p + 1) * 128)
                k = k_ref[k_rows, cols]
                v = v_ref[k_rows, cols]
                dqs, dks, dvs = [], None, None
                for h in (2 * p, 2 * p + 1):
                    s = dot_t(k, q_h[h]) + b
                    prob = jnp.exp(s - lse_r[h])
                    dp = dot_t(v, do_h[h])
                    ds = (prob * (dp - delta_r[h])).astype(jnp.bfloat16)
                    dv = dot_n(prob.astype(jnp.bfloat16), do_h[h])
                    dk = dot_n(ds, q_h[h])
                    dvs = dv if dvs is None else dvs + dv
                    dks = dk if dks is None else dks + dk
                    dqs.append(dot_c(ds, k))
                dv_acc[k_rows, cols] += dvs
                dk_acc[k_rows, cols] += dks
                dq_sc[p] += jnp.where(even, dqs[0], dqs[1])
            return 0
        lax.fori_loop(low, high, backward, 0)
        own_rows = pl.ds(pl.multiple_of(tokens + qb * BQ, BQ), BQ)
        for p in range(pairs):
            dq_ref[q_rows, p * 128:(p + 1) * 128] = unrotate(
                dq_sc[p] * 0.125, cos_ref[own_rows, :], sin_ref[own_rows, :]).astype(jnp.bfloat16)
        return 0
    lax.fori_loop(0, blocks, one_q, 0)

    def finish(kb, _):
        rows = pl.ds(pl.multiple_of(kb * BQ, BQ), BQ)
        for p in range(pairs):
            cols = slice(p * 128, (p + 1) * 128)
            dk_ref[rows, cols] = unrotate(dk_acc[rows, cols], cos_ref[rows, :], sin_ref[rows, :]).astype(jnp.bfloat16)
            dv_ref[rows, cols] = dv_acc[rows, cols].astype(jnp.bfloat16)
        return 0
    lax.fori_loop(0, 2 * blocks, finish, 0)

def swap_pairs(x):
    odd = lax.broadcasted_iota(jnp.int32, x.shape, 1) % 2 == 1
    n = x.shape[1]
    return jnp.where(odd, pltpu.roll(x, 1, 1), pltpu.roll(x, n - 1, 1))

def rotate(x, cosine, sine):
    return x * cosine + swap_pairs(x) * sine

def unrotate(x, cosine, sine):
    return x * cosine - swap_pairs(x) * sine

def attention(lows, starts, cosine, sine, mixed, d_out):
    tokens, width = d_out.shape
    pairs = 2
    wide = 128 * pairs
    groups = width // wide
    blocks = tokens // BQ
    whole = lambda shape: pl.BlockSpec(shape, lambda g, lows: (0,) * len(shape))
    own = pl.BlockSpec((tokens, wide), lambda g, lows: (0, g))
    both = pl.BlockSpec((2 * tokens, wide), lambda g, lows: (0, g))
    q_spec = pl.BlockSpec((tokens, wide), lambda g, lows: (1, g))
    k_spec = pl.BlockSpec((2 * tokens, wide), lambda g, lows: (0, groups + g))
    v_spec = pl.BlockSpec((2 * tokens, wide), lambda g, lows: (0, 2 * groups + g))
    bf, f32 = jnp.bfloat16, jnp.float32
    slots = blocks * (blocks + 1)
    one, two = jax.ShapeDtypeStruct((tokens, width), bf), jax.ShapeDtypeStruct((2 * tokens, width), bf)
    return pl.pallas_call(
        functools.partial(attention_kernel, pairs, tokens),
        out_shape=[one, one, two, two],
        grid_spec=pltpu.PrefetchScalarGridSpec(
            num_scalar_prefetch=1,
            grid=(groups,),
            in_specs=[whole((tokens, 1)), whole((1, tokens)), whole((2 * tokens, 128)), whole((2 * tokens, 128)),
                      q_spec, k_spec, v_spec, own],
            out_specs=[own, own, both, both],
            scratch_shapes=[pltpu.VMEM((slots, BQ, BQ), f32), pltpu.VMEM((slots, BQ, BQ), f32),
                            pltpu.VMEM((2 * tokens, wide), f32), pltpu.VMEM((2 * tokens, wide), f32),
                            pltpu.VMEM((2 * pairs, BQ, 128), f32), pltpu.VMEM((2 * pairs, BQ, 128), f32),
                            pltpu.VMEM((pairs, BQ, 128), f32), pltpu.VMEM((pairs, BQ, 128), f32)],
        ),
        compiler_params=pltpu.CompilerParams(vmem_limit_bytes=56 * 2**20),
        cost_estimate=pl.CostEstimate(flops=60 * 10**9, bytes_accessed=30 * 2**20, transcendentals=0),
        name="attention",
    )(lows, starts[:, None], starts[None, :], cosine, sine, mixed, mixed, mixed, d_out)


def qkv_kernel(cols, normed_ref, w_ref, cos_ref, sin_ref, out_ref):
    block = pl.program_id(1)
    mixed = dot_n(normed_ref[...], w_ref[...])

    @pl.when(block < 2 * cols)
    def _():
        scale = jnp.where(block < cols, 0.125, 1.0)
        cosine = cos_ref[...] * scale
        sine = sin_ref[...] * scale
        for i in range(mixed.shape[1] // 128):
            lanes = slice(i * 128, (i + 1) * 128)
            out_ref[:, lanes] = rotate(mixed[:, lanes], cosine, sine).astype(jnp.bfloat16)

    @pl.when(block >= 2 * cols)
    def _():
        out_ref[...] = mixed.astype(jnp.bfloat16)


def project(normed, w_qkv, cosine, sine):
    rows, width = normed.shape
    wide, tall = 512, 1024
    cols = width // wide
    return pl.pallas_call(
        functools.partial(qkv_kernel, cols),
        out_shape=jax.ShapeDtypeStruct((rows, 3 * width), jnp.bfloat16),
        grid=(rows // tall, 3 * cols),
        in_specs=[
            pl.BlockSpec((tall, width), lambda i, j: (i, 0)),
            pl.BlockSpec((width, wide), lambda i, j: (0, j)),
            pl.BlockSpec((tall, 128), lambda i, j: (i, 0)),
            pl.BlockSpec((tall, 128), lambda i, j: (i, 0)),
        ],
        out_specs=pl.BlockSpec((tall, wide), lambda i, j: (i, j)),
        compiler_params=pltpu.CompilerParams(vmem_limit_bytes=48 * 2**20),
        cost_estimate=pl.CostEstimate(flops=12 * 10**9, bytes_accessed=24 * 2**20, transcendentals=0),
        name="project",
    )(normed, w_qkv, cosine, sine)


def rope_tables(position):
    lane = np.arange(128) % HEAD
    freqs = np.where(lane < ROT, 10000.0 ** (-2.0 * (lane // 2) / ROT), 0.0).astype(np.float32)
    sign = np.where(lane % 2 == 0, -1.0, 1.0).astype(np.float32)
    angles = position.astype(jnp.float32)[:, None] * freqs[None, :]
    return jnp.cos(angles), jnp.sin(angles) * sign[None, :]


def layer_norm_stats(values):
    mean = jnp.mean(values, axis=1, keepdims=True)
    centered = values - mean
    spread = jnp.mean(centered * centered, axis=1, keepdims=True)
    scale = lax.rsqrt(spread + EPS)
    return centered * scale, scale


def body(block_input, lengths, norm_gain, norm_bias, w_qkv, w_attn_out, w_fc_in, b_fc_in, w_fc_out, b_fc_out, cotangent):
    f32, bf = jnp.float32, jnp.bfloat16
    gather = lambda w: lax.all_gather(w, "rows", axis=0, tiled=True)
    seqs = lax.axis_size("seq")
    prior_input = lax.ppermute(block_input[0], "seq", [(i, i + 1) for i in range(seqs - 1)])
    gain, bias = gather(norm_gain).astype(f32), gather(norm_bias).astype(f32)
    w_qkv_all, w_out_all = gather(w_qkv), gather(w_attn_out)
    w_in_all, b_in_all, w_back_all, b_back_all = gather(w_fc_in), gather(b_fc_in), gather(w_fc_out), gather(b_fc_out)
    inputs = block_input[0].astype(f32)
    tokens, width = inputs.shape
    own_lengths = lengths[0]
    count = own_lengths.shape[0]
    first = lax.axis_index("seq") * tokens
    index = first - tokens + jnp.arange(2 * tokens, dtype=jnp.int32)
    order = np.arange(count)
    ends = jnp.sum(jnp.where(order[None, :] <= order[:, None], own_lengths[None, :], 0), axis=1)
    begin = jnp.sum(jnp.where(ends[None, :] <= index[:, None], own_lengths[None, :], 0), axis=1)
    cosine, sine = rope_tables(index - begin)
    starts = (begin - first + tokens)[tokens:]
    lows = starts[::BQ] // BQ

    unit, scale = layer_norm_stats(inputs)
    normed = (unit * gain + bias).astype(bf)
    prior_unit, _ = layer_norm_stats(prior_input.astype(f32))
    normed_both = jnp.concatenate([(prior_unit * gain + bias).astype(bf), normed], axis=0)
    mixed = project(normed_both, w_qkv_all, cosine, sine)
    grad_out = cotangent[0]
    d_attended = jnp.dot(grad_out, w_out_all.T, preferred_element_type=f32).astype(bf)
    attended, d_q, d_k, d_v = attention(lows, starts, cosine, sine, mixed, d_attended)

    d_normed_both = jnp.dot(d_k, w_qkv_all[:, width:2 * width].T, preferred_element_type=f32) + jnp.dot(
        d_v, w_qkv_all[:, 2 * width:].T, preferred_element_type=f32)
    back = lax.ppermute(d_normed_both[:tokens].astype(bf), "seq", [(i + 1, i) for i in range(seqs - 1)])
    grad_w_qkv = jnp.concatenate([
        jnp.dot(normed.T, d_q, preferred_element_type=f32).astype(bf),
        jnp.dot(normed_both.T, d_k, preferred_element_type=f32).astype(bf),
        jnp.dot(normed_both.T, d_v, preferred_element_type=f32).astype(bf)], axis=1)
    grad_w_out = jnp.dot(attended.T, grad_out, preferred_element_type=f32).astype(bf)

    pre = jnp.dot(normed, w_in_all, preferred_element_type=f32) + b_in_all.astype(f32)
    turn = jnp.tanh(GELU_COEF * (pre + 0.044715 * pre * pre * pre))
    hidden = (0.5 * pre * (1.0 + turn)).astype(bf)
    slope = 0.5 * (1.0 + turn) + 0.5 * pre * (1.0 - turn * turn) * (GELU_COEF * (1.0 + 3 * 0.044715 * pre * pre))
    d_pre = (jnp.dot(grad_out, w_back_all.T, preferred_element_type=f32) * slope).astype(bf)
    grad_w_back = jnp.dot(hidden.T, grad_out, preferred_element_type=f32).astype(bf)
    grad_w_in = jnp.dot(normed.T, d_pre, preferred_element_type=f32).astype(bf)
    grad_b_back = jnp.sum(grad_out.astype(f32), axis=0)
    grad_b_in = jnp.sum(d_pre.astype(f32), axis=0)
    d_normed = jnp.dot(d_pre, w_in_all.T, preferred_element_type=f32)
    d_normed = d_normed + jnp.dot(d_q, w_qkv_all[:, :width].T, preferred_element_type=f32)
    d_normed = d_normed + d_normed_both[tokens:] + back.astype(f32)

    block_output = (inputs + jnp.dot(attended, w_out_all, preferred_element_type=f32)
                    + jnp.dot(hidden, w_back_all, preferred_element_type=f32) + b_back_all.astype(f32)).astype(bf)
    grad_gain = jnp.sum(d_normed * unit, axis=0)
    grad_bias = jnp.sum(d_normed, axis=0)
    d_unit = d_normed * gain
    d_input = (d_unit - jnp.mean(d_unit, axis=1, keepdims=True)
               - unit * jnp.mean(d_unit * unit, axis=1, keepdims=True)) * scale
    grad_input = d_input + grad_out.astype(f32)

    def reduce(term):
        share = lax.psum_scatter(term.astype(bf), "rows", scatter_dimension=0, tiled=True)
        return lax.psum(share, "seq").astype(f32)

    return (block_output[None], grad_input[None], reduce(grad_gain), reduce(grad_bias), reduce(grad_w_qkv),
            reduce(grad_w_out), reduce(grad_w_in), reduce(grad_b_in), reduce(grad_w_back), reduce(grad_b_back))


def solution(mesh):
    vector, matrix, tokens = P("rows"), P("rows", None), P("rows", "seq", None)
    in_specs = (tokens, matrix, vector, vector, matrix, matrix, matrix, vector, matrix, vector, tokens)
    out_specs = (tokens, tokens, vector, vector, matrix, matrix, matrix, vector, matrix, vector)
    return jax.shard_map(body, mesh=mesh, in_specs=in_specs, out_specs=out_specs, check_vma=False)
```

```python
import functools

import jax
import jax.numpy as jnp
import numpy as np
from jax import lax
from jax.experimental import pallas as pl
from jax.experimental.pallas import tpu as pltpu
from jax.sharding import PartitionSpec as P

HEADS = 16
HEAD = 64
ROT = 32
EPS = 1e-05
GELU_COEF = 0.7978845608028654

NEG = -1e30
BQ = 256

def dot_t(a, b):
    return lax.dot_general(a, b, (((1,), (1,)), ((), ())), preferred_element_type=jnp.float32)

def dot_n(a, b):
    return lax.dot_general(a, b, (((1,), (0,)), ((), ())), preferred_element_type=jnp.float32)

def dot_c(a, b):
    return lax.dot_general(a, b, (((0,), (0,)), ((), ())), preferred_element_type=jnp.float32)

def attention_kernel(pairs, tokens, lows, start_col, start_row, cos_ref, sin_ref, q_ref, k_ref, v_ref, do_ref,
                     out_ref, dq_ref, dk_ref, dv_ref, bias, bias_t, dk_acc, dv_acc, m_sc, l_sc, acc_sc, dq_sc):
    blocks = tokens // BQ
    span = blocks + 1
    lane = lax.broadcasted_iota(jnp.int32, (BQ, 128), 1)
    even = lane < 64

    @pl.when(pl.program_id(0) == 0)
    def _():
        for qb in range(blocks):
            start_c = start_col[qb * BQ:(qb + 1) * BQ, :]
            start_r = start_row[:, qb * BQ:(qb + 1) * BQ]
            q_c = tokens + qb * BQ + lax.broadcasted_iota(jnp.int32, (BQ, BQ), 0)
            q_r = tokens + qb * BQ + lax.broadcasted_iota(jnp.int32, (BQ, BQ), 1)

            def fill(kb, _):
                k_r = kb * BQ + lax.broadcasted_iota(jnp.int32, (BQ, BQ), 1)
                k_c = kb * BQ + lax.broadcasted_iota(jnp.int32, (BQ, BQ), 0)
                slot = qb * span + kb - qb
                bias[slot] = jnp.where((k_r >= start_c) & (k_r <= q_c), 0.0, NEG)
                bias_t[slot] = jnp.where((k_c >= start_r) & (k_c <= q_r), 0.0, NEG)
                return 0
            lax.fori_loop(lows[qb], blocks + qb + 1, fill, 0)

    dk_acc[...] = jnp.zeros_like(dk_acc)
    dv_acc[...] = jnp.zeros_like(dv_acc)
    heads = 2 * pairs

    def one_q(qb, _):
        q_rows = pl.ds(pl.multiple_of(qb * BQ, BQ), BQ)
        low = lows[qb]
        high = blocks + qb + 1
        q_h = []
        for p in range(pairs):
            q = q_ref[q_rows, p * 128:(p + 1) * 128]
            q_h += [jnp.where(even, q, 0), jnp.where(even, 0, q)]
        m_sc[...] = jnp.full_like(m_sc, NEG)
        l_sc[...] = jnp.zeros_like(l_sc)
        acc_sc[...] = jnp.zeros_like(acc_sc)

        def forward(kb, _):
            k_rows = pl.ds(pl.multiple_of(kb * BQ, BQ), BQ)
            b = bias[qb * span + kb - qb]
            for p in range(pairs):
                cols = slice(p * 128, (p + 1) * 128)
                k = k_ref[k_rows, cols]
                v = v_ref[k_rows, cols]
                outs, scales = [], []
                for h in (2 * p, 2 * p + 1):
                    s = dot_t(q_h[h], k) + b
                    m_old = m_sc[h]
                    m_new = jnp.maximum(m_old, jnp.max(s, axis=1, keepdims=True))
                    e = jnp.exp(s - m_new[:, :1])
                    a = jnp.exp(m_old - m_new)
                    l_sc[h] = a * l_sc[h] + jnp.sum(e, axis=1, keepdims=True)
                    m_sc[h] = m_new
                    outs.append(dot_n(e.astype(jnp.bfloat16), v))
                    scales.append(a)
                acc_sc[p] = acc_sc[p] * jnp.where(even, scales[0], scales[1]) + jnp.where(even, outs[0], outs[1])
            return 0
        lax.fori_loop(low, high, forward, 0)

        do_h, lse_r, delta_r = [], [], []
        for p in range(pairs):
            cols = slice(p * 128, (p + 1) * 128)
            o = acc_sc[p] / jnp.where(even, l_sc[2 * p], l_sc[2 * p + 1])
            out_ref[q_rows, cols] = o.astype(jnp.bfloat16)
            do = do_ref[q_rows, cols]
            prod = o * do.astype(jnp.float32)
            for h in (2 * p, 2 * p + 1):
                mine = even if h % 2 == 0 else ~even
                delta = jnp.sum(jnp.where(mine, prod, 0.0), axis=1, keepdims=True)
                lse = m_sc[h] + jnp.log(l_sc[h])
                both = jnp.where(even, lse, delta)
                turned = both.T
                lse_r.append(turned[0:1, :])
                delta_r.append(turned[64:65, :])
                do_h.append(jnp.where(mine, do, 0))
        dq_sc[...] = jnp.zeros_like(dq_sc)

        def backward(kb, _):
            k_rows = pl.ds(pl.multiple_of(kb * BQ, BQ), BQ)
            b = bias_t[qb * span + kb - qb]
            for p in range(pairs):
                cols = slice(p * 128, (p + 1) * 128)
                k = k_ref[k_rows, cols]
                v = v_ref[k_rows, cols]
                dqs, dks, dvs = [], None, None
                for h in (2 * p, 2 * p + 1):
                    s = dot_t(k, q_h[h]) + b
                    prob = jnp.exp(s - lse_r[h])
                    dp = dot_t(v, do_h[h])
                    ds = (prob * (dp - delta_r[h])).astype(jnp.bfloat16)
                    dv = dot_n(prob.astype(jnp.bfloat16), do_h[h])
                    dk = dot_n(ds, q_h[h])
                    dvs = dv if dvs is None else dvs + dv
                    dks = dk if dks is None else dks + dk
                    dqs.append(dot_c(ds, k))
                dv_acc[k_rows, cols] += dvs
                dk_acc[k_rows, cols] += dks
                dq_sc[p] += jnp.where(even, dqs[0], dqs[1])
            return 0
        lax.fori_loop(low, high, backward, 0)
        own_rows = pl.ds(pl.multiple_of(tokens + qb * BQ, BQ), BQ)
        for p in range(pairs):
            dq_ref[q_rows, p * 128:(p + 1) * 128] = unrotate(
                dq_sc[p] * 0.125, cos_ref[own_rows, :], sin_ref[own_rows, :]).astype(jnp.bfloat16)
        return 0
    lax.fori_loop(0, blocks, one_q, 0)

    def finish(kb, _):
        rows = pl.ds(pl.multiple_of(kb * BQ, BQ), BQ)
        for p in range(pairs):
            cols = slice(p * 128, (p + 1) * 128)
            dk_ref[rows, cols] = unrotate(dk_acc[rows, cols], cos_ref[rows, :], sin_ref[rows, :]).astype(jnp.bfloat16)
            dv_ref[rows, cols] = dv_acc[rows, cols].astype(jnp.bfloat16)
        return 0
    lax.fori_loop(0, 2 * blocks, finish, 0)

def swap_pairs(x):
    odd = lax.broadcasted_iota(jnp.int32, x.shape, 1) % 2 == 1
    n = x.shape[1]
    return jnp.where(odd, pltpu.roll(x, 1, 1), pltpu.roll(x, n - 1, 1))

def rotate(x, cosine, sine):
    return x * cosine + swap_pairs(x) * sine

def unrotate(x, cosine, sine):
    return x * cosine - swap_pairs(x) * sine

def attention(lows, starts, cosine, sine, mixed, d_out):
    tokens, width = d_out.shape
    pairs = 2
    wide = 128 * pairs
    groups = width // wide
    blocks = tokens // BQ
    whole = lambda shape: pl.BlockSpec(shape, lambda g, lows: (0,) * len(shape))
    own = pl.BlockSpec((tokens, wide), lambda g, lows: (0, g))
    both = pl.BlockSpec((2 * tokens, wide), lambda g, lows: (0, g))
    q_spec = pl.BlockSpec((tokens, wide), lambda g, lows: (1, g))
    k_spec = pl.BlockSpec((2 * tokens, wide), lambda g, lows: (0, groups + g))
    v_spec = pl.BlockSpec((2 * tokens, wide), lambda g, lows: (0, 2 * groups + g))
    bf, f32 = jnp.bfloat16, jnp.float32
    slots = blocks * (blocks + 1)
    one, two = jax.ShapeDtypeStruct((tokens, width), bf), jax.ShapeDtypeStruct((2 * tokens, width), bf)
    return pl.pallas_call(
        functools.partial(attention_kernel, pairs, tokens),
        out_shape=[one, one, two, two],
        grid_spec=pltpu.PrefetchScalarGridSpec(
            num_scalar_prefetch=1,
            grid=(groups,),
            in_specs=[whole((tokens, 1)), whole((1, tokens)), whole((2 * tokens, 128)), whole((2 * tokens, 128)),
                      q_spec, k_spec, v_spec, own],
            out_specs=[own, own, both, both],
            scratch_shapes=[pltpu.VMEM((slots, BQ, BQ), f32), pltpu.VMEM((slots, BQ, BQ), f32),
                            pltpu.VMEM((2 * tokens, wide), f32), pltpu.VMEM((2 * tokens, wide), f32),
                            pltpu.VMEM((2 * pairs, BQ, 128), f32), pltpu.VMEM((2 * pairs, BQ, 128), f32),
                            pltpu.VMEM((pairs, BQ, 128), f32), pltpu.VMEM((pairs, BQ, 128), f32)],
        ),
        compiler_params=pltpu.CompilerParams(vmem_limit_bytes=56 * 2**20),
        cost_estimate=pl.CostEstimate(flops=60 * 10**9, bytes_accessed=30 * 2**20, transcendentals=0),
        name="attention",
    )(lows, starts[:, None], starts[None, :], cosine, sine, mixed, mixed, mixed, d_out)


def qkv_kernel(cols, normed_ref, w_ref, cos_ref, sin_ref, out_ref):
    block = pl.program_id(1)
    mixed = dot_n(normed_ref[...], w_ref[...])

    @pl.when(block < 2 * cols)
    def _():
        scale = jnp.where(block < cols, 0.125, 1.0)
        cosine = cos_ref[...] * scale
        sine = sin_ref[...] * scale
        for i in range(mixed.shape[1] // 128):
            lanes = slice(i * 128, (i + 1) * 128)
            out_ref[:, lanes] = rotate(mixed[:, lanes], cosine, sine).astype(jnp.bfloat16)

    @pl.when(block >= 2 * cols)
    def _():
        out_ref[...] = mixed.astype(jnp.bfloat16)


def project(normed, w_qkv, cosine, sine):
    rows, width = normed.shape
    wide, tall = 512, 1024
    cols = width // wide
    return pl.pallas_call(
        functools.partial(qkv_kernel, cols),
        out_shape=jax.ShapeDtypeStruct((rows, 3 * width), jnp.bfloat16),
        grid=(rows // tall, 3 * cols),
        in_specs=[
            pl.BlockSpec((tall, width), lambda i, j: (i, 0)),
            pl.BlockSpec((width, wide), lambda i, j: (0, j)),
            pl.BlockSpec((tall, 128), lambda i, j: (i, 0)),
            pl.BlockSpec((tall, 128), lambda i, j: (i, 0)),
        ],
        out_specs=pl.BlockSpec((tall, wide), lambda i, j: (i, j)),
        compiler_params=pltpu.CompilerParams(vmem_limit_bytes=48 * 2**20),
        cost_estimate=pl.CostEstimate(flops=12 * 10**9, bytes_accessed=24 * 2**20, transcendentals=0),
        name="project",
    )(normed, w_qkv, cosine, sine)


def rope_tables(position):
    lane = np.arange(128) % HEAD
    freqs = np.where(lane < ROT, 10000.0 ** (-2.0 * (lane // 2) / ROT), 0.0).astype(np.float32)
    sign = np.where(lane % 2 == 0, -1.0, 1.0).astype(np.float32)
    angles = position.astype(jnp.float32)[:, None] * freqs[None, :]
    return jnp.cos(angles), jnp.sin(angles) * sign[None, :]


def layer_norm_stats(values):
    mean = jnp.mean(values, axis=1, keepdims=True)
    centered = values - mean
    spread = jnp.mean(centered * centered, axis=1, keepdims=True)
    scale = lax.rsqrt(spread + EPS)
    return centered * scale, scale


MESH = pl.DeviceIdType.MESH
RING = 12
SLOTS = 4


def reduce_kernel(dims, g_qkv, g_out, normed, normed_t, grad, grad_t, x_ref, w_in, w_back, b_in, base_out, base_dn,
                  vec_in, o_qkv, o_out, o_in, o_back, o_vec, block_out, d_normed,
                  buf, core_recv, chip, x_recv, y_recv, part, z_recv, fin, fin_recv, res, acc_out, hidden, d_pre, win_buf, wback_buf,
                  vec, vec_recv, load_sem, acc_sem, w_sem, send_sem, recv_sem, zsend_sem, zrecv_sem, vsend_sem, vrecv_sem):
    rows, seqs, q_rows, edge, tokens, width, ff = dims
    bf, f32 = jnp.bfloat16, jnp.float32
    levels = rows // 4
    region = q_rows - edge
    r, s = lax.axis_index("rows"), lax.axis_index("seq")
    core, y, z = lax.rem(r, 2), lax.rem(r // 2, 2), r // 4
    odd = lax.rem(s, 2)
    core_id = {"rows": r + 1 - 2 * core}
    y_id = {"rows": r + 2 - 4 * y}
    flip = lambda bit: {"seq": s + bit - 2 * bit * lax.rem(s // bit, 2)}
    z_of = lambda d: lax.rem(z + d, levels)
    z_id = lambda d: {"rows": z_of(d) * 4 + lax.rem(r, 4)}
    bits = []
    while 2 ** (len(bits) + 1) < seqs:
        bits.append(2 ** (len(bits) + 1))
    finals = bits + [1]

    barrier = pltpu.get_barrier_semaphore()
    partners = [core_id, y_id] + [z_id(d) for d in range(1, levels)] + [flip(b) for b in finals]
    for partner in partners:
        pl.semaphore_signal(barrier, inc=1, device_id=partner, device_id_type=MESH)
    pl.semaphore_wait(barrier, len(partners))

    piece = q_rows // 4
    n_qkv, n_out, n_in, n_back = 3 * width // 512, width // 512, ff // 512, width // 128
    n_first = n_qkv + n_out
    n_mlp = n_first + n_in
    total = n_mlp + n_back
    own_rows = pl.ds(pl.multiple_of(odd * edge, edge), region)
    c_mine = pl.ds(pl.multiple_of(odd * (q_rows - edge), edge), edge)
    c_other = pl.ds(pl.multiple_of((1 - odd) * (q_rows - edge), edge), edge)

    def remote(src, dst, stage, slot, target):
        return pltpu.make_async_remote_copy(src, dst, send_sem.at[stage, slot], recv_sem.at[stage, slot],
                                            device_id=target, device_id_type=MESH)

    def core_copy(k):
        return remote(buf.at[lax.rem(k, RING), :, 1 - core], core_recv.at[lax.rem(k, SLOTS)], 0, lax.rem(k, SLOTS), core_id)

    def x_copy(k):
        t = lax.rem(k, SLOTS)
        return remote(chip.at[t, :, :, c_other], x_recv.at[t], 1, t, flip(1))

    def y_copy(k):
        t = lax.rem(k, SLOTS)
        return remote(chip.at[t, :, 1 - y, own_rows], y_recv.at[t], 2, t, y_id)

    def z_copy(k, d):
        t = lax.rem(k, SLOTS)
        return pltpu.make_async_remote_copy(part.at[t, z_of(d)], z_recv.at[t, d - 1], zsend_sem.at[d - 1, t],
                                            zrecv_sem.at[d - 1, t], device_id=z_id(d), device_id_type=MESH)

    def fin_copy(k, i):
        t = lax.rem(k, SLOTS)
        return remote(fin.at[t, i], fin_recv.at[t, i], 3 + i, t, flip(finals[i]))

    def load_copies(source, col, k):
        slot = lax.rem(k, RING)
        return [pltpu.make_async_copy(source.at[:, :, :, pl.ds(pl.multiple_of(col + 128 * j, 128), 128)],
                                      buf.at[slot, :, :, pl.ds(j * piece, piece)], load_sem.at[j]) for j in range(4)]

    def load(k):
        @pl.when(k < n_qkv)
        def _():
            for copy in load_copies(g_qkv, k * 512, k):
                copy.start()

        @pl.when((k >= n_qkv) & (k < n_first))
        def _():
            for copy in load_copies(g_out, (k - n_qkv) * 512, k):
                copy.start()

    def weights(j):
        t = lax.rem(j, 2)
        cols = pl.ds(pl.multiple_of(j * 512, 512), 512)
        return [pltpu.make_async_copy(w_in.at[:, cols], win_buf.at[t], w_sem.at[0, t]),
                pltpu.make_async_copy(w_back.at[cols, :], wback_buf.at[t], w_sem.at[1, t])]

    starts = [pltpu.make_async_copy(base_out, acc_out, acc_sem.at[0]), pltpu.make_async_copy(base_dn, d_normed, acc_sem.at[1])]
    for copy in weights(0) + starts:
        copy.start()
    load(0)

    def mlp(j):
        @pl.when(j == 0)
        def _():
            for copy in starts:
                copy.wait()
        for copy in weights(j):
            copy.wait()

        @pl.when(j + 1 < n_in)
        def _():
            for copy in weights(j + 1):
                copy.start()
        t = lax.rem(j, 2)
        cols = pl.ds(pl.multiple_of(j * 512, 512), 512)
        tall = 512
        bias = b_in[:, cols]

        def rows_step(i, sums):
            block = pl.ds(pl.multiple_of(i * tall, tall), tall)
            pre = dot_n(normed[block, :], win_buf[t]) + bias
            up = dot_t(grad[block, :], wback_buf[t])
            square = pre * pre
            turn = jnp.tanh(pre * (GELU_COEF + (GELU_COEF * 0.044715) * square))
            half = 0.5 + 0.5 * turn
            hid = (pre * half).astype(bf)
            slope = half + (0.5 * pre) * (1.0 - turn * turn) * (GELU_COEF + (3 * 0.044715 * GELU_COEF) * square)
            down = (up * slope).astype(bf)
            hidden[block, cols] = hid
            d_pre[block, :] = down
            acc_out[block, :] += dot_n(hid, wback_buf[t])
            d_normed[block, :] += dot_t(down, win_buf[t])
            return sums + jnp.sum(down.astype(f32), axis=0, keepdims=True)
        sums = lax.fori_loop(0, tokens // tall, rows_step, jnp.zeros((1, 512), f32))
        vec[pl.ds(3 + j // 2, 1), pl.ds(pl.multiple_of(lax.rem(j, 2) * 512, 512), 512)] = sums
        slot = lax.rem(n_first + j, RING)
        per = 8
        big = per * width // rows

        def grads_step(i, _):
            value = dot_n(normed_t[pl.ds(pl.multiple_of(i * big, big), big), :], d_pre[...]).astype(bf)
            for m in range(per):
                for a in range(4):
                    buf[slot, i * (per // 2) + m // 2, m % 2, a * piece:(a + 1) * piece, :] = (
                        value[m * piece:(m + 1) * piece, a * 128:(a + 1) * 128])
            return 0
        lax.fori_loop(0, rows // per, grads_step, 0)

    def finish_tokens():
        gain = vec_in[0:1, :]
        bias = vec_in[1:2, :]
        back = jnp.zeros((1, width), f32)
        tall = 256
        def step(i, sums):
            gain, bias, back = sums
            block = pl.ds(pl.multiple_of(i * tall, tall), tall)
            block_out[block, :] = acc_out[block, :].astype(bf)
            values = x_ref[block, :].astype(f32)
            centered = values - jnp.mean(values, axis=1, keepdims=True)
            unit = centered * lax.rsqrt(jnp.mean(centered * centered, axis=1, keepdims=True) + EPS)
            d = d_normed[block, :]
            return (gain + jnp.sum(d * unit, axis=0, keepdims=True), bias + jnp.sum(d, axis=0, keepdims=True),
                    back + jnp.sum(grad[block, :].astype(f32), axis=0, keepdims=True))
        gain, bias, back = lax.fori_loop(0, tokens // tall, step, (gain, bias, back))
        vec[0:1, :] = gain
        vec[1:2, :] = bias
        vec[2:3, :] = back
        vec[7:8, :] = jnp.zeros((1, width), f32)

    def back_grads(j):
        value = dot_n(grad_t[pl.ds(pl.multiple_of(j * 128, 128), 128), :], hidden[...]).astype(bf)
        slot = lax.rem(n_mlp + j, RING)
        parts = q_rows // 128
        for d in range(rows):
            for a in range(parts):
                buf[slot, d // 2, d % 2, a * 128:(a + 1) * 128, :] = value[:, (d * parts + a) * 128:(d * parts + a + 1) * 128]

    def vec_copy(i, target):
        return pltpu.make_async_remote_copy(vec, vec_recv.at[i], vsend_sem.at[i], vrecv_sem.at[i],
                                            device_id=target, device_id_type=MESH)
    vec_stages = [[(0, core_id)], [(1, y_id)], [(2 + d - 1, z_id(d)) for d in range(1, levels)]]
    vec_stages += [[(1 + levels + i, flip(b))] for i, b in enumerate(finals)]

    def store(k):
        def place(out, col):
            for j in range(4):
                out[:, pl.ds(pl.multiple_of(col + 128 * j, 128), 128)] = res[j * piece:(j + 1) * piece, :]

        @pl.when(k < n_qkv)
        def _():
            place(o_qkv, k * 512)

        @pl.when((k >= n_qkv) & (k < n_first))
        def _():
            place(o_out, (k - n_qkv) * 512)

        @pl.when((k >= n_first) & (k < n_mlp))
        def _():
            place(o_in, (k - n_first) * 512)

        @pl.when(k >= n_mlp)
        def _():
            for a in range(q_rows // 128):
                o_back[a * 128:(a + 1) * 128, pl.ds(pl.multiple_of((k - n_mlp) * 128, 128), 128)] = (
                    res[a * 128:(a + 1) * 128, :].T)

    def stage(lag, it, body):
        k = it - lag

        @pl.when((k >= 0) & (k < total))
        def _():
            body(k, lax.rem(k, SLOTS))

    def send_first(k, t):
        @pl.when(k < n_first)
        def _():
            for copy in load_copies(g_qkv, 0, k):
                copy.wait()
        load(k + 1)
        core_copy(k).start()

    def core_add(k, t):
        core_copy(k).wait()
        slot = lax.rem(k, RING)
        for i in range(rows // 2):
            chip[t, i // 2, i % 2] = buf[slot, i, core] + core_recv[t, i]
        x_copy(k).start()

    def x_add(k, t):
        x_copy(k).wait()
        for i in range(rows // 2):
            chip[t, i // 2, i % 2, c_mine] = chip[t, i // 2, i % 2, c_mine] + x_recv[t, i // 2, i % 2]
        y_copy(k).start()

    def y_add(k, t):
        y_copy(k).wait()
        for i in range(levels):
            part[t, i] = chip[t, i, y, own_rows] + y_recv[t, i]
        for d in range(1, levels):
            z_copy(k, d).start()

    def z_add(k, t):
        for d in range(1, levels):
            z_copy(k, d).wait()
        value = part[t, z].astype(f32)
        for d in range(1, levels):
            value = value + z_recv[t, d - 1].astype(f32)
        fin[t, 0] = value.astype(bf)
        fin_copy(k, 0).start()

    def fin_add(i):
        def body(k, t):
            fin_copy(k, i).wait()
            fin[t, i + 1] = fin[t, i] + fin_recv[t, i]
            fin_copy(k, i + 1).start()
        return body

    def last(k, t):
        i = len(finals) - 1
        fin_copy(k, i).wait()
        middle = q_rows - 2 * edge
        at = lambda start, size: pl.ds(pl.multiple_of(start, edge), size)
        res[c_mine, :] = fin[t, i, at(odd * middle, edge)].astype(f32)
        res[c_other, :] = fin_recv[t, i, at((1 - odd) * middle, edge)].astype(f32)
        res[edge:q_rows - edge, :] = (fin[t, i, at((1 - odd) * edge, middle)].astype(f32)
                                      + fin_recv[t, i, at(odd * edge, middle)].astype(f32))
        store(k)

    pipeline = [send_first, core_add, x_add, y_add, z_add] + [fin_add(i) for i in range(len(bits))] + [last]

    def step(it, _):
        for lag, body in enumerate(pipeline):
            stage(lag, it, body)

        @pl.when(it < n_in)
        def _():
            mlp(it)

        @pl.when(it == n_in)
        def _():
            finish_tokens()
            for i, target in vec_stages[0]:
                vec_copy(i, target).start()
        for number, stages in enumerate(vec_stages):
            @pl.when(it == n_in + 1 + number)
            def _():
                for i, target in stages:
                    vec_copy(i, target).wait()
                value = vec[...]
                for i, target in stages:
                    value = value + vec_recv[i]
                if number + 1 < len(vec_stages):
                    vec[...] = value
                    for i, target in vec_stages[number + 1]:
                        vec_copy(i, target).start()
                else:
                    o_vec[...] = value

        @pl.when((it >= n_in) & (it < n_in + n_back))
        def _():
            back_grads(it - n_in)
        return 0
    lax.fori_loop(0, total + len(pipeline) - 1, step, 0)


def reduce_all(rows, seqs, g_qkv, g_out, normed, normed_t, grad, grad_t, x, w_in, w_back, b_in, base_out, base_dn, vec_in):
    tokens, width = normed.shape
    ff = w_in.shape[1]
    share = width // rows
    q_rows = 4 * share
    edge = q_rows // 4
    levels = rows // 4
    region = q_rows - edge
    finals = max(1, (seqs - 1).bit_length())
    bf, f32 = jnp.bfloat16, jnp.float32
    vmem, hbm = pl.BlockSpec(memory_space=pltpu.VMEM), pl.BlockSpec(memory_space=pl.ANY)
    dma = pltpu.SemaphoreType.DMA
    return pl.pallas_call(
        functools.partial(reduce_kernel, (rows, seqs, q_rows, edge, tokens, width, ff)),
        out_shape=[jax.ShapeDtypeStruct((share, 3 * width), f32), jax.ShapeDtypeStruct((share, width), f32),
                   jax.ShapeDtypeStruct((share, ff), f32), jax.ShapeDtypeStruct((ff // rows, width), f32),
                   jax.ShapeDtypeStruct((8, width), f32), jax.ShapeDtypeStruct((tokens, width), bf),
                   jax.ShapeDtypeStruct((tokens, width), f32)],
        in_specs=[hbm, hbm, vmem, vmem, vmem, vmem, vmem, hbm, hbm, vmem, hbm, hbm, vmem],
        out_specs=[vmem] * 7,
        scratch_shapes=[
            pltpu.VMEM((RING, rows // 2, 2, q_rows, 128), bf),
            pltpu.VMEM((SLOTS, rows // 2, q_rows, 128), bf),
            pltpu.VMEM((SLOTS, levels, 2, q_rows, 128), bf),
            pltpu.VMEM((SLOTS, levels, 2, edge, 128), bf),
            pltpu.VMEM((SLOTS, levels, region, 128), bf),
            pltpu.VMEM((SLOTS, levels, region, 128), bf),
            pltpu.VMEM((SLOTS, levels - 1, region, 128), bf),
            pltpu.VMEM((SLOTS, finals, region, 128), bf),
            pltpu.VMEM((SLOTS, finals, region, 128), bf),
            pltpu.VMEM((q_rows, 128), f32),
            pltpu.VMEM((tokens, width), f32),
            pltpu.VMEM((tokens, ff), bf),
            pltpu.VMEM((tokens, 512), bf),
            pltpu.VMEM((2, width, 512), bf),
            pltpu.VMEM((2, 512, width), bf),
            pltpu.VMEM((8, width), f32),
            pltpu.VMEM((1 + levels + finals, 8, width), f32),
            dma((4,)), dma((2,)), dma((2, 2)), dma((3 + finals, SLOTS)), dma((3 + finals, SLOTS)),
            dma((levels - 1, SLOTS)), dma((levels - 1, SLOTS)), dma((1 + levels + finals,)), dma((1 + levels + finals,)),
        ],
        compiler_params=pltpu.CompilerParams(collective_id=1, has_side_effects=True, vmem_limit_bytes=62 * 2**20),
        cost_estimate=pl.CostEstimate(flops=100 * 10**9, bytes_accessed=100 * 2**20, transcendentals=0),
        name="reduce",
    )(g_qkv.reshape(rows // 2, 2, share, 3 * width), g_out.reshape(rows // 2, 2, share, width), normed, normed_t, grad, grad_t, x,
      w_in, w_back, b_in, base_out, base_dn, vec_in)


def body(block_input, lengths, norm_gain, norm_bias, w_qkv, w_attn_out, w_fc_in, b_fc_in, w_fc_out, b_fc_out, cotangent):
    f32, bf = jnp.float32, jnp.bfloat16
    gather = lambda w: lax.all_gather(w, "rows", axis=0, tiled=True)
    rows, seqs = lax.axis_size("rows"), lax.axis_size("seq")
    prior_input = lax.ppermute(block_input[0], "seq", [(i, i + 1) for i in range(seqs - 1)])
    gain, bias = gather(norm_gain).astype(f32), gather(norm_bias).astype(f32)
    w_qkv_all, w_out_all = gather(w_qkv), gather(w_attn_out)
    w_in_all, b_in_all, w_back_all, b_back_all = gather(w_fc_in), gather(b_fc_in), gather(w_fc_out), gather(b_fc_out)
    inputs = block_input[0].astype(f32)
    tokens, width = inputs.shape
    own_lengths = lengths[0]
    count = own_lengths.shape[0]
    first = lax.axis_index("seq") * tokens
    index = first - tokens + jnp.arange(2 * tokens, dtype=jnp.int32)
    order = np.arange(count)
    ends = jnp.sum(jnp.where(order[None, :] <= order[:, None], own_lengths[None, :], 0), axis=1)
    begin = jnp.sum(jnp.where(ends[None, :] <= index[:, None], own_lengths[None, :], 0), axis=1)
    cosine, sine = rope_tables(index - begin)
    starts = (begin - first + tokens)[tokens:]
    lows = starts[::BQ] // BQ

    unit, scale = layer_norm_stats(inputs)
    normed = (unit * gain + bias).astype(bf)
    prior_unit, _ = layer_norm_stats(prior_input.astype(f32))
    normed_both = jnp.concatenate([(prior_unit * gain + bias).astype(bf), normed], axis=0)
    mixed = project(normed_both, w_qkv_all, cosine, sine)
    grad_out = cotangent[0]
    d_attended = jnp.dot(grad_out, w_out_all.T, preferred_element_type=f32).astype(bf)
    attended, d_q, d_k, d_v = attention(lows, starts, cosine, sine, mixed, d_attended)

    d_normed_both = jnp.dot(d_k, w_qkv_all[:, width:2 * width].T, preferred_element_type=f32) + jnp.dot(
        d_v, w_qkv_all[:, 2 * width:].T, preferred_element_type=f32)
    d_prior = d_normed_both[:tokens]
    back = lax.ppermute(d_prior.astype(bf), "seq", [(i + 1, i) for i in range(seqs - 1)])
    vec_in = jnp.stack([jnp.sum(d_prior * prior_unit, axis=0), jnp.sum(d_prior, axis=0)])
    grad_w_qkv = jnp.concatenate([
        jnp.dot(normed.T, d_q, preferred_element_type=f32).astype(bf),
        jnp.dot(normed_both.T, d_k, preferred_element_type=f32).astype(bf),
        jnp.dot(normed_both.T, d_v, preferred_element_type=f32).astype(bf)], axis=1)
    grad_w_out = jnp.dot(attended.T, grad_out, preferred_element_type=f32).astype(bf)
    base_dn = d_normed_both[tokens:] + jnp.dot(d_q, w_qkv_all[:, :width].T, preferred_element_type=f32)
    base_out = inputs + jnp.dot(attended, w_out_all, preferred_element_type=f32) + b_back_all.astype(f32)

    g_qkv, g_out, g_in, g_back, vec, block_output, d_normed = reduce_all(
        rows, seqs, grad_w_qkv, grad_w_out, normed, normed.T, grad_out, grad_out.T, block_input[0], w_in_all, w_back_all,
        b_in_all.astype(f32)[None], base_out, base_dn, vec_in)

    d_normed = d_normed + back.astype(f32)
    d_unit = d_normed * gain
    d_input = (d_unit - jnp.mean(d_unit, axis=1, keepdims=True)
               - unit * jnp.mean(d_unit * unit, axis=1, keepdims=True)) * scale
    grad_input = d_input + grad_out.astype(f32)
    share, wide = width // rows, 4 * width // rows
    r = lax.axis_index("rows")
    own = lambda vector, size: lax.dynamic_slice_in_dim(vector, r * size, size)
    return (block_output[None], grad_input[None], own(vec[0], share), own(vec[1], share), g_qkv, g_out, g_in,
            own(vec[3:7].reshape(4 * width), wide), g_back, own(vec[2], share))


def solution(mesh):
    vector, matrix, tokens = P("rows"), P("rows", None), P("rows", "seq", None)
    in_specs = (tokens, matrix, vector, vector, matrix, matrix, matrix, vector, matrix, vector, tokens)
    out_specs = (tokens, tokens, vector, vector, matrix, matrix, matrix, vector, matrix, vector)
    return jax.shard_map(body, mesh=mesh, in_specs=in_specs, out_specs=out_specs, check_vma=False)
```

```python
import functools

import jax
import jax.numpy as jnp
import numpy as np
from jax import lax
from jax.experimental import pallas as pl
from jax.experimental.pallas import tpu as pltpu
from jax.sharding import PartitionSpec as P

HEADS = 16
HEAD = 64
ROT = 32
EPS = 1e-05
GELU_COEF = 0.7978845608028654
MESH = pl.DeviceIdType.MESH

NEG = -1e30
BQ = 256

def dot_t(a, b):
    return lax.dot_general(a, b, (((1,), (1,)), ((), ())), preferred_element_type=jnp.float32)

def dot_n(a, b):
    return lax.dot_general(a, b, (((1,), (0,)), ((), ())), preferred_element_type=jnp.float32)

def dot_c(a, b):
    return lax.dot_general(a, b, (((0,), (0,)), ((), ())), preferred_element_type=jnp.float32)

def attention_kernel(pairs, tokens, lows, start_col, start_row, cos_ref, sin_ref, q_ref, k_ref, v_ref, do_ref,
                     out_ref, dq_ref, dk_ref, dv_ref, bias, bias_t, dk_acc, dv_acc, m_sc, l_sc, acc_sc, dq_sc):
    blocks = tokens // BQ
    span = blocks + 1
    lane = lax.broadcasted_iota(jnp.int32, (BQ, 128), 1)
    even = lane < 64

    @pl.when(pl.program_id(0) == 0)
    def _():
        for qb in range(blocks):
            start_c = start_col[qb * BQ:(qb + 1) * BQ, :]
            start_r = start_row[:, qb * BQ:(qb + 1) * BQ]
            q_c = tokens + qb * BQ + lax.broadcasted_iota(jnp.int32, (BQ, BQ), 0)
            q_r = tokens + qb * BQ + lax.broadcasted_iota(jnp.int32, (BQ, BQ), 1)

            def fill(kb, _):
                k_r = kb * BQ + lax.broadcasted_iota(jnp.int32, (BQ, BQ), 1)
                k_c = kb * BQ + lax.broadcasted_iota(jnp.int32, (BQ, BQ), 0)
                slot = qb * span + kb - qb
                bias[slot] = jnp.where((k_r >= start_c) & (k_r <= q_c), 0.0, NEG)
                bias_t[slot] = jnp.where((k_c >= start_r) & (k_c <= q_r), 0.0, NEG)
                return 0
            lax.fori_loop(lows[qb], blocks + qb + 1, fill, 0)

    dk_acc[...] = jnp.zeros_like(dk_acc)
    dv_acc[...] = jnp.zeros_like(dv_acc)
    heads = 2 * pairs

    def one_q(qb, _):
        q_rows = pl.ds(pl.multiple_of(qb * BQ, BQ), BQ)
        low = lows[qb]
        high = blocks + qb + 1
        q_h = []
        for p in range(pairs):
            q = q_ref[q_rows, p * 128:(p + 1) * 128]
            q_h += [jnp.where(even, q, 0), jnp.where(even, 0, q)]
        m_sc[...] = jnp.full_like(m_sc, NEG)
        l_sc[...] = jnp.zeros_like(l_sc)
        acc_sc[...] = jnp.zeros_like(acc_sc)

        def forward(kb, _):
            k_rows = pl.ds(pl.multiple_of(kb * BQ, BQ), BQ)
            b = bias[qb * span + kb - qb]
            for p in range(pairs):
                cols = slice(p * 128, (p + 1) * 128)
                k = k_ref[k_rows, cols]
                v = v_ref[k_rows, cols]
                outs, scales = [], []
                for h in (2 * p, 2 * p + 1):
                    s = dot_t(q_h[h], k) + b
                    m_old = m_sc[h]
                    m_new = jnp.maximum(m_old, jnp.max(s, axis=1, keepdims=True))
                    e = jnp.exp(s - m_new[:, :1])
                    a = jnp.exp(m_old - m_new)
                    l_sc[h] = a * l_sc[h] + jnp.sum(e, axis=1, keepdims=True)
                    m_sc[h] = m_new
                    outs.append(dot_n(e.astype(jnp.bfloat16), v))
                    scales.append(a)
                acc_sc[p] = acc_sc[p] * jnp.where(even, scales[0], scales[1]) + jnp.where(even, outs[0], outs[1])
            return 0
        lax.fori_loop(low, high, forward, 0)

        do_h, lse_r, delta_r = [], [], []
        for p in range(pairs):
            cols = slice(p * 128, (p + 1) * 128)
            o = acc_sc[p] / jnp.where(even, l_sc[2 * p], l_sc[2 * p + 1])
            out_ref[q_rows, cols] = o.astype(jnp.bfloat16)
            do = do_ref[q_rows, cols]
            prod = o * do.astype(jnp.float32)
            for h in (2 * p, 2 * p + 1):
                mine = even if h % 2 == 0 else ~even
                delta = jnp.sum(jnp.where(mine, prod, 0.0), axis=1, keepdims=True)
                lse = m_sc[h] + jnp.log(l_sc[h])
                both = jnp.where(even, lse, delta)
                turned = both.T
                lse_r.append(turned[0:1, :])
                delta_r.append(turned[64:65, :])
                do_h.append(jnp.where(mine, do, 0))
        dq_sc[...] = jnp.zeros_like(dq_sc)

        def backward(kb, _):
            k_rows = pl.ds(pl.multiple_of(kb * BQ, BQ), BQ)
            b = bias_t[qb * span + kb - qb]
            for p in range(pairs):
                cols = slice(p * 128, (p + 1) * 128)
                k = k_ref[k_rows, cols]
                v = v_ref[k_rows, cols]
                dqs, dks, dvs = [], None, None
                for h in (2 * p, 2 * p + 1):
                    s = dot_t(k, q_h[h]) + b
                    prob = jnp.exp(s - lse_r[h])
                    dp = dot_t(v, do_h[h])
                    ds = (prob * (dp - delta_r[h])).astype(jnp.bfloat16)
                    dv = dot_n(prob.astype(jnp.bfloat16), do_h[h])
                    dk = dot_n(ds, q_h[h])
                    dvs = dv if dvs is None else dvs + dv
                    dks = dk if dks is None else dks + dk
                    dqs.append(dot_c(ds, k))
                dv_acc[k_rows, cols] += dvs
                dk_acc[k_rows, cols] += dks
                dq_sc[p] += jnp.where(even, dqs[0], dqs[1])
            return 0
        lax.fori_loop(low, high, backward, 0)
        own_rows = pl.ds(pl.multiple_of(tokens + qb * BQ, BQ), BQ)
        for p in range(pairs):
            dq_ref[q_rows, p * 128:(p + 1) * 128] = unrotate(
                dq_sc[p] * 0.125, cos_ref[own_rows, :], sin_ref[own_rows, :]).astype(jnp.bfloat16)
        return 0
    lax.fori_loop(0, blocks, one_q, 0)

    def finish(kb, _):
        rows = pl.ds(pl.multiple_of(kb * BQ, BQ), BQ)
        for p in range(pairs):
            cols = slice(p * 128, (p + 1) * 128)
            dk_ref[rows, cols] = unrotate(dk_acc[rows, cols], cos_ref[rows, :], sin_ref[rows, :]).astype(jnp.bfloat16)
            dv_ref[rows, cols] = dv_acc[rows, cols].astype(jnp.bfloat16)
        return 0
    lax.fori_loop(0, 2 * blocks, finish, 0)

def swap_pairs(x):
    odd = lax.broadcasted_iota(jnp.int32, x.shape, 1) % 2 == 1
    n = x.shape[1]
    return jnp.where(odd, pltpu.roll(x, 1, 1), pltpu.roll(x, n - 1, 1))

def rotate(x, cosine, sine):
    return x * cosine + swap_pairs(x) * sine

def unrotate(x, cosine, sine):
    return x * cosine - swap_pairs(x) * sine

def attention(lows, starts, cosine, sine, mixed, d_out):
    tokens, width = d_out.shape
    pairs = 2
    wide = 128 * pairs
    groups = width // wide
    blocks = tokens // BQ
    whole = lambda shape: pl.BlockSpec(shape, lambda g, lows: (0,) * len(shape))
    own = pl.BlockSpec((tokens, wide), lambda g, lows: (0, g))
    both = pl.BlockSpec((2 * tokens, wide), lambda g, lows: (0, g))
    q_spec = pl.BlockSpec((tokens, wide), lambda g, lows: (1, g))
    k_spec = pl.BlockSpec((2 * tokens, wide), lambda g, lows: (0, groups + g))
    v_spec = pl.BlockSpec((2 * tokens, wide), lambda g, lows: (0, 2 * groups + g))
    bf, f32 = jnp.bfloat16, jnp.float32
    slots = blocks * (blocks + 1)
    one, two = jax.ShapeDtypeStruct((tokens, width), bf), jax.ShapeDtypeStruct((2 * tokens, width), bf)
    return pl.pallas_call(
        functools.partial(attention_kernel, pairs, tokens),
        out_shape=[one, one, two, two],
        grid_spec=pltpu.PrefetchScalarGridSpec(
            num_scalar_prefetch=1,
            grid=(groups,),
            in_specs=[whole((tokens, 1)), whole((1, tokens)), whole((2 * tokens, 128)), whole((2 * tokens, 128)),
                      q_spec, k_spec, v_spec, own],
            out_specs=[own, own, both, both],
            scratch_shapes=[pltpu.VMEM((slots, BQ, BQ), f32), pltpu.VMEM((slots, BQ, BQ), f32),
                            pltpu.VMEM((2 * tokens, wide), f32), pltpu.VMEM((2 * tokens, wide), f32),
                            pltpu.VMEM((2 * pairs, BQ, 128), f32), pltpu.VMEM((2 * pairs, BQ, 128), f32),
                            pltpu.VMEM((pairs, BQ, 128), f32), pltpu.VMEM((pairs, BQ, 128), f32)],
        ),
        compiler_params=pltpu.CompilerParams(vmem_limit_bytes=56 * 2**20),
        cost_estimate=pl.CostEstimate(flops=60 * 10**9, bytes_accessed=30 * 2**20, transcendentals=0),
        name="attention",
    )(lows, starts[:, None], starts[None, :], cosine, sine, mixed, mixed, mixed, d_out)


def rope_tables(position):
    lane = np.arange(128) % HEAD
    freqs = np.where(lane < ROT, 10000.0 ** (-2.0 * (lane // 2) / ROT), 0.0).astype(np.float32)
    sign = np.where(lane % 2 == 0, -1.0, 1.0).astype(np.float32)
    angles = position.astype(jnp.float32)[:, None] * freqs[None, :]
    return jnp.cos(angles), jnp.sin(angles) * sign[None, :]


def layer_norm_stats(values):
    mean = jnp.mean(values, axis=1, keepdims=True)
    centered = values - mean
    spread = jnp.mean(centered * centered, axis=1, keepdims=True)
    scale = lax.rsqrt(spread + EPS)
    return centered * scale, scale


CHUNK = 256


def gather_kernel(dims, w_out, w_qkv, x_hbm, grad, vec_own, cos_ref, sin_ref,
                  wout_all, wqkv_all, normed_all, mixed_all, d_attended, prior_all, vec_all,
                  wbuf, own, prior, normed, mixed, d_att, vec, vec_recv, in_sem, load_sem, out_sem, zsend, zrecv, ysend, yrecv,
                  csend, crecv, psend, precv, vsend, vrecv):
    rows, seqs, tokens, width = dims
    bf, f32 = jnp.bfloat16, jnp.float32
    levels = rows // 4
    r, s = lax.axis_index("rows"), lax.axis_index("seq")
    core, y, z = lax.rem(r, 2), lax.rem(r // 2, 2), r // 4
    core_id = {"rows": r + 1 - 2 * core}
    y_id = {"rows": r + 2 - 4 * y}
    z_of = lambda d: lax.rem(z + d, levels)
    z_id = lambda d: {"rows": z_of(d) * 4 + lax.rem(r, 4)}
    has_next, has_prior = s < seqs - 1, s > 0
    n_out, n_qkv = width // CHUNK, 3 * width // CHUNK
    total = n_out + n_qkv
    quarter = tokens // 4

    def load(k):
        source = w_out if k < n_out else w_qkv
        col = (k if k < n_out else k - n_out) * CHUNK
        return pltpu.make_async_copy(source.at[:, col:col + CHUNK], wbuf.at[k, z, y, core], load_sem.at[k])

    fetch = pltpu.make_async_copy(x_hbm, own, in_sem)
    fetch.start()
    for k in range(total):
        load(k).start()

    barrier = pltpu.get_barrier_semaphore()
    partners = [core_id, y_id] + [z_id(d) for d in range(1, levels)]
    for partner in partners:
        pl.semaphore_signal(barrier, inc=1, device_id=partner, device_id_type=MESH)

    @pl.when(has_next)
    def _():
        pl.semaphore_signal(barrier, inc=1, device_id={"seq": s + 1}, device_id_type=MESH)

    @pl.when(has_prior)
    def _():
        pl.semaphore_signal(barrier, inc=1, device_id={"seq": s - 1}, device_id_type=MESH)
    pl.semaphore_wait(barrier, len(partners) + jnp.where(has_next, 1, 0) + jnp.where(has_prior, 1, 0))

    def prior_copy(i):
        block = pl.ds(i * quarter, quarter)
        return pltpu.make_async_remote_copy(x_hbm.at[block], prior.at[block], psend.at[i], precv.at[i],
                                            device_id={"seq": jnp.minimum(s + 1, seqs - 1)}, device_id_type=MESH)

    def vec_copy(i, target):
        return pltpu.make_async_remote_copy(vec.at[i], vec_recv.at[i], vsend.at[i], vrecv.at[i],
                                            device_id=target, device_id_type=MESH)

    def z_vec(d):
        return pltpu.make_async_remote_copy(vec.at[0], vec_recv.at[1 + d], vsend.at[1 + d], vrecv.at[1 + d],
                                            device_id=z_id(d), device_id_type=MESH)

    def z_copy(k, d):
        mine = wbuf.at[k, z, y, core]
        return pltpu.make_async_remote_copy(mine, mine, zsend.at[k, d - 1], zrecv.at[k, d - 1],
                                            device_id=z_id(d), device_id_type=MESH)

    def z_landed(k, d):
        theirs = wbuf.at[k, z_of(levels - d), y, core]
        return pltpu.make_async_remote_copy(theirs, theirs, zsend.at[k, d - 1], zrecv.at[k, d - 1],
                                            device_id=z_id(d), device_id_type=MESH)

    def y_copy(k, side):
        part = wbuf.at[k, :, side, core]
        return pltpu.make_async_remote_copy(part, part, ysend.at[k], yrecv.at[k], device_id=y_id, device_id_type=MESH)

    def core_copy(k, side):
        part = wbuf.at[k, :, :, side]
        return pltpu.make_async_remote_copy(part, part, csend.at[k], crecv.at[k], device_id=core_id, device_id_type=MESH)

    vec[0] = vec_own[...]
    for d in range(1, levels):
        z_vec(d).start()

    @pl.when(has_next)
    def _():
        for i in range(4):
            prior_copy(i).start()
    for k in range(total):
        load(k).wait()
        for d in range(1, levels):
            z_copy(k, d).start()

    for d in range(1, levels):
        z_vec(d).wait()
    value = vec[0]
    for d in range(1, levels):
        value = value + vec_recv[1 + d]
    vec[1] = value
    vec_copy(1, y_id).start()
    fetch.wait()
    vec_copy(1, y_id).wait()
    vec[2] = value + vec_recv[1]
    swap = pltpu.make_async_remote_copy(vec.at[2], vec_recv.at[0], vsend.at[0], vrecv.at[0], device_id=core_id,
                                        device_id_type=MESH)
    swap.start()
    swap.wait()
    vec_all[...] = vec[2] + vec_recv[0]
    gain, bias = vec_all[0:1, :], vec_all[1:2, :]

    def normalize(source, half):
        def body(i, _):
            block = pl.ds(pl.multiple_of(i * quarter, quarter), quarter)
            values = source[block, :].astype(f32)
            centered = values - jnp.mean(values, axis=1, keepdims=True)
            unit = centered * lax.rsqrt(jnp.mean(centered * centered, axis=1, keepdims=True) + EPS)
            normed[half, block, :] = (unit * gain + bias).astype(bf)
            return 0
        return body
    lax.fori_loop(0, 4, normalize(own, 1), 0)

    outs = []

    def send_out(src, dst):
        copy = pltpu.make_async_copy(src, dst, out_sem.at[len(outs)])
        copy.start()
        outs.append(copy)
    send_out(normed.at[1], normed_all.at[1])

    def multiply(half, j):
        cols = slice(j * CHUNK, (j + 1) * CHUNK)
        tall = tokens // 2

        def body(i, _):
            block = pl.ds(pl.multiple_of(i * tall, tall), tall)
            product = dot_n(normed[half, block, :], wbuf[n_out + j].reshape(width, CHUNK))
            if j * CHUNK < 2 * width:
                scale = 0.125 if j * CHUNK < width else 1.0
                place = pl.ds(pl.multiple_of(half * tokens + i * tall, tall), tall)
                cosine, sine = cos_ref[place, :] * scale, sin_ref[place, :] * scale
                for a in range(CHUNK // 128):
                    mixed[half, block, j * CHUNK + a * 128:j * CHUNK + (a + 1) * 128] = rotate(
                        product[:, a * 128:(a + 1) * 128], cosine, sine).astype(bf)
            else:
                mixed[half, block, cols] = product.astype(bf)
            return 0
        lax.fori_loop(0, 2, body, 0)
        send_out(mixed.at[half, :, cols], mixed_all.at[half, :, cols])

    def project_back():
        tall = tokens // 4

        def body(i, _):
            block = pl.ds(pl.multiple_of(i * tall, tall), tall)
            value = dot_t(grad[block, 0:CHUNK], wbuf[0].reshape(width, CHUNK))
            for k in range(1, n_out):
                value = value + dot_t(grad[block, k * CHUNK:(k + 1) * CHUNK], wbuf[k].reshape(width, CHUNK))
            d_att[block, :] = value.astype(bf)
            return 0
        lax.fori_loop(0, 4, body, 0)
        send_out(d_att, d_attended)

    for it in range(total + 2):
        if it < total:
            for d in range(1, levels):
                z_landed(it, d).wait_recv()
            y_copy(it, y).start()
        if 0 <= it - 1 < total:
            y_copy(it - 1, 1 - y).wait_recv()
            core_copy(it - 1, core).start()
        if 0 <= it - 2 < total:
            k = it - 2
            core_copy(k, 1 - core).wait_recv()
            if k < n_out:
                send_out(wbuf.at[k], wout_all.at[:, :, :, :, k * CHUNK:(k + 1) * CHUNK])
                if k == n_out - 1:
                    project_back()
            else:
                send_out(wbuf.at[k], wqkv_all.at[:, :, :, :, (k - n_out) * CHUNK:(k - n_out + 1) * CHUNK])
                multiply(1, k - n_out)

    @pl.when(has_prior)
    def _():
        for i in range(4):
            prior_copy(i).wait_recv()

    @pl.when(jnp.logical_not(has_prior))
    def _():
        prior[...] = jnp.zeros_like(prior)
    send_out(prior, prior_all)
    lax.fori_loop(0, 4, normalize(prior, 0), 0)
    send_out(normed.at[0], normed_all.at[0])
    for j in range(n_qkv // 3, n_qkv):
        multiply(0, j)

    @pl.when(has_next)
    def _():
        for i in range(4):
            prior_copy(i).wait_send()
    for k in range(total):
        for d in range(1, levels):
            z_copy(k, d).wait_send()
        y_copy(k, y).wait_send()
        core_copy(k, core).wait_send()
    for copy in outs:
        copy.wait()


def gather_all(rows, seqs, w_out, w_qkv, x, grad, vec_own, cosine, sine):
    tokens, width = x.shape
    share, levels = width // rows, rows // 4
    bf, f32 = jnp.bfloat16, jnp.float32
    vmem, hbm = pl.BlockSpec(memory_space=pltpu.VMEM), pl.BlockSpec(memory_space=pl.ANY)
    dma = pltpu.SemaphoreType.DMA
    total = 4 * width // CHUNK
    shape = jax.ShapeDtypeStruct
    wout_all, wqkv_all, normed, mixed, d_att, prior, vec = pl.pallas_call(
        functools.partial(gather_kernel, (rows, seqs, tokens, width)),
        out_shape=[shape((levels, 2, 2, share, width), bf), shape((levels, 2, 2, share, 3 * width), bf), shape((2, tokens, width), bf),
                   shape((2, tokens, 3 * width), bf), shape((tokens, width), bf), shape((tokens, width), bf), shape((8, width), f32)],
        in_specs=[hbm, hbm, hbm, vmem, vmem, vmem, vmem],
        out_specs=[hbm] * 6 + [vmem],
        scratch_shapes=[
            pltpu.VMEM((total, levels, 2, 2, share, CHUNK), bf),
            pltpu.VMEM((tokens, width), bf), pltpu.VMEM((tokens, width), bf), pltpu.VMEM((2, tokens, width), bf),
            pltpu.VMEM((2, tokens, 3 * width), bf), pltpu.VMEM((tokens, width), bf),
            pltpu.VMEM((3, 8, width), f32), pltpu.VMEM((1 + levels, 8, width), f32),
            dma, dma((total,)), dma((2 * total + 8,)), dma((total, levels - 1)), dma((total, levels - 1)),
            dma((total,)), dma((total,)), dma((total,)), dma((total,)), dma((4,)), dma((4,)), dma((1 + levels,)), dma((1 + levels,)),
        ],
        compiler_params=pltpu.CompilerParams(collective_id=0, has_side_effects=True, vmem_limit_bytes=60 * 2**20),
        cost_estimate=pl.CostEstimate(flops=20 * 10**9, bytes_accessed=40 * 2**20, transcendentals=0),
        name="gather",
    )(w_out, w_qkv, x, grad, vec_own, cosine, sine)
    return (wout_all.reshape(width, width), wqkv_all.reshape(width, 3 * width), normed.reshape(2 * tokens, width),
            mixed.reshape(2 * tokens, 3 * width), d_att, prior, vec)


RING = 12
SLOTS = 6


def reduce_kernel(dims, g_q, g_k, g_v, g_out, normed, normed_t, grad, grad_t, x_ref, w_in, w_back, b_in, base_out, base_dn,
                  vec_in, o_qkv, o_out, o_in, o_back, o_vec, block_out, d_normed,
                  buf, core_recv, chip, x_recv, y_recv, part, z_recv, fin, fin_recv, res, acc_out, hidden, d_pre, win_buf, wback_buf,
                  vec, vec_recv, load_sem, acc_sem, w_sem, send_sem, recv_sem, zsend_sem, zrecv_sem, vsend_sem, vrecv_sem):
    rows, seqs, q_rows, edge, tokens, width, ff = dims
    bf, f32 = jnp.bfloat16, jnp.float32
    levels = rows // 4
    region = q_rows - edge
    r, s = lax.axis_index("rows"), lax.axis_index("seq")
    core, y, z = lax.rem(r, 2), lax.rem(r // 2, 2), r // 4
    odd = lax.rem(s, 2)
    core_id = {"rows": r + 1 - 2 * core}
    y_id = {"rows": r + 2 - 4 * y}
    flip = lambda bit: {"seq": s + bit - 2 * bit * lax.rem(s // bit, 2)}
    z_of = lambda d: lax.rem(z + d, levels)
    z_id = lambda d: {"rows": z_of(d) * 4 + lax.rem(r, 4)}
    bits = []
    while 2 ** (len(bits) + 1) < seqs:
        bits.append(2 ** (len(bits) + 1))
    finals = bits + [1]

    barrier = pltpu.get_barrier_semaphore()
    partners = [core_id, y_id] + [z_id(d) for d in range(1, levels)] + [flip(b) for b in finals]
    for partner in partners:
        pl.semaphore_signal(barrier, inc=1, device_id=partner, device_id_type=MESH)
    pl.semaphore_wait(barrier, len(partners))

    piece = q_rows // 4
    n_qkv, n_out, n_in, n_back = 3 * width // 512, width // 512, ff // 512, width // 128
    n_first = n_qkv + n_out
    n_mlp = n_first + n_in
    total = n_mlp + n_back
    own_rows = pl.ds(pl.multiple_of(odd * edge, edge), region)
    c_mine = pl.ds(pl.multiple_of(odd * (q_rows - edge), edge), edge)
    c_other = pl.ds(pl.multiple_of((1 - odd) * (q_rows - edge), edge), edge)

    def remote(src, dst, stage, slot, target):
        return pltpu.make_async_remote_copy(src, dst, send_sem.at[stage, slot], recv_sem.at[stage, slot],
                                            device_id=target, device_id_type=MESH)

    def core_copy(k):
        return remote(buf.at[lax.rem(k, RING), :, 1 - core], core_recv.at[lax.rem(k, SLOTS)], 0, lax.rem(k, SLOTS), core_id)

    def x_copy(k):
        t = lax.rem(k, SLOTS)
        return remote(chip.at[t, :, :, c_other], x_recv.at[t], 1, t, flip(1))

    def y_copy(k):
        t = lax.rem(k, SLOTS)
        return remote(chip.at[t, :, 1 - y, own_rows], y_recv.at[t], 2, t, y_id)

    def z_copy(k, d):
        t = lax.rem(k, SLOTS)
        return pltpu.make_async_remote_copy(part.at[t, z_of(d)], z_recv.at[t, d - 1], zsend_sem.at[d - 1, t],
                                            zrecv_sem.at[d - 1, t], device_id=z_id(d), device_id_type=MESH)

    def fin_copy(k, i):
        t = lax.rem(k, SLOTS)
        return remote(fin.at[t, i], fin_recv.at[t, i], 3 + i, t, flip(finals[i]))

    def load_copies(source, col, k):
        slot = lax.rem(k, RING)
        return [pltpu.make_async_copy(source.at[:, :, :, pl.ds(pl.multiple_of(col + 128 * j, 128), 128)],
                                      buf.at[slot, :, :, pl.ds(j * piece, piece)], load_sem.at[j]) for j in range(4)]

    def load(k):
        for i, source in enumerate((g_q, g_k, g_v, g_out)):
            @pl.when((k >= i * n_out) & (k < (i + 1) * n_out))
            def _():
                for copy in load_copies(source, (k - i * n_out) * 512, k):
                    copy.start()

    def weights(j):
        t = lax.rem(j, 2)
        cols = pl.ds(pl.multiple_of(j * 512, 512), 512)
        return [pltpu.make_async_copy(w_in.at[:, cols], win_buf.at[t], w_sem.at[0, t]),
                pltpu.make_async_copy(w_back.at[cols, :], wback_buf.at[t], w_sem.at[1, t])]

    starts = [pltpu.make_async_copy(base_out, acc_out, acc_sem.at[0]), pltpu.make_async_copy(base_dn, d_normed, acc_sem.at[1])]
    for copy in weights(0) + starts:
        copy.start()
    load(0)

    def mlp(j):
        @pl.when(j == 0)
        def _():
            for copy in starts:
                copy.wait()
        for copy in weights(j):
            copy.wait()

        @pl.when(j + 1 < n_in)
        def _():
            for copy in weights(j + 1):
                copy.start()
        t = lax.rem(j, 2)
        cols = pl.ds(pl.multiple_of(j * 512, 512), 512)
        tall = 512
        bias = b_in[:, cols]

        def rows_step(i, sums):
            block = pl.ds(pl.multiple_of(i * tall, tall), tall)
            pre = dot_n(normed[block, :], win_buf[t]) + bias
            up = dot_t(grad[block, :], wback_buf[t])
            square = pre * pre
            turn = jnp.tanh(pre * (GELU_COEF + (GELU_COEF * 0.044715) * square))
            half = 0.5 + 0.5 * turn
            hid = (pre * half).astype(bf)
            slope = half + (0.5 * pre) * (1.0 - turn * turn) * (GELU_COEF + (3 * 0.044715 * GELU_COEF) * square)
            down = (up * slope).astype(bf)
            hidden[block, cols] = hid
            d_pre[block, :] = down
            acc_out[block, :] += dot_n(hid, wback_buf[t])
            d_normed[block, :] += dot_t(down, win_buf[t])
            return sums + jnp.sum(down.astype(f32), axis=0, keepdims=True)
        sums = lax.fori_loop(0, tokens // tall, rows_step, jnp.zeros((1, 512), f32))
        vec[pl.ds(3 + j // 2, 1), pl.ds(pl.multiple_of(lax.rem(j, 2) * 512, 512), 512)] = sums
        slot = lax.rem(n_first + j, RING)
        per = 8
        big = per * width // rows

        def grads_step(i, _):
            value = dot_n(normed_t[pl.ds(pl.multiple_of(i * big, big), big), :], d_pre[...]).astype(bf)
            for m in range(per):
                for a in range(4):
                    buf[slot, i * (per // 2) + m // 2, m % 2, a * piece:(a + 1) * piece, :] = (
                        value[m * piece:(m + 1) * piece, a * 128:(a + 1) * 128])
            return 0
        lax.fori_loop(0, rows // per, grads_step, 0)

    def finish_tokens():
        gain = vec_in[0:1, :]
        bias = vec_in[1:2, :]
        back = jnp.zeros((1, width), f32)
        tall = 256
        def step(i, sums):
            gain, bias, back = sums
            block = pl.ds(pl.multiple_of(i * tall, tall), tall)
            block_out[block, :] = acc_out[block, :].astype(bf)
            values = x_ref[block, :].astype(f32)
            centered = values - jnp.mean(values, axis=1, keepdims=True)
            unit = centered * lax.rsqrt(jnp.mean(centered * centered, axis=1, keepdims=True) + EPS)
            d = d_normed[block, :]
            return (gain + jnp.sum(d * unit, axis=0, keepdims=True), bias + jnp.sum(d, axis=0, keepdims=True),
                    back + jnp.sum(grad[block, :].astype(f32), axis=0, keepdims=True))
        gain, bias, back = lax.fori_loop(0, tokens // tall, step, (gain, bias, back))
        vec[0:1, :] = gain
        vec[1:2, :] = bias
        vec[2:3, :] = back
        vec[7:8, :] = jnp.zeros((1, width), f32)

    def back_grads(j):
        value = dot_n(grad_t[pl.ds(pl.multiple_of(j * 128, 128), 128), :], hidden[...]).astype(bf)
        slot = lax.rem(n_mlp + j, RING)
        parts = q_rows // 128
        for d in range(rows):
            for a in range(parts):
                buf[slot, d // 2, d % 2, a * 128:(a + 1) * 128, :] = value[:, (d * parts + a) * 128:(d * parts + a + 1) * 128]

    def vec_copy(i, target):
        return pltpu.make_async_remote_copy(vec, vec_recv.at[i], vsend_sem.at[i], vrecv_sem.at[i],
                                            device_id=target, device_id_type=MESH)
    vec_stages = [[(0, core_id)], [(1, y_id)], [(2 + d - 1, z_id(d)) for d in range(1, levels)]]
    vec_stages += [[(1 + levels + i, flip(b))] for i, b in enumerate(finals)]

    def store(k):
        def place(out, col):
            for j in range(4):
                out[:, pl.ds(pl.multiple_of(col + 128 * j, 128), 128)] = res[j * piece:(j + 1) * piece, :]

        @pl.when(k < n_qkv)
        def _():
            place(o_qkv, k * 512)

        @pl.when((k >= n_qkv) & (k < n_first))
        def _():
            place(o_out, (k - n_qkv) * 512)

        @pl.when((k >= n_first) & (k < n_mlp))
        def _():
            place(o_in, (k - n_first) * 512)

        @pl.when(k >= n_mlp)
        def _():
            for a in range(q_rows // 128):
                o_back[a * 128:(a + 1) * 128, pl.ds(pl.multiple_of((k - n_mlp) * 128, 128), 128)] = (
                    res[a * 128:(a + 1) * 128, :].T)

    def stage(lag, it, body):
        k = it - lag

        @pl.when((k >= 0) & (k < total))
        def _():
            body(k, lax.rem(k, SLOTS))

    def send_first(k, t):
        @pl.when(k < n_first)
        def _():
            for copy in load_copies(g_q, 0, k):
                copy.wait()
        load(k + 1)
        core_copy(k).start()

    def core_add(k, t):
        core_copy(k).wait()
        slot = lax.rem(k, RING)
        for i in range(rows // 2):
            chip[t, i // 2, i % 2] = buf[slot, i, core] + core_recv[t, i]
        x_copy(k).start()

    def x_add(k, t):
        x_copy(k).wait()
        for i in range(rows // 2):
            chip[t, i // 2, i % 2, c_mine] = chip[t, i // 2, i % 2, c_mine] + x_recv[t, i // 2, i % 2]
        y_copy(k).start()

    def y_add(k, t):
        y_copy(k).wait()
        for i in range(levels):
            part[t, i] = chip[t, i, y, own_rows] + y_recv[t, i]
        for d in range(1, levels):
            z_copy(k, d).start()

    def z_add(k, t):
        for d in range(1, levels):
            z_copy(k, d).wait()
        value = part[t, z].astype(f32)
        for d in range(1, levels):
            value = value + z_recv[t, d - 1].astype(f32)
        fin[t, 0] = value.astype(bf)
        fin_copy(k, 0).start()

    def fin_add(i):
        def body(k, t):
            fin_copy(k, i).wait()
            fin[t, i + 1] = fin[t, i] + fin_recv[t, i]
            fin_copy(k, i + 1).start()
        return body

    def last(k, t):
        i = len(finals) - 1
        fin_copy(k, i).wait()
        middle = q_rows - 2 * edge
        at = lambda start, size: pl.ds(pl.multiple_of(start, edge), size)
        res[c_mine, :] = fin[t, i, at(odd * middle, edge)].astype(f32)
        res[c_other, :] = fin_recv[t, i, at((1 - odd) * middle, edge)].astype(f32)
        res[edge:q_rows - edge, :] = (fin[t, i, at((1 - odd) * edge, middle)].astype(f32)
                                      + fin_recv[t, i, at(odd * edge, middle)].astype(f32))
        store(k)

    pipeline = [send_first, core_add, x_add, y_add, z_add] + [fin_add(i) for i in range(len(bits))] + [last]

    def step(it, _):
        for lag, body in enumerate(pipeline):
            stage(2 * lag, it, body)

        @pl.when(it < n_in)
        def _():
            mlp(it)

        @pl.when(it == n_in)
        def _():
            finish_tokens()
            for i, target in vec_stages[0]:
                vec_copy(i, target).start()
        for number, stages in enumerate(vec_stages):
            @pl.when(it == n_in + 1 + number)
            def _():
                for i, target in stages:
                    vec_copy(i, target).wait()
                value = vec[...]
                for i, target in stages:
                    value = value + vec_recv[i]
                if number + 1 < len(vec_stages):
                    vec[...] = value
                    for i, target in vec_stages[number + 1]:
                        vec_copy(i, target).start()
                else:
                    o_vec[...] = value

        @pl.when((it >= n_in) & (it < n_in + n_back))
        def _():
            back_grads(it - n_in)
        return 0
    lax.fori_loop(0, total + 2 * len(pipeline) - 2, step, 0)


def reduce_all(rows, seqs, g_q, g_k, g_v, g_out, normed, normed_t, grad, grad_t, x, w_in, w_back, b_in, base_out, base_dn, vec_in):
    tokens, width = normed.shape
    ff = w_in.shape[1]
    share = width // rows
    q_rows = 4 * share
    edge = q_rows // 4
    levels = rows // 4
    region = q_rows - edge
    finals = max(1, (seqs - 1).bit_length())
    bf, f32 = jnp.bfloat16, jnp.float32
    vmem, hbm = pl.BlockSpec(memory_space=pltpu.VMEM), pl.BlockSpec(memory_space=pl.ANY)
    dma = pltpu.SemaphoreType.DMA
    return pl.pallas_call(
        functools.partial(reduce_kernel, (rows, seqs, q_rows, edge, tokens, width, ff)),
        out_shape=[jax.ShapeDtypeStruct((share, 3 * width), f32), jax.ShapeDtypeStruct((share, width), f32),
                   jax.ShapeDtypeStruct((share, ff), f32), jax.ShapeDtypeStruct((ff // rows, width), f32),
                   jax.ShapeDtypeStruct((8, width), f32), jax.ShapeDtypeStruct((tokens, width), bf),
                   jax.ShapeDtypeStruct((tokens, width), f32)],
        in_specs=[hbm, hbm, hbm, hbm, vmem, vmem, vmem, vmem, vmem, hbm, hbm, vmem, hbm, hbm, vmem],
        out_specs=[vmem] * 7,
        scratch_shapes=[
            pltpu.VMEM((RING, rows // 2, 2, q_rows, 128), bf),
            pltpu.VMEM((SLOTS, rows // 2, q_rows, 128), bf),
            pltpu.VMEM((SLOTS, levels, 2, q_rows, 128), bf),
            pltpu.VMEM((SLOTS, levels, 2, edge, 128), bf),
            pltpu.VMEM((SLOTS, levels, region, 128), bf),
            pltpu.VMEM((SLOTS, levels, region, 128), bf),
            pltpu.VMEM((SLOTS, levels - 1, region, 128), bf),
            pltpu.VMEM((SLOTS, finals, region, 128), bf),
            pltpu.VMEM((SLOTS, finals, region, 128), bf),
            pltpu.VMEM((q_rows, 128), f32),
            pltpu.VMEM((tokens, width), f32),
            pltpu.VMEM((tokens, ff), bf),
            pltpu.VMEM((tokens, 512), bf),
            pltpu.VMEM((2, width, 512), bf),
            pltpu.VMEM((2, 512, width), bf),
            pltpu.VMEM((8, width), f32),
            pltpu.VMEM((1 + levels + finals, 8, width), f32),
            dma((4,)), dma((2,)), dma((2, 2)), dma((3 + finals, SLOTS)), dma((3 + finals, SLOTS)),
            dma((levels - 1, SLOTS)), dma((levels - 1, SLOTS)), dma((1 + levels + finals,)), dma((1 + levels + finals,)),
        ],
        compiler_params=pltpu.CompilerParams(collective_id=1, has_side_effects=True, vmem_limit_bytes=62 * 2**20),
        cost_estimate=pl.CostEstimate(flops=100 * 10**9, bytes_accessed=100 * 2**20, transcendentals=0),
        name="reduce",
    )(*[g.reshape(rows // 2, 2, share, width) for g in (g_q, g_k, g_v, g_out)], normed, normed_t, grad, grad_t, x,
      w_in, w_back, b_in, base_out, base_dn, vec_in)


def body(block_input, lengths, norm_gain, norm_bias, w_qkv, w_attn_out, w_fc_in, b_fc_in, w_fc_out, b_fc_out, cotangent):
    f32, bf = jnp.float32, jnp.bfloat16
    rows, seqs = lax.axis_size("rows"), lax.axis_size("seq")
    inputs = block_input[0].astype(f32)
    tokens, width = inputs.shape
    own_lengths = lengths[0]
    count = own_lengths.shape[0]
    first = lax.axis_index("seq") * tokens
    index = first - tokens + jnp.arange(2 * tokens, dtype=jnp.int32)
    order = np.arange(count)
    ends = jnp.sum(jnp.where(order[None, :] <= order[:, None], own_lengths[None, :], 0), axis=1)
    begin = jnp.sum(jnp.where(ends[None, :] <= index[:, None], own_lengths[None, :], 0), axis=1)
    cosine, sine = rope_tables(index - begin)
    starts = (begin - first + tokens)[tokens:]
    lows = starts[::BQ] // BQ

    share, wide = width // rows, 4 * width // rows
    r = lax.axis_index("rows")
    place = lambda vector, lines: jnp.where(np.arange(lines * width).reshape(rows, -1) // (lines * share) == r,
                                            vector.astype(f32)[None, :], 0.0).reshape(lines, width)
    vec_own = jnp.concatenate([place(norm_gain, 1), place(norm_bias, 1), place(b_fc_out, 1), place(b_fc_in, 4),
                               jnp.zeros((1, width), f32)])
    grad_out = cotangent[0]
    w_out_all, w_qkv_all, normed_both, mixed, d_attended, prior_input, vectors = gather_all(
        rows, seqs, w_attn_out, w_qkv, block_input[0], grad_out, vec_own, cosine, sine)
    w_fc_in, w_fc_out, vectors = lax.optimization_barrier((w_fc_in, w_fc_out, vectors))
    w_in_all = lax.all_gather(w_fc_in, "rows", axis=0, tiled=True)
    w_back_all = lax.all_gather(w_fc_out, "rows", axis=0, tiled=True)
    gain, bias, b_back_all = vectors[0], vectors[1], vectors[2]
    b_in_all = vectors[3:7].reshape(1, 4 * width)
    normed = normed_both[tokens:]
    unit, scale = layer_norm_stats(inputs)
    prior_unit, _ = layer_norm_stats(prior_input.astype(f32))
    attended, d_q, d_k, d_v = attention(lows, starts, cosine, sine, mixed, d_attended)

    d_normed_both = jnp.dot(d_k, w_qkv_all[:, width:2 * width].T, preferred_element_type=f32) + jnp.dot(
        d_v, w_qkv_all[:, 2 * width:].T, preferred_element_type=f32)
    d_prior = d_normed_both[:tokens]
    back = lax.ppermute(d_prior.astype(bf), "seq", [(i + 1, i) for i in range(seqs - 1)])
    vec_in = jnp.stack([jnp.sum(d_prior * prior_unit, axis=0), jnp.sum(d_prior, axis=0)])
    grads = [jnp.dot(normed.T, d_q, preferred_element_type=f32).astype(bf),
             jnp.dot(normed_both.T, d_k, preferred_element_type=f32).astype(bf),
             jnp.dot(normed_both.T, d_v, preferred_element_type=f32).astype(bf)]
    grad_w_out = jnp.dot(attended.T, grad_out, preferred_element_type=f32).astype(bf)
    base_dn = d_normed_both[tokens:] + jnp.dot(d_q, w_qkv_all[:, :width].T, preferred_element_type=f32)
    base_out = inputs + jnp.dot(attended, w_out_all, preferred_element_type=f32) + b_back_all

    g_qkv, g_out, g_in, g_back, vec, block_output, d_normed = reduce_all(
        rows, seqs, *grads, grad_w_out, normed, normed.T, grad_out, grad_out.T, block_input[0], w_in_all, w_back_all,
        b_in_all, base_out, base_dn, vec_in)

    d_normed = d_normed + back.astype(f32)
    d_unit = d_normed * gain
    d_input = (d_unit - jnp.mean(d_unit, axis=1, keepdims=True)
               - unit * jnp.mean(d_unit * unit, axis=1, keepdims=True)) * scale
    grad_input = d_input + grad_out.astype(f32)
    own = lambda vector, size: lax.dynamic_slice_in_dim(vector, r * size, size)
    return (block_output[None], grad_input[None], own(vec[0], share), own(vec[1], share), g_qkv, g_out, g_in,
            own(vec[3:7].reshape(4 * width), wide), g_back, own(vec[2], share))


def solution(mesh):
    vector, matrix, tokens = P("rows"), P("rows", None), P("rows", "seq", None)
    in_specs = (tokens, matrix, vector, vector, matrix, matrix, matrix, vector, matrix, vector, tokens)
    out_specs = (tokens, tokens, vector, vector, matrix, matrix, matrix, vector, matrix, vector)
    return jax.shard_map(body, mesh=mesh, in_specs=in_specs, out_specs=out_specs, check_vma=False)
```

```python
import functools

import jax
import jax.numpy as jnp
import numpy as np
from jax import lax
from jax.experimental import pallas as pl
from jax.experimental.pallas import tpu as pltpu
from jax.sharding import PartitionSpec as P

HEADS = 16
HEAD = 64
ROT = 32
EPS = 1e-05
GELU_COEF = 0.7978845608028654
MESH = pl.DeviceIdType.MESH

NEG = -1e30
BQ = 256
PAIRS = 4

def dot_t(a, b):
    return lax.dot_general(a, b, (((1,), (1,)), ((), ())), preferred_element_type=jnp.float32)

def dot_n(a, b):
    return lax.dot_general(a, b, (((1,), (0,)), ((), ())), preferred_element_type=jnp.float32)

def dot_c(a, b):
    return lax.dot_general(a, b, (((0,), (0,)), ((), ())), preferred_element_type=jnp.float32)

def attention_kernel(pairs, tokens, lows, start_row, cos_ref, sin_ref, q_ref, k_ref, v_ref, do_ref,
                     out_ref, turned_ref, dq_ref, dk_ref, dv_ref, bias, scores, weights, k_turned, v_turned, dk_acc, dv_acc, out_acc, dq_acc, slope):
    bf, f32 = jnp.bfloat16, jnp.float32
    blocks = tokens // BQ
    span = blocks + 1
    heads = 2 * pairs
    even = lax.broadcasted_iota(jnp.int32, (BQ, 128), 1) < HEAD
    fold = lambda x, op: op(x.reshape(BQ // 8, 8, BQ), axis=0)

    @pl.when(pl.program_id(0) == 0)
    def _():
        for qb in range(blocks):
            start = start_row[:, qb * BQ:(qb + 1) * BQ]
            query = tokens + qb * BQ + lax.broadcasted_iota(jnp.int32, (BQ, BQ), 1)

            def fill(kb, _):
                key = kb * BQ + lax.broadcasted_iota(jnp.int32, (BQ, BQ), 0)
                bias[qb * span + kb - qb] = jnp.where((key >= start) & (key <= query), 0.0, NEG).astype(bf)
                return 0
            lax.fori_loop(lows[qb], blocks + qb + 1, fill, 0)

    def prepare(kb, _):
        rows = pl.ds(pl.multiple_of(kb * BQ, BQ), BQ)
        for p in range(pairs):
            cols = slice(p * 128, (p + 1) * 128)
            k_turned[p, :, rows] = k_ref[rows, cols].T
            v_turned[p, :, rows] = v_ref[rows, cols].T
        return 0
    lax.fori_loop(lows[0], 2 * blocks, prepare, 0)
    dk_acc[...] = jnp.zeros_like(dk_acc)
    dv_acc[...] = jnp.zeros_like(dv_acc)

    def one_q(qb, _):
        q_rows = pl.ds(pl.multiple_of(qb * BQ, BQ), BQ)
        own_rows = pl.ds(pl.multiple_of(tokens + qb * BQ, BQ), BQ)
        low, high = lows[qb], blocks + qb + 1
        q_h = []
        for p in range(pairs):
            q = q_ref[q_rows, p * 128:(p + 1) * 128]
            q_h += [jnp.where(even, q, 0), jnp.where(even, 0, q)]

        def score(kb, tops):
            rows = pl.ds(pl.multiple_of(kb * BQ, BQ), BQ)
            b = bias[qb * span + kb - qb].astype(f32)
            new = []
            for h in range(heads):
                s = dot_t(k_ref[rows, (h // 2) * 128:(h // 2 + 1) * 128], q_h[h]) + b
                scores[kb - qb, h] = s
                new.append(jnp.maximum(tops[h], fold(s, jnp.max)))
            return tuple(new)
        tops = lax.fori_loop(low, high, score, tuple(jnp.full((8, BQ), NEG, f32) for _ in range(heads)))
        tops = [jnp.max(t, axis=0, keepdims=True) for t in tops]
        out_acc[...] = jnp.zeros_like(out_acc)
        dq_acc[...] = jnp.zeros_like(dq_acc)

        def attend(kb, sums):
            rows = pl.ds(pl.multiple_of(kb * BQ, BQ), BQ)
            new = []
            for h in range(heads):
                e = jnp.exp(scores[kb - qb, h] - tops[h])
                new.append(sums[h] + fold(e, jnp.sum))
                e = e.astype(bf)
                weights[kb - qb, h] = e
            for h in range(heads):
                half = slice((h % 2) * HEAD, (h % 2 + 1) * HEAD)
                out_acc[h // 2, half, :] += dot_n(v_turned[h // 2, half, rows], weights[kb - qb, h])
            return tuple(new)
        sums = lax.fori_loop(low, high, attend, tuple(jnp.zeros((8, BQ), f32) for _ in range(heads)))

        do_h, deltas = [], []
        for p in range(pairs):
            cols = slice(p * 128, (p + 1) * 128)
            inverse = [1.0 / jnp.sum(sums[h], axis=0, keepdims=True) for h in (2 * p, 2 * p + 1)]
            inverse = jnp.concatenate([jnp.broadcast_to(v, (HEAD, BQ)) for v in inverse], axis=0)
            out = out_acc[p] * inverse
            out_ref[q_rows, cols] = out.T.astype(bf)
            turned_ref[cols, q_rows] = out.astype(bf)
            d_out = do_ref[q_rows, cols].astype(f32).T * inverse
            product = out * d_out
            deltas += [jnp.sum(product[:HEAD], axis=0, keepdims=True), jnp.sum(product[HEAD:], axis=0, keepdims=True)]
            d_out = d_out.T.astype(bf)
            do_h += [jnp.where(even, d_out, 0), jnp.where(even, 0, d_out)]

        def back(kb, _):
            rows = pl.ds(pl.multiple_of(kb * BQ, BQ), BQ)
            for p in range(pairs):
                v = v_ref[rows, p * 128:(p + 1) * 128]
                for h in (2 * p, 2 * p + 1):
                    d_prob = dot_t(v, do_h[h])
                    slope[h] = (weights[kb - qb, h].astype(f32) * (d_prob - deltas[h])).astype(bf)
            for p in range(pairs):
                cols = slice(p * 128, (p + 1) * 128)
                dv_acc[rows, cols] += dot_n(weights[kb - qb, 2 * p], do_h[2 * p]) + dot_n(weights[kb - qb, 2 * p + 1], do_h[2 * p + 1])
                dk_acc[rows, cols] += dot_n(slope[2 * p], q_h[2 * p]) + dot_n(slope[2 * p + 1], q_h[2 * p + 1])
            for h in range(heads):
                half = slice((h % 2) * HEAD, (h % 2 + 1) * HEAD)
                dq_acc[h // 2, half, :] += dot_n(k_turned[h // 2, half, rows], slope[h])
            return 0
        lax.fori_loop(low, high, back, 0)
        for p in range(pairs):
            dq_ref[q_rows, p * 128:(p + 1) * 128] = unrotate(
                dq_acc[p].T * 0.125, cos_ref[own_rows, :], sin_ref[own_rows, :]).astype(bf)
        return 0
    lax.fori_loop(0, blocks, one_q, 0)

    def finish(kb, _):
        rows = pl.ds(pl.multiple_of(kb * BQ, BQ), BQ)
        for p in range(pairs):
            cols = slice(p * 128, (p + 1) * 128)
            dk_ref[rows, cols] = unrotate(dk_acc[rows, cols], cos_ref[rows, :], sin_ref[rows, :]).astype(bf)
            dv_ref[rows, cols] = dv_acc[rows, cols].astype(bf)
        return 0
    lax.fori_loop(0, 2 * blocks, finish, 0)


def swap_pairs(x):
    odd = lax.broadcasted_iota(jnp.int32, x.shape, 1) % 2 == 1
    n = x.shape[1]
    return jnp.where(odd, pltpu.roll(x, 1, 1), pltpu.roll(x, n - 1, 1))

def rotate(x, cosine, sine):
    return x * cosine + swap_pairs(x) * sine

def unrotate(x, cosine, sine):
    return x * cosine - swap_pairs(x) * sine

def attention(lows, starts, cosine, sine, mixed, d_out):
    tokens, width = d_out.shape
    pairs = PAIRS
    wide = 128 * pairs
    groups = width // wide
    blocks = tokens // BQ
    whole = lambda shape: pl.BlockSpec(shape, lambda g, lows: (0,) * len(shape), pipeline_mode=pl.Buffered(1))
    own = pl.BlockSpec((tokens, wide), lambda g, lows: (0, g))
    both = pl.BlockSpec((2 * tokens, wide), lambda g, lows: (0, g))
    q_spec = pl.BlockSpec((tokens, wide), lambda g, lows: (1, g))
    k_spec = pl.BlockSpec((2 * tokens, wide), lambda g, lows: (0, groups + g))
    v_spec = pl.BlockSpec((2 * tokens, wide), lambda g, lows: (0, 2 * groups + g))
    bf, f32 = jnp.bfloat16, jnp.float32
    slots = blocks * (blocks + 1)
    one, two = jax.ShapeDtypeStruct((tokens, width), bf), jax.ShapeDtypeStruct((2 * tokens, width), bf)
    return pl.pallas_call(
        functools.partial(attention_kernel, pairs, tokens),
        out_shape=[one, jax.ShapeDtypeStruct((width, tokens), bf), one, two, two],
        grid_spec=pltpu.PrefetchScalarGridSpec(
            num_scalar_prefetch=1,
            grid=(groups,),
            in_specs=[whole((1, tokens)), whole((2 * tokens, 128)), whole((2 * tokens, 128)), q_spec, k_spec, v_spec, own],
            out_specs=[own, pl.BlockSpec((wide, tokens), lambda g, lows: (g, 0)), own, both, both],
            scratch_shapes=[pltpu.VMEM((slots, BQ, BQ), bf), pltpu.VMEM((blocks + 1, 2 * pairs, BQ, BQ), f32),
                            pltpu.VMEM((blocks + 1, 2 * pairs, BQ, BQ), bf), pltpu.VMEM((pairs, 128, 2 * tokens), bf),
                            pltpu.VMEM((pairs, 128, 2 * tokens), bf), pltpu.VMEM((2 * tokens, wide), f32),
                            pltpu.VMEM((2 * tokens, wide), f32), pltpu.VMEM((pairs, 128, BQ), f32),
                            pltpu.VMEM((pairs, 128, BQ), f32), pltpu.VMEM((2 * pairs, BQ, BQ), bf)],
        ),
        compiler_params=pltpu.CompilerParams(vmem_limit_bytes=62 * 2**20),
        cost_estimate=pl.CostEstimate(flops=60 * 10**9, bytes_accessed=30 * 2**20, transcendentals=0),
        name="attention",
    )(lows, starts[None, :], cosine, sine, mixed, mixed, mixed, d_out)


def rope_tables(position):
    lane = np.arange(128) % HEAD
    freqs = np.where(lane < ROT, 10000.0 ** (-2.0 * (lane // 2) / ROT), 0.0).astype(np.float32)
    sign = np.where(lane % 2 == 0, -1.0, 1.0).astype(np.float32)
    angles = position.astype(jnp.float32)[:, None] * freqs[None, :]
    return jnp.cos(angles), jnp.sin(angles) * sign[None, :]


def layer_norm_stats(values):
    mean = jnp.mean(values, axis=1, keepdims=True)
    centered = values - mean
    spread = jnp.mean(centered * centered, axis=1, keepdims=True)
    scale = lax.rsqrt(spread + EPS)
    return centered * scale, scale


CHUNK = 256
AHEAD = 3


def gather_kernel(dims, w_out, w_qkv, x_hbm, grad, vec_own, cos_ref, sin_ref,
                  wout_all, wqkv_all, normed_own, normed_prior, turned_own, turned_prior, grad_turned, mixed_all, d_attended, prior_all, vec_all,
                  wbuf, own, prior, normed, turned, mixed, d_att, vec, vec_recv, in_sem, load_sem, out_sem, zsend, zrecv, ysend, yrecv,
                  csend, crecv, psend, precv, vsend, vrecv):
    rows, seqs, tokens, width = dims
    bf, f32 = jnp.bfloat16, jnp.float32
    levels = rows // 4
    r, s = lax.axis_index("rows"), lax.axis_index("seq")
    core, y, z = lax.rem(r, 2), lax.rem(r // 2, 2), r // 4
    core_id = {"rows": r + 1 - 2 * core}
    y_id = {"rows": r + 2 - 4 * y}
    z_of = lambda d: lax.rem(z + d, levels)
    z_id = lambda d: {"rows": z_of(d) * 4 + lax.rem(r, 4)}
    has_next, has_prior = s < seqs - 1, s > 0
    n_out, n_qkv = width // CHUNK, 3 * width // CHUNK
    total = n_out + n_qkv
    quarter = tokens // 4

    def load(k):
        source = w_out if k < n_out else w_qkv
        col = (k if k < n_out else k - n_out) * CHUNK
        return pltpu.make_async_copy(source.at[:, col:col + CHUNK], wbuf.at[k, z, y, core], load_sem.at[k])

    fetch = pltpu.make_async_copy(x_hbm, own, in_sem)
    fetch.start()
    for k in range(total):
        load(k).start()

    barrier = pltpu.get_barrier_semaphore()
    partners = [core_id, y_id] + [z_id(d) for d in range(1, levels)]
    for partner in partners:
        pl.semaphore_signal(barrier, inc=1, device_id=partner, device_id_type=MESH)

    @pl.when(has_next)
    def _():
        pl.semaphore_signal(barrier, inc=1, device_id={"seq": s + 1}, device_id_type=MESH)

    @pl.when(has_prior)
    def _():
        pl.semaphore_signal(barrier, inc=1, device_id={"seq": s - 1}, device_id_type=MESH)
    pl.semaphore_wait(barrier, len(partners) + jnp.where(has_next, 1, 0) + jnp.where(has_prior, 1, 0))

    def prior_copy(i):
        block = pl.ds(i * quarter, quarter)
        return pltpu.make_async_remote_copy(x_hbm.at[block], prior.at[block], psend.at[i], precv.at[i],
                                            device_id={"seq": jnp.minimum(s + 1, seqs - 1)}, device_id_type=MESH)

    def vec_copy(i, target):
        return pltpu.make_async_remote_copy(vec.at[i], vec_recv.at[i], vsend.at[i], vrecv.at[i],
                                            device_id=target, device_id_type=MESH)

    def z_vec(d):
        return pltpu.make_async_remote_copy(vec.at[0], vec_recv.at[1 + d], vsend.at[1 + d], vrecv.at[1 + d],
                                            device_id=z_id(d), device_id_type=MESH)

    def z_copy(k, d):
        mine = wbuf.at[k, z, y, core]
        return pltpu.make_async_remote_copy(mine, mine, zsend.at[k, d - 1], zrecv.at[k, d - 1],
                                            device_id=z_id(d), device_id_type=MESH)

    def z_landed(k, d):
        theirs = wbuf.at[k, z_of(levels - d), y, core]
        return pltpu.make_async_remote_copy(theirs, theirs, zsend.at[k, d - 1], zrecv.at[k, d - 1],
                                            device_id=z_id(d), device_id_type=MESH)

    def y_copy(k, side):
        part = wbuf.at[k, :, side, core]
        return pltpu.make_async_remote_copy(part, part, ysend.at[k], yrecv.at[k], device_id=y_id, device_id_type=MESH)

    def core_copy(k, side):
        part = wbuf.at[k, :, :, side]
        return pltpu.make_async_remote_copy(part, part, csend.at[k], crecv.at[k], device_id=core_id, device_id_type=MESH)

    vec[0] = vec_own[...]
    for d in range(1, levels):
        z_vec(d).start()

    @pl.when(has_next)
    def _():
        for i in range(2):
            prior_copy(i).start()

    @pl.when(jnp.logical_not(has_prior))
    def _():
        prior[...] = jnp.zeros_like(prior)

    def z_start(k):
        load(k).wait()
        for d in range(1, levels):
            z_copy(k, d).start()
    for k in range(AHEAD):
        z_start(k)

    swap = pltpu.make_async_remote_copy(vec.at[2], vec_recv.at[0], vsend.at[0], vrecv.at[0], device_id=core_id,
                                        device_id_type=MESH)

    def share_vectors(it):
        if it == 0:
            for d in range(1, levels):
                z_vec(d).wait()
            value = vec[0]
            for d in range(1, levels):
                value = value + vec_recv[1 + d]
            vec[1] = value
            vec_copy(1, y_id).start()
        if it == 1:
            vec_copy(1, y_id).wait()
            vec[2] = vec[1] + vec_recv[1]
            swap.start()
        if it == 2:
            swap.wait()
            vec_all[...] = vec[2] + vec_recv[0]

    def normalize(source, half, i):
        block = slice(i * quarter, (i + 1) * quarter)
        values = source[block, :].astype(f32)
        centered = values - jnp.mean(values, axis=1, keepdims=True)
        unit = centered * lax.rsqrt(jnp.mean(centered * centered, axis=1, keepdims=True) + EPS)
        normed[half, block, :] = (unit * vec_all[0:1, :] + vec_all[1:2, :]).astype(bf)

    def turn(source, place, i):
        block = slice(i * quarter, (i + 1) * quarter)
        turned[place, :, block] = source[block, :].T

    outs = []

    def send_out(src, dst):
        copy = pltpu.make_async_copy(src, dst, out_sem.at[len(outs)])
        copy.start()
        outs.append(copy)

    def multiply(half, j, parts):
        cols = slice(j * CHUNK, (j + 1) * CHUNK)
        tall = tokens // 2
        for i in parts:
            block = slice(i * tall, (i + 1) * tall)
            product = dot_n(normed[half, block, :], wbuf[n_out + j].reshape(width, CHUNK))
            if j * CHUNK < 2 * width:
                scale = 0.125 if j * CHUNK < width else 1.0
                place = slice(half * tokens + i * tall, half * tokens + (i + 1) * tall)
                cosine, sine = cos_ref[place, :] * scale, sin_ref[place, :] * scale
                for a in range(CHUNK // 128):
                    mixed[half, block, j * CHUNK + a * 128:j * CHUNK + (a + 1) * 128] = rotate(
                        product[:, a * 128:(a + 1) * 128], cosine, sine).astype(bf)
            else:
                mixed[half, block, cols] = product.astype(bf)
            send_out(mixed.at[half, block, cols], mixed_all.at[half, block, cols])

    def project_back():
        tall = tokens // 4

        def body(i, _):
            block = pl.ds(pl.multiple_of(i * tall, tall), tall)
            value = dot_t(grad[block, 0:CHUNK], wbuf[0].reshape(width, CHUNK))
            for k in range(1, n_out):
                value = value + dot_t(grad[block, k * CHUNK:(k + 1) * CHUNK], wbuf[k].reshape(width, CHUNK))
            d_att[block, :] = value.astype(bf)
            return 0
        lax.fori_loop(0, 4, body, 0)
        send_out(d_att, d_attended)

    def prior_landed(i):
        @pl.when(has_prior)
        def _():
            prior_copy(i).wait_recv()

    def prior_next(i):
        @pl.when(has_next)
        def _():
            prior_copy(i).wait_send()
            prior_copy(i + 2).start()

    for it in range(total + 2):
        if it < total:
            for d in range(1, levels):
                z_landed(it, d).wait_recv()
            if it + AHEAD < total:
                z_start(it + AHEAD)
            y_copy(it, y).start()
        if 0 <= it - 1 < total:
            y_copy(it - 1, 1 - y).wait_recv()
            core_copy(it - 1, core).start()
        share_vectors(it)
        if it == 3:
            fetch.wait()
        if 3 <= it <= 4:
            normalize(own, 1, 2 * it - 6)
            normalize(own, 1, 2 * it - 5)
        if it == 5:
            send_out(normed.at[1], normed_own)
        if 0 <= it - 2 < total:
            k = it - 2
            core_copy(k, 1 - core).wait_recv()
            if k < n_out:
                send_out(wbuf.at[k], wout_all.at[:, :, :, :, k * CHUNK:(k + 1) * CHUNK])
                if k == n_out - 1:
                    project_back()
            else:
                send_out(wbuf.at[k], wqkv_all.at[:, :, :, :, (k - n_out) * CHUNK:(k - n_out + 1) * CHUNK])
                multiply(1, k - n_out, (0, 1))
        if it < 4:
            turn(grad, 2, it)
        if it == 4:
            send_out(turned.at[2], grad_turned)
        if 8 <= it < 12:
            turn(normed.at[1], 1, it - 8)
        if it == 12:
            send_out(turned.at[1], turned_own)
        if it in (4, 8):
            prior_next(it // 4 - 1)
        if it in (5, 9, 13):
            i = it // 4 - 1
            prior_landed(i)
            normalize(prior, 0, i)
            turn(normed.at[0], 0, i)
        if it - 2 - n_out >= n_qkv // 3:
            multiply(0, it - 2 - n_out, (0,))

    prior_landed(3)
    normalize(prior, 0, 3)
    turn(normed.at[0], 0, 3)
    send_out(prior, prior_all)
    send_out(normed.at[0], normed_prior)
    send_out(turned.at[0], turned_prior)
    for j in range(n_qkv // 3, n_qkv):
        multiply(0, j, (1,))

    @pl.when(has_next)
    def _():
        for i in (2, 3):
            prior_copy(i).wait_send()
    for k in range(total):
        for d in range(1, levels):
            z_copy(k, d).wait_send()
        y_copy(k, y).wait_send()
        core_copy(k, core).wait_send()
    for copy in outs:
        copy.wait()


def gather_all(rows, seqs, w_out, w_qkv, x, grad, vec_own, cosine, sine):
    tokens, width = x.shape
    share, levels = width // rows, rows // 4
    bf, f32 = jnp.bfloat16, jnp.float32
    vmem, hbm = pl.BlockSpec(memory_space=pltpu.VMEM), pl.BlockSpec(memory_space=pl.ANY)
    dma = pltpu.SemaphoreType.DMA
    total = 4 * width // CHUNK
    shape = jax.ShapeDtypeStruct
    token, turned = shape((tokens, width), bf), shape((width, tokens), bf)
    wout_all, wqkv_all, normed, normed_prior, turned_own, turned_prior, grad_turned, mixed, d_att, prior, vec = pl.pallas_call(
        functools.partial(gather_kernel, (rows, seqs, tokens, width)),
        out_shape=[shape((levels, 2, 2, share, width), bf), shape((levels, 2, 2, share, 3 * width), bf), token, token,
                   turned, turned, turned, shape((2, tokens, 3 * width), bf), token, token, shape((8, width), f32)],
        in_specs=[hbm, hbm, hbm, vmem, vmem, vmem, vmem],
        out_specs=[hbm] * 10 + [vmem],
        scratch_shapes=[
            pltpu.VMEM((total, levels, 2, 2, share, CHUNK), bf),
            pltpu.VMEM((tokens, width), bf), pltpu.VMEM((tokens, width), bf), pltpu.VMEM((2, tokens, width), bf), pltpu.VMEM((3, width, tokens), bf),
            pltpu.VMEM((2, tokens, 3 * width), bf), pltpu.VMEM((tokens, width), bf),
            pltpu.VMEM((3, 8, width), f32), pltpu.VMEM((1 + levels, 8, width), f32),
            dma, dma((total,)), dma((5 * total,)), dma((total, levels - 1)), dma((total, levels - 1)),
            dma((total,)), dma((total,)), dma((total,)), dma((total,)), dma((4,)), dma((4,)), dma((1 + levels,)), dma((1 + levels,)),
        ],
        compiler_params=pltpu.CompilerParams(collective_id=0, has_side_effects=True, vmem_limit_bytes=60 * 2**20),
        cost_estimate=pl.CostEstimate(flops=20 * 10**9, bytes_accessed=40 * 2**20, transcendentals=0),
        name="gather",
    )(w_out, w_qkv, x, grad, vec_own, cosine, sine)
    return (wout_all.reshape(width, width), wqkv_all.reshape(width, 3 * width), normed, normed_prior, turned_own, turned_prior,
            grad_turned, mixed.reshape(2 * tokens, 3 * width), d_att, prior, vec)


RING = 12
SLOTS = 6


def reduce_kernel(dims, g_q, g_k, g_v, g_out, normed, normed_t, grad, grad_t, x_ref, w_in, w_back, b_in, base_out, base_dn,
                  vec_in, o_qkv, o_out, o_in, o_back, o_vec, block_out, d_normed,
                  buf, core_recv, chip, x_recv, y_recv, part, z_recv, fin, fin_recv, res, acc_out, hidden, d_pre, win_buf, wback_buf,
                  vec, vec_recv, load_sem, acc_sem, w_sem, send_sem, recv_sem, zsend_sem, zrecv_sem, vsend_sem, vrecv_sem):
    rows, seqs, q_rows, edge, tokens, width, ff = dims
    bf, f32 = jnp.bfloat16, jnp.float32
    levels = rows // 4
    region = q_rows - edge
    r, s = lax.axis_index("rows"), lax.axis_index("seq")
    core, y, z = lax.rem(r, 2), lax.rem(r // 2, 2), r // 4
    odd = lax.rem(s, 2)
    core_id = {"rows": r + 1 - 2 * core}
    y_id = {"rows": r + 2 - 4 * y}
    flip = lambda bit: {"seq": s + bit - 2 * bit * lax.rem(s // bit, 2)}
    z_of = lambda d: lax.rem(z + d, levels)
    z_id = lambda d: {"rows": z_of(d) * 4 + lax.rem(r, 4)}
    bits = []
    while 2 ** (len(bits) + 1) < seqs:
        bits.append(2 ** (len(bits) + 1))
    finals = bits + [1]

    barrier = pltpu.get_barrier_semaphore()
    partners = [core_id, y_id] + [z_id(d) for d in range(1, levels)] + [flip(b) for b in finals]
    for partner in partners:
        pl.semaphore_signal(barrier, inc=1, device_id=partner, device_id_type=MESH)
    pl.semaphore_wait(barrier, len(partners))

    piece = q_rows // 4
    n_qkv, n_out, n_in, n_back = 3 * width // 512, width // 512, ff // 512, width // 128
    n_first = n_qkv + n_out
    n_mlp = n_first + n_in
    total = n_mlp + n_back
    own_rows = pl.ds(pl.multiple_of(odd * edge, edge), region)
    c_mine = pl.ds(pl.multiple_of(odd * (q_rows - edge), edge), edge)
    c_other = pl.ds(pl.multiple_of((1 - odd) * (q_rows - edge), edge), edge)

    def remote(src, dst, stage, slot, target):
        return pltpu.make_async_remote_copy(src, dst, send_sem.at[stage, slot], recv_sem.at[stage, slot],
                                            device_id=target, device_id_type=MESH)

    def core_copy(k):
        return remote(buf.at[lax.rem(k, RING), :, 1 - core], core_recv.at[lax.rem(k, SLOTS)], 0, lax.rem(k, SLOTS), core_id)

    def x_copy(k):
        t = lax.rem(k, SLOTS)
        return remote(chip.at[t, :, :, c_other], x_recv.at[t], 1, t, flip(1))

    def y_copy(k):
        t = lax.rem(k, SLOTS)
        return remote(chip.at[t, :, 1 - y, own_rows], y_recv.at[t], 2, t, y_id)

    def z_copy(k, d):
        t = lax.rem(k, SLOTS)
        return pltpu.make_async_remote_copy(part.at[t, z_of(d)], z_recv.at[t, d - 1], zsend_sem.at[d - 1, t],
                                            zrecv_sem.at[d - 1, t], device_id=z_id(d), device_id_type=MESH)

    def fin_copy(k, i):
        t = lax.rem(k, SLOTS)
        return remote(fin.at[t, i], fin_recv.at[t, i], 3 + i, t, flip(finals[i]))

    def load_copies(source, col, k):
        slot = lax.rem(k, RING)
        return [pltpu.make_async_copy(source.at[:, :, :, pl.ds(pl.multiple_of(col + 128 * j, 128), 128)],
                                      buf.at[slot, :, :, pl.ds(j * piece, piece)], load_sem.at[j]) for j in range(4)]

    def load(k):
        for i, source in enumerate((g_q, g_k, g_v, g_out)):
            @pl.when((k >= i * n_out) & (k < (i + 1) * n_out))
            def _():
                for copy in load_copies(source, (k - i * n_out) * 512, k):
                    copy.start()

    def weights(j):
        t = lax.rem(j, 2)
        cols = pl.ds(pl.multiple_of(j * 512, 512), 512)
        return [pltpu.make_async_copy(w_in.at[:, cols], win_buf.at[t], w_sem.at[0, t]),
                pltpu.make_async_copy(w_back.at[cols, :], wback_buf.at[t], w_sem.at[1, t])]

    starts = [pltpu.make_async_copy(base_out, acc_out, acc_sem.at[0]), pltpu.make_async_copy(base_dn, d_normed, acc_sem.at[1])]
    for copy in weights(0) + starts:
        copy.start()
    load(0)

    def mlp(j):
        @pl.when(j == 0)
        def _():
            for copy in starts:
                copy.wait()
        for copy in weights(j):
            copy.wait()

        @pl.when(j + 1 < n_in)
        def _():
            for copy in weights(j + 1):
                copy.start()
        t = lax.rem(j, 2)
        cols = pl.ds(pl.multiple_of(j * 512, 512), 512)
        tall = 512
        bias = b_in[:, cols]

        def rows_step(i, sums):
            block = pl.ds(pl.multiple_of(i * tall, tall), tall)
            pre = dot_n(normed[block, :], win_buf[t]) + bias
            up = dot_t(grad[block, :], wback_buf[t])
            square = pre * pre
            turn = jnp.tanh(pre * (GELU_COEF + (GELU_COEF * 0.044715) * square))
            half = 0.5 + 0.5 * turn
            hid = (pre * half).astype(bf)
            slope = half + (0.5 * pre) * (1.0 - turn * turn) * (GELU_COEF + (3 * 0.044715 * GELU_COEF) * square)
            down = (up * slope).astype(bf)
            hidden[block, cols] = hid
            d_pre[block, :] = down
            acc_out[block, :] += dot_n(hid, wback_buf[t])
            d_normed[block, :] += dot_t(down, win_buf[t])
            return sums + jnp.sum(down.astype(f32), axis=0, keepdims=True)
        sums = lax.fori_loop(0, tokens // tall, rows_step, jnp.zeros((1, 512), f32))
        vec[pl.ds(3 + j // 2, 1), pl.ds(pl.multiple_of(lax.rem(j, 2) * 512, 512), 512)] = sums
        slot = lax.rem(n_first + j, RING)
        per = 8
        big = per * width // rows

        def grads_step(i, _):
            value = dot_n(normed_t[pl.ds(pl.multiple_of(i * big, big), big), :], d_pre[...]).astype(bf)
            for m in range(per):
                for a in range(4):
                    buf[slot, i * (per // 2) + m // 2, m % 2, a * piece:(a + 1) * piece, :] = (
                        value[m * piece:(m + 1) * piece, a * 128:(a + 1) * 128])
            return 0
        lax.fori_loop(0, rows // per, grads_step, 0)

    def finish_tokens():
        gain = vec_in[0:1, :]
        bias = vec_in[1:2, :]
        back = jnp.zeros((1, width), f32)
        tall = 256
        def step(i, sums):
            gain, bias, back = sums
            block = pl.ds(pl.multiple_of(i * tall, tall), tall)
            block_out[block, :] = acc_out[block, :].astype(bf)
            values = x_ref[block, :].astype(f32)
            centered = values - jnp.mean(values, axis=1, keepdims=True)
            unit = centered * lax.rsqrt(jnp.mean(centered * centered, axis=1, keepdims=True) + EPS)
            d = d_normed[block, :]
            return (gain + jnp.sum(d * unit, axis=0, keepdims=True), bias + jnp.sum(d, axis=0, keepdims=True),
                    back + jnp.sum(grad[block, :].astype(f32), axis=0, keepdims=True))
        gain, bias, back = lax.fori_loop(0, tokens // tall, step, (gain, bias, back))
        vec[0:1, :] = gain
        vec[1:2, :] = bias
        vec[2:3, :] = back
        vec[7:8, :] = jnp.zeros((1, width), f32)

    def back_grads(j):
        value = dot_n(grad_t[pl.ds(pl.multiple_of(j * 128, 128), 128), :], hidden[...]).astype(bf)
        slot = lax.rem(n_mlp + j, RING)
        parts = q_rows // 128
        for d in range(rows):
            for a in range(parts):
                buf[slot, d // 2, d % 2, a * 128:(a + 1) * 128, :] = value[:, (d * parts + a) * 128:(d * parts + a + 1) * 128]

    def vec_copy(i, target):
        return pltpu.make_async_remote_copy(vec, vec_recv.at[i], vsend_sem.at[i], vrecv_sem.at[i],
                                            device_id=target, device_id_type=MESH)
    vec_stages = [[(0, core_id)], [(1, y_id)], [(2 + d - 1, z_id(d)) for d in range(1, levels)]]
    vec_stages += [[(1 + levels + i, flip(b))] for i, b in enumerate(finals)]

    def store(k):
        def place(out, col):
            for j in range(4):
                out[:, pl.ds(pl.multiple_of(col + 128 * j, 128), 128)] = res[j * piece:(j + 1) * piece, :]

        @pl.when(k < n_qkv)
        def _():
            place(o_qkv, k * 512)

        @pl.when((k >= n_qkv) & (k < n_first))
        def _():
            place(o_out, (k - n_qkv) * 512)

        @pl.when((k >= n_first) & (k < n_mlp))
        def _():
            place(o_in, (k - n_first) * 512)

        @pl.when(k >= n_mlp)
        def _():
            for a in range(q_rows // 128):
                o_back[a * 128:(a + 1) * 128, pl.ds(pl.multiple_of((k - n_mlp) * 128, 128), 128)] = (
                    res[a * 128:(a + 1) * 128, :].T)

    def stage(lag, it, body):
        k = it - lag

        @pl.when((k >= 0) & (k < total))
        def _():
            body(k, lax.rem(k, SLOTS))

    def send_first(k, t):
        @pl.when(k < n_first)
        def _():
            for copy in load_copies(g_q, 0, k):
                copy.wait()
        load(k + 1)
        core_copy(k).start()

    def core_add(k, t):
        core_copy(k).wait()
        slot = lax.rem(k, RING)
        for i in range(rows // 2):
            chip[t, i // 2, i % 2] = buf[slot, i, core] + core_recv[t, i]
        x_copy(k).start()

    def x_add(k, t):
        x_copy(k).wait()
        for i in range(rows // 2):
            chip[t, i // 2, i % 2, c_mine] = chip[t, i // 2, i % 2, c_mine] + x_recv[t, i // 2, i % 2]
        y_copy(k).start()

    def y_add(k, t):
        y_copy(k).wait()
        for i in range(levels):
            part[t, i] = chip[t, i, y, own_rows] + y_recv[t, i]
        for d in range(1, levels):
            z_copy(k, d).start()

    def z_add(k, t):
        for d in range(1, levels):
            z_copy(k, d).wait()
        value = part[t, z].astype(f32)
        for d in range(1, levels):
            value = value + z_recv[t, d - 1].astype(f32)
        fin[t, 0] = value.astype(bf)
        fin_copy(k, 0).start()

    def fin_add(i):
        def body(k, t):
            fin_copy(k, i).wait()
            fin[t, i + 1] = fin[t, i] + fin_recv[t, i]
            fin_copy(k, i + 1).start()
        return body

    def last(k, t):
        i = len(finals) - 1
        fin_copy(k, i).wait()
        middle = q_rows - 2 * edge
        at = lambda start, size: pl.ds(pl.multiple_of(start, edge), size)
        res[c_mine, :] = fin[t, i, at(odd * middle, edge)].astype(f32)
        res[c_other, :] = fin_recv[t, i, at((1 - odd) * middle, edge)].astype(f32)
        res[edge:q_rows - edge, :] = (fin[t, i, at((1 - odd) * edge, middle)].astype(f32)
                                      + fin_recv[t, i, at(odd * edge, middle)].astype(f32))
        store(k)

    pipeline = [send_first, core_add, x_add, y_add, z_add] + [fin_add(i) for i in range(len(bits))] + [last]

    def step(it, _):
        for lag, body in enumerate(pipeline):
            stage(2 * lag, it, body)

        @pl.when(it < n_in)
        def _():
            mlp(it)

        @pl.when(it == n_in)
        def _():
            finish_tokens()
            for i, target in vec_stages[0]:
                vec_copy(i, target).start()
        for number, stages in enumerate(vec_stages):
            @pl.when(it == n_in + 1 + number)
            def _():
                for i, target in stages:
                    vec_copy(i, target).wait()
                value = vec[...]
                for i, target in stages:
                    value = value + vec_recv[i]
                if number + 1 < len(vec_stages):
                    vec[...] = value
                    for i, target in vec_stages[number + 1]:
                        vec_copy(i, target).start()
                else:
                    o_vec[...] = value

        @pl.when((it >= n_in) & (it < n_in + n_back))
        def _():
            back_grads(it - n_in)
        return 0
    lax.fori_loop(0, total + 2 * len(pipeline) - 2, step, 0)


def reduce_all(rows, seqs, g_q, g_k, g_v, g_out, normed, normed_t, grad, grad_t, x, w_in, w_back, b_in, base_out, base_dn, vec_in):
    tokens, width = normed.shape
    ff = w_in.shape[1]
    share = width // rows
    q_rows = 4 * share
    edge = q_rows // 4
    levels = rows // 4
    region = q_rows - edge
    finals = max(1, (seqs - 1).bit_length())
    bf, f32 = jnp.bfloat16, jnp.float32
    vmem, hbm = pl.BlockSpec(memory_space=pltpu.VMEM), pl.BlockSpec(memory_space=pl.ANY)
    dma = pltpu.SemaphoreType.DMA
    return pl.pallas_call(
        functools.partial(reduce_kernel, (rows, seqs, q_rows, edge, tokens, width, ff)),
        out_shape=[jax.ShapeDtypeStruct((share, 3 * width), f32), jax.ShapeDtypeStruct((share, width), f32),
                   jax.ShapeDtypeStruct((share, ff), f32), jax.ShapeDtypeStruct((ff // rows, width), f32),
                   jax.ShapeDtypeStruct((8, width), f32), jax.ShapeDtypeStruct((tokens, width), bf),
                   jax.ShapeDtypeStruct((tokens, width), f32)],
        in_specs=[hbm, hbm, hbm, hbm, vmem, vmem, vmem, vmem, vmem, hbm, hbm, vmem, hbm, hbm, vmem],
        out_specs=[vmem] * 7,
        scratch_shapes=[
            pltpu.VMEM((RING, rows // 2, 2, q_rows, 128), bf),
            pltpu.VMEM((SLOTS, rows // 2, q_rows, 128), bf),
            pltpu.VMEM((SLOTS, levels, 2, q_rows, 128), bf),
            pltpu.VMEM((SLOTS, levels, 2, edge, 128), bf),
            pltpu.VMEM((SLOTS, levels, region, 128), bf),
            pltpu.VMEM((SLOTS, levels, region, 128), bf),
            pltpu.VMEM((SLOTS, levels - 1, region, 128), bf),
            pltpu.VMEM((SLOTS, finals, region, 128), bf),
            pltpu.VMEM((SLOTS, finals, region, 128), bf),
            pltpu.VMEM((q_rows, 128), f32),
            pltpu.VMEM((tokens, width), f32),
            pltpu.VMEM((tokens, ff), bf),
            pltpu.VMEM((tokens, 512), bf),
            pltpu.VMEM((2, width, 512), bf),
            pltpu.VMEM((2, 512, width), bf),
            pltpu.VMEM((8, width), f32),
            pltpu.VMEM((1 + levels + finals, 8, width), f32),
            dma((4,)), dma((2,)), dma((2, 2)), dma((3 + finals, SLOTS)), dma((3 + finals, SLOTS)),
            dma((levels - 1, SLOTS)), dma((levels - 1, SLOTS)), dma((1 + levels + finals,)), dma((1 + levels + finals,)),
        ],
        compiler_params=pltpu.CompilerParams(collective_id=1, has_side_effects=True, vmem_limit_bytes=62 * 2**20),
        cost_estimate=pl.CostEstimate(flops=100 * 10**9, bytes_accessed=100 * 2**20, transcendentals=0),
        name="reduce",
    )(*[g.reshape(rows // 2, 2, share, width) for g in (g_q, g_k, g_v, g_out)], normed, normed_t, grad, grad_t, x,
      w_in, w_back, b_in, base_out, base_dn, vec_in)


def body(block_input, lengths, norm_gain, norm_bias, w_qkv, w_attn_out, w_fc_in, b_fc_in, w_fc_out, b_fc_out, cotangent):
    f32, bf = jnp.float32, jnp.bfloat16
    rows, seqs = lax.axis_size("rows"), lax.axis_size("seq")
    inputs = block_input[0].astype(f32)
    tokens, width = inputs.shape
    own_lengths = lengths[0]
    count = own_lengths.shape[0]
    first = lax.axis_index("seq") * tokens
    index = first - tokens + jnp.arange(2 * tokens, dtype=jnp.int32)
    order = np.arange(count)
    ends = jnp.sum(jnp.where(order[None, :] <= order[:, None], own_lengths[None, :], 0), axis=1)
    begin = jnp.sum(jnp.where(ends[None, :] <= index[:, None], own_lengths[None, :], 0), axis=1)
    cosine, sine = rope_tables(index - begin)
    starts = (begin - first + tokens)[tokens:]
    lows = starts[::BQ] // BQ

    share, wide = width // rows, 4 * width // rows
    r = lax.axis_index("rows")
    place = lambda vector, lines: jnp.where(np.arange(lines * width).reshape(rows, -1) // (lines * share) == r,
                                            vector.astype(f32)[None, :], 0.0).reshape(lines, width)
    vec_own = jnp.concatenate([place(norm_gain, 1), place(norm_bias, 1), place(b_fc_out, 1), place(b_fc_in, 4),
                               jnp.zeros((1, width), f32)])
    grad_out = cotangent[0]
    (w_out_all, w_qkv_all, normed, normed_prior, turned_own, turned_prior, grad_turned, mixed, d_attended, prior_input,
     vectors) = gather_all(
        rows, seqs, w_attn_out, w_qkv, block_input[0], grad_out, vec_own, cosine, sine)
    w_fc_in, w_fc_out, vectors = lax.optimization_barrier((w_fc_in, w_fc_out, vectors))
    w_in_all = lax.all_gather(w_fc_in, "rows", axis=0, tiled=True)
    w_back_all = lax.all_gather(w_fc_out, "rows", axis=0, tiled=True)
    gain, bias, b_back_all = vectors[0], vectors[1], vectors[2]
    b_in_all = vectors[3:7].reshape(1, 4 * width)
    unit, scale = layer_norm_stats(inputs)
    prior_unit, _ = layer_norm_stats(prior_input.astype(f32))
    attended, attended_turned, d_q, d_k, d_v = attention(lows, starts, cosine, sine, mixed, d_attended)

    d_normed_both = jnp.dot(d_k, w_qkv_all[:, width:2 * width].T, preferred_element_type=f32) + jnp.dot(
        d_v, w_qkv_all[:, 2 * width:].T, preferred_element_type=f32)
    d_prior = d_normed_both[:tokens]
    back = lax.ppermute(d_prior.astype(bf), "seq", [(i + 1, i) for i in range(seqs - 1)])
    vec_in = jnp.stack([jnp.sum(d_prior * prior_unit, axis=0), jnp.sum(d_prior, axis=0)])
    product = lambda turned, values: jnp.dot(turned, values, preferred_element_type=f32)
    grads = [product(turned_own, d_q).astype(bf),
             (product(turned_own, d_k[tokens:]) + product(turned_prior, d_k[:tokens])).astype(bf),
             (product(turned_own, d_v[tokens:]) + product(turned_prior, d_v[:tokens])).astype(bf)]
    grad_w_out = product(attended_turned, grad_out).astype(bf)
    base_dn = d_normed_both[tokens:] + jnp.dot(d_q, w_qkv_all[:, :width].T, preferred_element_type=f32)
    base_out = inputs + jnp.dot(attended, w_out_all, preferred_element_type=f32) + b_back_all

    g_qkv, g_out, g_in, g_back, vec, block_output, d_normed = reduce_all(
        rows, seqs, *grads, grad_w_out, normed, turned_own, grad_out, grad_turned, block_input[0], w_in_all, w_back_all,
        b_in_all, base_out, base_dn, vec_in)

    d_normed = d_normed + back.astype(f32)
    d_unit = d_normed * gain
    d_input = (d_unit - jnp.mean(d_unit, axis=1, keepdims=True)
               - unit * jnp.mean(d_unit * unit, axis=1, keepdims=True)) * scale
    grad_input = d_input + grad_out.astype(f32)
    own = lambda vector, size: lax.dynamic_slice_in_dim(vector, r * size, size)
    return (block_output[None], grad_input[None], own(vec[0], share), own(vec[1], share), g_qkv, g_out, g_in,
            own(vec[3:7].reshape(4 * width), wide), g_back, own(vec[2], share))


def solution(mesh):
    vector, matrix, tokens = P("rows"), P("rows", None), P("rows", "seq", None)
    in_specs = (tokens, matrix, vector, vector, matrix, matrix, matrix, vector, matrix, vector, tokens)
    out_specs = (tokens, tokens, vector, vector, matrix, matrix, matrix, vector, matrix, vector)
    return jax.shard_map(body, mesh=mesh, in_specs=in_specs, out_specs=out_specs, check_vma=False)
```

```python
import functools

import jax
import jax.numpy as jnp
import numpy as np
from jax import lax
from jax.experimental import pallas as pl
from jax.experimental.pallas import tpu as pltpu
from jax.sharding import PartitionSpec as P

HEADS = 16
HEAD = 64
ROT = 32
EPS = 1e-05
GELU_COEF = 0.7978845608028654
MESH = pl.DeviceIdType.MESH

NEG = -1e30
BQ = 256
PAIRS = 4

def dot_t(a, b):
    return lax.dot_general(a, b, (((1,), (1,)), ((), ())), preferred_element_type=jnp.float32)

def dot_n(a, b):
    return lax.dot_general(a, b, (((1,), (0,)), ((), ())), preferred_element_type=jnp.float32)

def dot_c(a, b):
    return lax.dot_general(a, b, (((0,), (0,)), ((), ())), preferred_element_type=jnp.float32)

def attention_kernel(pairs, tokens, lows, start_row, cos_ref, sin_ref, q_ref, k_ref, v_ref, do_ref,
                     out_ref, turned_ref, dq_ref, dk_ref, dv_ref, bias, scores, weights, k_turned, v_turned, dk_acc, dv_acc, out_acc, dq_acc, slope):
    bf, f32 = jnp.bfloat16, jnp.float32
    blocks = tokens // BQ
    span = blocks + 1
    heads = 2 * pairs
    even = lax.broadcasted_iota(jnp.int32, (BQ, 128), 1) < HEAD
    fold = lambda x, op: op(x.reshape(BQ // 8, 8, BQ), axis=0)

    @pl.when(pl.program_id(0) == 0)
    def _():
        for qb in range(blocks):
            start = start_row[:, qb * BQ:(qb + 1) * BQ]
            query = tokens + qb * BQ + lax.broadcasted_iota(jnp.int32, (BQ, BQ), 1)

            def fill(kb, _):
                key = kb * BQ + lax.broadcasted_iota(jnp.int32, (BQ, BQ), 0)
                bias[qb * span + kb - qb] = jnp.where((key >= start) & (key <= query), 0.0, NEG).astype(bf)
                return 0
            lax.fori_loop(lows[qb], blocks + qb + 1, fill, 0)

    def prepare(kb, _):
        rows = pl.ds(pl.multiple_of(kb * BQ, BQ), BQ)
        for p in range(pairs):
            cols = slice(p * 128, (p + 1) * 128)
            k_turned[p, :, rows] = k_ref[rows, cols].T
            v_turned[p, :, rows] = v_ref[rows, cols].T
        return 0
    lax.fori_loop(lows[0], 2 * blocks, prepare, 0)
    dk_acc[...] = jnp.zeros_like(dk_acc)
    dv_acc[...] = jnp.zeros_like(dv_acc)

    def one_q(qb, _):
        q_rows = pl.ds(pl.multiple_of(qb * BQ, BQ), BQ)
        own_rows = pl.ds(pl.multiple_of(tokens + qb * BQ, BQ), BQ)
        low, high = lows[qb], blocks + qb + 1
        q_h = []
        for p in range(pairs):
            q = q_ref[q_rows, p * 128:(p + 1) * 128]
            q_h += [jnp.where(even, q, 0), jnp.where(even, 0, q)]

        def score(kb, tops):
            rows = pl.ds(pl.multiple_of(kb * BQ, BQ), BQ)
            b = bias[qb * span + kb - qb].astype(f32)
            new = []
            for h in range(heads):
                s = dot_t(k_ref[rows, (h // 2) * 128:(h // 2 + 1) * 128], q_h[h]) + b
                scores[kb - qb, h] = s
                new.append(jnp.maximum(tops[h], fold(s, jnp.max)))
            return tuple(new)
        tops = lax.fori_loop(low, high, score, tuple(jnp.full((8, BQ), NEG, f32) for _ in range(heads)))
        tops = [jnp.max(t, axis=0, keepdims=True) for t in tops]
        out_acc[...] = jnp.zeros_like(out_acc)
        dq_acc[...] = jnp.zeros_like(dq_acc)

        def attend(kb, sums):
            rows = pl.ds(pl.multiple_of(kb * BQ, BQ), BQ)
            new = []
            for h in range(heads):
                e = jnp.exp(scores[kb - qb, h] - tops[h])
                new.append(sums[h] + fold(e, jnp.sum))
                e = e.astype(bf)
                weights[kb - qb, h] = e
            for h in range(heads):
                half = slice((h % 2) * HEAD, (h % 2 + 1) * HEAD)
                out_acc[h // 2, half, :] += dot_n(v_turned[h // 2, half, rows], weights[kb - qb, h])
            return tuple(new)
        sums = lax.fori_loop(low, high, attend, tuple(jnp.zeros((8, BQ), f32) for _ in range(heads)))

        do_h, deltas = [], []
        for p in range(pairs):
            cols = slice(p * 128, (p + 1) * 128)
            inverse = [1.0 / jnp.sum(sums[h], axis=0, keepdims=True) for h in (2 * p, 2 * p + 1)]
            inverse = jnp.concatenate([jnp.broadcast_to(v, (HEAD, BQ)) for v in inverse], axis=0)
            out = out_acc[p] * inverse
            out_ref[q_rows, cols] = out.T.astype(bf)
            turned_ref[cols, q_rows] = out.astype(bf)
            d_out = do_ref[q_rows, cols].astype(f32).T * inverse
            product = out * d_out
            deltas += [jnp.sum(product[:HEAD], axis=0, keepdims=True), jnp.sum(product[HEAD:], axis=0, keepdims=True)]
            d_out = d_out.T.astype(bf)
            do_h += [jnp.where(even, d_out, 0), jnp.where(even, 0, d_out)]

        def back(kb, _):
            rows = pl.ds(pl.multiple_of(kb * BQ, BQ), BQ)
            for p in range(pairs):
                v = v_ref[rows, p * 128:(p + 1) * 128]
                for h in (2 * p, 2 * p + 1):
                    d_prob = dot_t(v, do_h[h])
                    slope[h] = (weights[kb - qb, h].astype(f32) * (d_prob - deltas[h])).astype(bf)
            for p in range(pairs):
                cols = slice(p * 128, (p + 1) * 128)
                dv_acc[rows, cols] += dot_n(weights[kb - qb, 2 * p], do_h[2 * p]) + dot_n(weights[kb - qb, 2 * p + 1], do_h[2 * p + 1])
                dk_acc[rows, cols] += dot_n(slope[2 * p], q_h[2 * p]) + dot_n(slope[2 * p + 1], q_h[2 * p + 1])
            for h in range(heads):
                half = slice((h % 2) * HEAD, (h % 2 + 1) * HEAD)
                dq_acc[h // 2, half, :] += dot_n(k_turned[h // 2, half, rows], slope[h])
            return 0
        lax.fori_loop(low, high, back, 0)
        for p in range(pairs):
            dq_ref[q_rows, p * 128:(p + 1) * 128] = unrotate(
                dq_acc[p].T * 0.125, cos_ref[own_rows, :], sin_ref[own_rows, :]).astype(bf)
        return 0
    lax.fori_loop(0, blocks, one_q, 0)

    def finish(kb, _):
        rows = pl.ds(pl.multiple_of(kb * BQ, BQ), BQ)
        for p in range(pairs):
            cols = slice(p * 128, (p + 1) * 128)
            dk_ref[rows, cols] = unrotate(dk_acc[rows, cols], cos_ref[rows, :], sin_ref[rows, :]).astype(bf)
            dv_ref[rows, cols] = dv_acc[rows, cols].astype(bf)
        return 0
    lax.fori_loop(0, 2 * blocks, finish, 0)


def swap_pairs(x):
    odd = lax.broadcasted_iota(jnp.int32, x.shape, 1) % 2 == 1
    n = x.shape[1]
    return jnp.where(odd, pltpu.roll(x, 1, 1), pltpu.roll(x, n - 1, 1))

def rotate(x, cosine, sine):
    return x * cosine + swap_pairs(x) * sine

def unrotate(x, cosine, sine):
    return x * cosine - swap_pairs(x) * sine

def attention(lows, starts, cosine, sine, mixed, d_out):
    tokens, width = d_out.shape
    pairs = PAIRS
    wide = 128 * pairs
    groups = width // wide
    blocks = tokens // BQ
    whole = lambda shape: pl.BlockSpec(shape, lambda g, lows: (0,) * len(shape), pipeline_mode=pl.Buffered(1))
    own = pl.BlockSpec((tokens, wide), lambda g, lows: (0, g))
    both = pl.BlockSpec((2 * tokens, wide), lambda g, lows: (0, g))
    q_spec = pl.BlockSpec((tokens, wide), lambda g, lows: (1, g))
    k_spec = pl.BlockSpec((2 * tokens, wide), lambda g, lows: (0, groups + g))
    v_spec = pl.BlockSpec((2 * tokens, wide), lambda g, lows: (0, 2 * groups + g))
    bf, f32 = jnp.bfloat16, jnp.float32
    slots = blocks * (blocks + 1)
    one, two = jax.ShapeDtypeStruct((tokens, width), bf), jax.ShapeDtypeStruct((2 * tokens, width), bf)
    return pl.pallas_call(
        functools.partial(attention_kernel, pairs, tokens),
        out_shape=[one, jax.ShapeDtypeStruct((width, tokens), bf), one, two, two],
        grid_spec=pltpu.PrefetchScalarGridSpec(
            num_scalar_prefetch=1,
            grid=(groups,),
            in_specs=[whole((1, tokens)), whole((2 * tokens, 128)), whole((2 * tokens, 128)), q_spec, k_spec, v_spec, own],
            out_specs=[own, pl.BlockSpec((wide, tokens), lambda g, lows: (g, 0)), own, both, both],
            scratch_shapes=[pltpu.VMEM((slots, BQ, BQ), bf), pltpu.VMEM((blocks + 1, 2 * pairs, BQ, BQ), f32),
                            pltpu.VMEM((blocks + 1, 2 * pairs, BQ, BQ), bf), pltpu.VMEM((pairs, 128, 2 * tokens), bf),
                            pltpu.VMEM((pairs, 128, 2 * tokens), bf), pltpu.VMEM((2 * tokens, wide), f32),
                            pltpu.VMEM((2 * tokens, wide), f32), pltpu.VMEM((pairs, 128, BQ), f32),
                            pltpu.VMEM((pairs, 128, BQ), f32), pltpu.VMEM((2 * pairs, BQ, BQ), bf)],
        ),
        compiler_params=pltpu.CompilerParams(vmem_limit_bytes=62 * 2**20),
        cost_estimate=pl.CostEstimate(flops=60 * 10**9, bytes_accessed=30 * 2**20, transcendentals=0),
        name="attention",
    )(lows, starts[None, :], cosine, sine, mixed, mixed, mixed, d_out)


def rope_tables(position):
    lane = np.arange(128) % HEAD
    freqs = np.where(lane < ROT, 10000.0 ** (-2.0 * (lane // 2) / ROT), 0.0).astype(np.float32)
    sign = np.where(lane % 2 == 0, -1.0, 1.0).astype(np.float32)
    angles = position.astype(jnp.float32)[:, None] * freqs[None, :]
    return jnp.cos(angles), jnp.sin(angles) * sign[None, :]


def layer_norm_stats(values):
    mean = jnp.mean(values, axis=1, keepdims=True)
    centered = values - mean
    spread = jnp.mean(centered * centered, axis=1, keepdims=True)
    scale = lax.rsqrt(spread + EPS)
    return centered * scale, scale


CHUNK = 256
AHEAD = 3


def gather_kernel(dims, w_out, w_qkv, x_hbm, grad, vec_own, cos_ref, sin_ref,
                  wout_all, wqkv_all, normed_own, normed_prior, turned_own, turned_prior, grad_turned, mixed_all, d_attended, prior_all, vec_all,
                  wbuf, own, prior, normed, turned, mixed, d_att, vec, vec_recv, in_sem, load_sem, out_sem, zsend, zrecv, ysend, yrecv,
                  csend, crecv, psend, precv, vsend, vrecv):
    rows, seqs, tokens, width = dims
    bf, f32 = jnp.bfloat16, jnp.float32
    levels = rows // 4
    r, s = lax.axis_index("rows"), lax.axis_index("seq")
    core, y, z = lax.rem(r, 2), lax.rem(r // 2, 2), r // 4
    core_id = {"rows": r + 1 - 2 * core}
    y_id = {"rows": r + 2 - 4 * y}
    z_of = lambda d: lax.rem(z + d, levels)
    z_id = lambda d: {"rows": z_of(d) * 4 + lax.rem(r, 4)}
    has_next, has_prior = s < seqs - 1, s > 0
    n_out, n_qkv = width // CHUNK, 3 * width // CHUNK
    total = n_out + n_qkv
    quarter = tokens // 4

    def load(k):
        source = w_out if k < n_out else w_qkv
        col = (k if k < n_out else k - n_out) * CHUNK
        return pltpu.make_async_copy(source.at[:, col:col + CHUNK], wbuf.at[k, z, y, core], load_sem.at[k])

    fetch = pltpu.make_async_copy(x_hbm, own, in_sem)
    fetch.start()
    for k in range(total):
        load(k).start()

    barrier = pltpu.get_barrier_semaphore()
    partners = [core_id, y_id] + [z_id(d) for d in range(1, levels)]
    for partner in partners:
        pl.semaphore_signal(barrier, inc=1, device_id=partner, device_id_type=MESH)

    @pl.when(has_next)
    def _():
        pl.semaphore_signal(barrier, inc=1, device_id={"seq": s + 1}, device_id_type=MESH)

    @pl.when(has_prior)
    def _():
        pl.semaphore_signal(barrier, inc=1, device_id={"seq": s - 1}, device_id_type=MESH)
    pl.semaphore_wait(barrier, len(partners) + jnp.where(has_next, 1, 0) + jnp.where(has_prior, 1, 0))

    def prior_copy(i):
        block = pl.ds(i * quarter, quarter)
        return pltpu.make_async_remote_copy(x_hbm.at[block], prior.at[block], psend.at[i], precv.at[i],
                                            device_id={"seq": jnp.minimum(s + 1, seqs - 1)}, device_id_type=MESH)

    def vec_copy(i, target):
        return pltpu.make_async_remote_copy(vec.at[i], vec_recv.at[i], vsend.at[i], vrecv.at[i],
                                            device_id=target, device_id_type=MESH)

    def z_vec(d):
        return pltpu.make_async_remote_copy(vec.at[0], vec_recv.at[1 + d], vsend.at[1 + d], vrecv.at[1 + d],
                                            device_id=z_id(d), device_id_type=MESH)

    def z_copy(k, d):
        mine = wbuf.at[k, z, y, core]
        return pltpu.make_async_remote_copy(mine, mine, zsend.at[k, d - 1], zrecv.at[k, d - 1],
                                            device_id=z_id(d), device_id_type=MESH)

    def z_landed(k, d):
        theirs = wbuf.at[k, z_of(levels - d), y, core]
        return pltpu.make_async_remote_copy(theirs, theirs, zsend.at[k, d - 1], zrecv.at[k, d - 1],
                                            device_id=z_id(d), device_id_type=MESH)

    def y_copy(k, side):
        part = wbuf.at[k, :, side, core]
        return pltpu.make_async_remote_copy(part, part, ysend.at[k], yrecv.at[k], device_id=y_id, device_id_type=MESH)

    def core_copy(k, side):
        part = wbuf.at[k, :, :, side]
        return pltpu.make_async_remote_copy(part, part, csend.at[k], crecv.at[k], device_id=core_id, device_id_type=MESH)

    vec[0] = vec_own[...]
    for d in range(1, levels):
        z_vec(d).start()

    @pl.when(has_next)
    def _():
        for i in range(2):
            prior_copy(i).start()

    @pl.when(jnp.logical_not(has_prior))
    def _():
        prior[...] = jnp.zeros_like(prior)

    def z_start(k):
        load(k).wait()
        for d in range(1, levels):
            z_copy(k, d).start()
    for k in range(AHEAD):
        z_start(k)

    swap = pltpu.make_async_remote_copy(vec.at[2], vec_recv.at[0], vsend.at[0], vrecv.at[0], device_id=core_id,
                                        device_id_type=MESH)

    def share_vectors(it):
        if it == 0:
            for d in range(1, levels):
                z_vec(d).wait()
            value = vec[0]
            for d in range(1, levels):
                value = value + vec_recv[1 + d]
            vec[1] = value
            vec_copy(1, y_id).start()
        if it == 1:
            vec_copy(1, y_id).wait()
            vec[2] = vec[1] + vec_recv[1]
            swap.start()
        if it == 2:
            swap.wait()
            vec_all[...] = vec[2] + vec_recv[0]

    def normalize(source, half, i):
        block = slice(i * quarter, (i + 1) * quarter)
        values = source[block, :].astype(f32)
        centered = values - jnp.mean(values, axis=1, keepdims=True)
        unit = centered * lax.rsqrt(jnp.mean(centered * centered, axis=1, keepdims=True) + EPS)
        normed[half, block, :] = (unit * vec_all[0:1, :] + vec_all[1:2, :]).astype(bf)

    def turn(source, place, i):
        block = slice(i * quarter, (i + 1) * quarter)
        turned[place, :, block] = source[block, :].T

    outs = []

    def send_out(src, dst):
        copy = pltpu.make_async_copy(src, dst, out_sem.at[len(outs)])
        copy.start()
        outs.append(copy)

    def multiply(half, j, parts):
        cols = slice(j * CHUNK, (j + 1) * CHUNK)
        tall = tokens // 2
        for i in parts:
            block = slice(i * tall, (i + 1) * tall)
            product = dot_n(normed[half, block, :], wbuf[n_out + j].reshape(width, CHUNK))
            if j * CHUNK < 2 * width:
                scale = 0.125 if j * CHUNK < width else 1.0
                place = slice(half * tokens + i * tall, half * tokens + (i + 1) * tall)
                cosine, sine = cos_ref[place, :] * scale, sin_ref[place, :] * scale
                for a in range(CHUNK // 128):
                    mixed[half, block, j * CHUNK + a * 128:j * CHUNK + (a + 1) * 128] = rotate(
                        product[:, a * 128:(a + 1) * 128], cosine, sine).astype(bf)
            else:
                mixed[half, block, cols] = product.astype(bf)
            send_out(mixed.at[half, block, cols], mixed_all.at[half, block, cols])

    def project_back():
        tall = tokens // 4

        def body(i, _):
            block = pl.ds(pl.multiple_of(i * tall, tall), tall)
            value = dot_t(grad[block, 0:CHUNK], wbuf[0].reshape(width, CHUNK))
            for k in range(1, n_out):
                value = value + dot_t(grad[block, k * CHUNK:(k + 1) * CHUNK], wbuf[k].reshape(width, CHUNK))
            d_att[block, :] = value.astype(bf)
            return 0
        lax.fori_loop(0, 4, body, 0)
        send_out(d_att, d_attended)

    def prior_landed(i):
        @pl.when(has_prior)
        def _():
            prior_copy(i).wait_recv()

    def prior_next(i):
        @pl.when(has_next)
        def _():
            prior_copy(i).wait_send()
            prior_copy(i + 2).start()

    for it in range(total + 2):
        if it < total:
            for d in range(1, levels):
                z_landed(it, d).wait_recv()
            if it + AHEAD < total:
                z_start(it + AHEAD)
            y_copy(it, y).start()
        if 0 <= it - 1 < total:
            y_copy(it - 1, 1 - y).wait_recv()
            core_copy(it - 1, core).start()
        share_vectors(it)
        if it == 3:
            fetch.wait()
        if 3 <= it <= 4:
            normalize(own, 1, 2 * it - 6)
            normalize(own, 1, 2 * it - 5)
        if it == 5:
            send_out(normed.at[1], normed_own)
        if 0 <= it - 2 < total:
            k = it - 2
            core_copy(k, 1 - core).wait_recv()
            if k < n_out:
                send_out(wbuf.at[k], wout_all.at[:, :, :, :, k * CHUNK:(k + 1) * CHUNK])
                if k == n_out - 1:
                    project_back()
            else:
                send_out(wbuf.at[k], wqkv_all.at[:, :, :, :, (k - n_out) * CHUNK:(k - n_out + 1) * CHUNK])
                multiply(1, k - n_out, (0, 1))
        if it < 4:
            turn(grad, 2, it)
        if it == 4:
            send_out(turned.at[2], grad_turned)
        if 8 <= it < 12:
            turn(normed.at[1], 1, it - 8)
        if it == 12:
            send_out(turned.at[1], turned_own)
        if it in (4, 8):
            prior_next(it // 4 - 1)
        if it in (5, 9, 13):
            i = it // 4 - 1
            prior_landed(i)
            normalize(prior, 0, i)
            turn(normed.at[0], 0, i)
        if it - 2 - n_out >= n_qkv // 3:
            multiply(0, it - 2 - n_out, (0,))

    prior_landed(3)
    normalize(prior, 0, 3)
    turn(normed.at[0], 0, 3)
    send_out(prior, prior_all)
    send_out(normed.at[0], normed_prior)
    send_out(turned.at[0], turned_prior)
    for j in range(n_qkv // 3, n_qkv):
        multiply(0, j, (1,))

    @pl.when(has_next)
    def _():
        for i in (2, 3):
            prior_copy(i).wait_send()
    for k in range(total):
        for d in range(1, levels):
            z_copy(k, d).wait_send()
        y_copy(k, y).wait_send()
        core_copy(k, core).wait_send()
    for copy in outs:
        copy.wait()


def gather_all(rows, seqs, w_out, w_qkv, x, grad, vec_own, cosine, sine):
    tokens, width = x.shape
    share, levels = width // rows, rows // 4
    bf, f32 = jnp.bfloat16, jnp.float32
    vmem, hbm = pl.BlockSpec(memory_space=pltpu.VMEM), pl.BlockSpec(memory_space=pl.ANY)
    dma = pltpu.SemaphoreType.DMA
    total = 4 * width // CHUNK
    shape = jax.ShapeDtypeStruct
    token, turned = shape((tokens, width), bf), shape((width, tokens), bf)
    wout_all, wqkv_all, normed, normed_prior, turned_own, turned_prior, grad_turned, mixed, d_att, prior, vec = pl.pallas_call(
        functools.partial(gather_kernel, (rows, seqs, tokens, width)),
        out_shape=[shape((levels, 2, 2, share, width), bf), shape((levels, 2, 2, share, 3 * width), bf), token, token,
                   turned, turned, turned, shape((2, tokens, 3 * width), bf), token, token, shape((8, width), f32)],
        in_specs=[hbm, hbm, hbm, vmem, vmem, vmem, vmem],
        out_specs=[hbm] * 10 + [vmem],
        scratch_shapes=[
            pltpu.VMEM((total, levels, 2, 2, share, CHUNK), bf),
            pltpu.VMEM((tokens, width), bf), pltpu.VMEM((tokens, width), bf), pltpu.VMEM((2, tokens, width), bf), pltpu.VMEM((3, width, tokens), bf),
            pltpu.VMEM((2, tokens, 3 * width), bf), pltpu.VMEM((tokens, width), bf),
            pltpu.VMEM((3, 8, width), f32), pltpu.VMEM((1 + levels, 8, width), f32),
            dma, dma((total,)), dma((5 * total,)), dma((total, levels - 1)), dma((total, levels - 1)),
            dma((total,)), dma((total,)), dma((total,)), dma((total,)), dma((4,)), dma((4,)), dma((1 + levels,)), dma((1 + levels,)),
        ],
        compiler_params=pltpu.CompilerParams(collective_id=0, has_side_effects=True, vmem_limit_bytes=60 * 2**20),
        cost_estimate=pl.CostEstimate(flops=20 * 10**9, bytes_accessed=40 * 2**20, transcendentals=0),
        name="gather",
    )(w_out, w_qkv, x, grad, vec_own, cosine, sine)
    return (wout_all.reshape(width, width), wqkv_all.reshape(width, 3 * width), normed, normed_prior, turned_own, turned_prior,
            grad_turned, mixed.reshape(2 * tokens, 3 * width), d_att, prior, vec)


RING = 6
SLOTS = 6


def reduce_kernel(dims, g_q, g_k, g_v, g_out, normed, normed_t, grad, grad_t, x_ref, w_in, w_back, b_in, base_out, base_dn,
                  vec_in, gain_in, returned, o_qkv, o_out, o_in, o_back, o_vec, block_out, d_normed,
                  buf, core_recv, chip, x_recv, y_recv, part, z_recv, fin, fin_recv, res, acc_out, hidden, d_pre, win_buf, wback_buf,
                  came, vec, vec_recv, came_sem, load_sem, acc_sem, w_sem, send_sem, recv_sem, zsend_sem, zrecv_sem, vsend_sem, vrecv_sem):
    rows, seqs, q_rows, edge, tokens, width, ff = dims
    bf, f32 = jnp.bfloat16, jnp.float32
    levels = rows // 4
    region = q_rows - edge
    r, s = lax.axis_index("rows"), lax.axis_index("seq")
    core, y, z = lax.rem(r, 2), lax.rem(r // 2, 2), r // 4
    odd = lax.rem(s, 2)
    core_id = {"rows": r + 1 - 2 * core}
    y_id = {"rows": r + 2 - 4 * y}
    flip = lambda bit: {"seq": s + bit - 2 * bit * lax.rem(s // bit, 2)}
    z_of = lambda d: lax.rem(z + d, levels)
    z_id = lambda d: {"rows": z_of(d) * 4 + lax.rem(r, 4)}
    bits = []
    while 2 ** (len(bits) + 1) < seqs:
        bits.append(2 ** (len(bits) + 1))
    finals = bits + [1]

    barrier = pltpu.get_barrier_semaphore()
    partners = [core_id, y_id] + [z_id(d) for d in range(1, levels)] + [flip(b) for b in finals]
    for partner in partners:
        pl.semaphore_signal(barrier, inc=1, device_id=partner, device_id_type=MESH)
    pl.semaphore_wait(barrier, len(partners))

    piece = q_rows // 4
    n_qkv, n_out, n_in, n_back = 3 * width // 512, width // 512, ff // 512, width // 128
    n_first = n_qkv + n_out
    n_mlp = n_first + n_in
    assert n_first == n_in
    ready = lambda k: (k < n_mlp) & (lax.rem(k, 2) == 0)
    total = n_mlp + n_back
    own_rows = pl.ds(pl.multiple_of(odd * edge, edge), region)
    c_mine = pl.ds(pl.multiple_of(odd * (q_rows - edge), edge), edge)
    c_other = pl.ds(pl.multiple_of((1 - odd) * (q_rows - edge), edge), edge)

    def remote(src, dst, stage, slot, target):
        return pltpu.make_async_remote_copy(src, dst, send_sem.at[stage, slot], recv_sem.at[stage, slot],
                                            device_id=target, device_id_type=MESH)

    def core_copy(k):
        return remote(buf.at[lax.rem(k, RING), :, 1 - core], core_recv.at[lax.rem(k, SLOTS)], 0, lax.rem(k, SLOTS), core_id)

    def x_copy(k):
        t = lax.rem(k, SLOTS)
        return remote(chip.at[t, :, :, c_other], x_recv.at[t], 1, t, flip(1))

    def y_copy(k):
        t = lax.rem(k, SLOTS)
        return remote(chip.at[t, :, 1 - y, own_rows], y_recv.at[t], 2, t, y_id)

    def z_copy(k, d):
        t = lax.rem(k, SLOTS)
        return pltpu.make_async_remote_copy(part.at[t, z_of(d)], z_recv.at[t, d - 1], zsend_sem.at[d - 1, t],
                                            zrecv_sem.at[d - 1, t], device_id=z_id(d), device_id_type=MESH)

    def fin_copy(k, i):
        t = lax.rem(k, SLOTS)
        return remote(fin.at[t, i], fin_recv.at[t, i], 3 + i, t, flip(finals[i]))

    def load_copies(source, col, k):
        slot = lax.rem(k, RING)
        return [pltpu.make_async_copy(source.at[:, :, :, pl.ds(pl.multiple_of(col + 128 * j, 128), 128)],
                                      buf.at[slot, :, :, pl.ds(j * piece, piece)], load_sem.at[j]) for j in range(4)]

    def load(k):
        for i, source in enumerate((g_q, g_k, g_v, g_out)):
            @pl.when(ready(k) & (k // 2 >= i * n_out) & (k // 2 < (i + 1) * n_out))
            def _():
                for copy in load_copies(source, (k // 2 - i * n_out) * 512, k):
                    copy.start()

    def weights(j):
        t = lax.rem(j, 2)
        cols = pl.ds(pl.multiple_of(j * 512, 512), 512)
        return [pltpu.make_async_copy(w_in.at[:, cols], win_buf.at[t], w_sem.at[0, t]),
                pltpu.make_async_copy(w_back.at[cols, :], wback_buf.at[t], w_sem.at[1, t])]

    starts = [pltpu.make_async_copy(base_out, acc_out, acc_sem.at[0]), pltpu.make_async_copy(base_dn, d_normed, acc_sem.at[1])]
    for copy in weights(0) + starts:
        copy.start()
    load(0)

    def mlp(j):
        @pl.when(j == 0)
        def _():
            for copy in starts:
                copy.wait()
        for copy in weights(j):
            copy.wait()

        @pl.when(j + 1 < n_in)
        def _():
            for copy in weights(j + 1):
                copy.start()
        t = lax.rem(j, 2)
        cols = pl.ds(pl.multiple_of(j * 512, 512), 512)
        tall = 512
        bias = b_in[:, cols]

        def rows_step(i, sums):
            block = pl.ds(pl.multiple_of(i * tall, tall), tall)
            pre = dot_n(normed[block, :], win_buf[t]) + bias
            up = dot_t(grad[block, :], wback_buf[t])
            square = pre * pre
            turn = jnp.tanh(pre * (GELU_COEF + (GELU_COEF * 0.044715) * square))
            half = 0.5 + 0.5 * turn
            hid = (pre * half).astype(bf)
            slope = half + (0.5 * pre) * (1.0 - turn * turn) * (GELU_COEF + (3 * 0.044715 * GELU_COEF) * square)
            down = (up * slope).astype(bf)
            hidden[block, cols] = hid
            d_pre[block, :] = down
            acc_out[block, :] += dot_n(hid, wback_buf[t])
            d_normed[block, :] += dot_t(down, win_buf[t])
            return sums + jnp.sum(down.astype(f32), axis=0, keepdims=True)
        sums = lax.fori_loop(0, tokens // tall, rows_step, jnp.zeros((1, 512), f32))
        vec[pl.ds(3 + j // 2, 1), pl.ds(pl.multiple_of(lax.rem(j, 2) * 512, 512), 512)] = sums
        slot = lax.rem(2 * j + 1, RING)
        per = 8
        big = per * width // rows

        def grads_step(i, _):
            value = dot_n(normed_t[pl.ds(pl.multiple_of(i * big, big), big), :], d_pre[...]).astype(bf)
            for m in range(per):
                for a in range(4):
                    buf[slot, i * (per // 2) + m // 2, m % 2, a * piece:(a + 1) * piece, :] = (
                        value[m * piece:(m + 1) * piece, a * 128:(a + 1) * 128])
            return 0
        lax.fori_loop(0, rows // per, grads_step, 0)

    tall_end = tokens // 4

    def returned_copy(i):
        return pltpu.make_async_copy(returned.at[pl.ds(pl.multiple_of(i * tall_end, tall_end), tall_end)], came, came_sem)

    def finish_tokens(i):
        @pl.when(i == 0)
        def _():
            returned_copy(0).start()
            vec[0:2, :] = vec_in[...]
            vec[2:3, :] = jnp.zeros((1, width), f32)
            vec[7:8, :] = jnp.zeros((1, width), f32)
        returned_copy(i).wait()
        small = tall_end // 4

        def part(n, sums):
            gain, bias, back = sums
            block = pl.ds(pl.multiple_of(i * tall_end + n * small, small), small)
            block_out[block, :] = acc_out[block, :].astype(bf)
            values = x_ref[block, :].astype(f32)
            centered = values - jnp.mean(values, axis=1, keepdims=True)
            scale = lax.rsqrt(jnp.mean(centered * centered, axis=1, keepdims=True) + EPS)
            unit = centered * scale
            d = d_normed[block, :]
            g = grad[block, :].astype(f32)
            d_unit = (d + came[pl.ds(pl.multiple_of(n * small, small), small), :].astype(f32)) * gain_in[...]
            inner = jnp.mean(d_unit * unit, axis=1, keepdims=True)
            d_normed[block, :] = g + (d_unit - jnp.mean(d_unit, axis=1, keepdims=True) - unit * inner) * scale
            return (gain + jnp.sum(d * unit, axis=0, keepdims=True), bias + jnp.sum(d, axis=0, keepdims=True),
                    back + jnp.sum(g, axis=0, keepdims=True))
        sums = lax.fori_loop(0, 4, part, (vec[0:1, :], vec[1:2, :], vec[2:3, :]))
        for row in range(3):
            vec[row:row + 1, :] = sums[row]

        @pl.when(i < 3)
        def _():
            returned_copy(i + 1).start()

    def back_grads(j):
        value = dot_n(grad_t[pl.ds(pl.multiple_of(j * 128, 128), 128), :], hidden[...]).astype(bf)
        slot = lax.rem(n_mlp + j, RING)
        parts = q_rows // 128
        for d in range(rows):
            for a in range(parts):
                buf[slot, d // 2, d % 2, a * 128:(a + 1) * 128, :] = value[:, (d * parts + a) * 128:(d * parts + a + 1) * 128]

    def vec_copy(i, target):
        return pltpu.make_async_remote_copy(vec, vec_recv.at[i], vsend_sem.at[i], vrecv_sem.at[i],
                                            device_id=target, device_id_type=MESH)
    vec_stages = [[(0, core_id)], [(1, y_id)], [(2 + d - 1, z_id(d)) for d in range(1, levels)]]
    vec_stages += [[(1 + levels + i, flip(b))] for i, b in enumerate(finals)]

    def store(k):
        def place(out, col):
            for j in range(4):
                out[:, pl.ds(pl.multiple_of(col + 128 * j, 128), 128)] = res[j * piece:(j + 1) * piece, :]

        @pl.when(ready(k) & (k < 2 * n_qkv))
        def _():
            place(o_qkv, (k // 2) * 512)

        @pl.when(ready(k) & (k >= 2 * n_qkv))
        def _():
            place(o_out, (k // 2 - n_qkv) * 512)

        @pl.when((k < n_mlp) & (lax.rem(k, 2) == 1))
        def _():
            place(o_in, (k // 2) * 512)

        @pl.when(k >= n_mlp)
        def _():
            for a in range(q_rows // 128):
                o_back[a * 128:(a + 1) * 128, pl.ds(pl.multiple_of((k - n_mlp) * 128, 128), 128)] = (
                    res[a * 128:(a + 1) * 128, :].T)

    def stage(lag, it, body):
        k = it - lag

        @pl.when((k >= 0) & (k < total))
        def _():
            body(k, lax.rem(k, SLOTS))

    def send_first(k, t):
        @pl.when(ready(k))
        def _():
            for copy in load_copies(g_q, 0, k):
                copy.wait()
        load(k + 1)
        core_copy(k).start()

    def core_add(k, t):
        core_copy(k).wait()
        slot = lax.rem(k, RING)
        for i in range(rows // 2):
            chip[t, i // 2, i % 2] = buf[slot, i, core] + core_recv[t, i]
        x_copy(k).start()

    def x_add(k, t):
        x_copy(k).wait()
        for i in range(rows // 2):
            chip[t, i // 2, i % 2, c_mine] = chip[t, i // 2, i % 2, c_mine] + x_recv[t, i // 2, i % 2]
        y_copy(k).start()

    def y_add(k, t):
        y_copy(k).wait()
        for i in range(levels):
            part[t, i] = chip[t, i, y, own_rows] + y_recv[t, i]
        for d in range(1, levels):
            z_copy(k, d).start()

    def z_add(k, t):
        for d in range(1, levels):
            z_copy(k, d).wait()
        value = part[t, z].astype(f32)
        for d in range(1, levels):
            value = value + z_recv[t, d - 1].astype(f32)
        fin[t, 0] = value.astype(bf)
        fin_copy(k, 0).start()

    def fin_add(i):
        def body(k, t):
            fin_copy(k, i).wait()
            fin[t, i + 1] = fin[t, i] + fin_recv[t, i]
            fin_copy(k, i + 1).start()
        return body

    def last(k, t):
        i = len(finals) - 1
        fin_copy(k, i).wait()
        middle = q_rows - 2 * edge
        at = lambda start, size: pl.ds(pl.multiple_of(start, edge), size)
        res[c_mine, :] = fin[t, i, at(odd * middle, edge)].astype(f32)
        res[c_other, :] = fin_recv[t, i, at((1 - odd) * middle, edge)].astype(f32)
        res[edge:q_rows - edge, :] = (fin[t, i, at((1 - odd) * edge, middle)].astype(f32)
                                      + fin_recv[t, i, at(odd * edge, middle)].astype(f32))
        store(k)

    pipeline = [send_first, core_add, x_add, y_add, z_add] + [fin_add(i) for i in range(len(bits))] + [last]

    def step(it, _):
        for lag, body in enumerate(pipeline):
            stage(2 * lag, it, body)

        @pl.when((it < n_mlp) & (lax.rem(it, 2) == 0))
        def _():
            mlp(it // 2)

        @pl.when((it >= n_mlp - 1) & (it < n_mlp + 3))
        def _():
            finish_tokens(it - (n_mlp - 1))

        @pl.when(it == n_mlp + 2)
        def _():
            for i, target in vec_stages[0]:
                vec_copy(i, target).start()
        for number, stages in enumerate(vec_stages):
            @pl.when(it == n_mlp + 4 + 2 * number)
            def _():
                for i, target in stages:
                    vec_copy(i, target).wait()
                value = vec[...]
                for i, target in stages:
                    value = value + vec_recv[i]
                if number + 1 < len(vec_stages):
                    vec[...] = value
                    for i, target in vec_stages[number + 1]:
                        vec_copy(i, target).start()
                else:
                    o_vec[...] = value

        @pl.when((it >= n_mlp - 1) & (it < total - 1))
        def _():
            back_grads(it - (n_mlp - 1))
        return 0
    lax.fori_loop(0, total + 2 * len(pipeline) - 2, step, 0)


def reduce_all(rows, seqs, g_q, g_k, g_v, g_out, normed, normed_t, grad, grad_t, x, w_in, w_back, b_in, base_out, base_dn, vec_in, gain,
               returned):
    tokens, width = normed.shape
    ff = w_in.shape[1]
    share = width // rows
    q_rows = 4 * share
    edge = q_rows // 4
    levels = rows // 4
    region = q_rows - edge
    finals = max(1, (seqs - 1).bit_length())
    bf, f32 = jnp.bfloat16, jnp.float32
    vmem, hbm = pl.BlockSpec(memory_space=pltpu.VMEM), pl.BlockSpec(memory_space=pl.ANY)
    dma = pltpu.SemaphoreType.DMA
    return pl.pallas_call(
        functools.partial(reduce_kernel, (rows, seqs, q_rows, edge, tokens, width, ff)),
        out_shape=[jax.ShapeDtypeStruct((share, 3 * width), f32), jax.ShapeDtypeStruct((share, width), f32),
                   jax.ShapeDtypeStruct((share, ff), f32), jax.ShapeDtypeStruct((ff // rows, width), f32),
                   jax.ShapeDtypeStruct((8, width), f32), jax.ShapeDtypeStruct((tokens, width), bf),
                   jax.ShapeDtypeStruct((tokens, width), f32)],
        in_specs=[hbm, hbm, hbm, hbm, vmem, vmem, vmem, vmem, vmem, hbm, hbm, vmem, hbm, hbm, vmem, vmem, hbm],
        out_specs=[vmem] * 7,
        scratch_shapes=[
            pltpu.VMEM((RING, rows // 2, 2, q_rows, 128), bf),
            pltpu.VMEM((SLOTS, rows // 2, q_rows, 128), bf),
            pltpu.VMEM((SLOTS, levels, 2, q_rows, 128), bf),
            pltpu.VMEM((SLOTS, levels, 2, edge, 128), bf),
            pltpu.VMEM((SLOTS, levels, region, 128), bf),
            pltpu.VMEM((SLOTS, levels, region, 128), bf),
            pltpu.VMEM((SLOTS, levels - 1, region, 128), bf),
            pltpu.VMEM((SLOTS, finals, region, 128), bf),
            pltpu.VMEM((SLOTS, finals, region, 128), bf),
            pltpu.VMEM((q_rows, 128), f32),
            pltpu.VMEM((tokens, width), f32),
            pltpu.VMEM((tokens, ff), bf),
            pltpu.VMEM((tokens, 512), bf),
            pltpu.VMEM((2, width, 512), bf),
            pltpu.VMEM((2, 512, width), bf),
            pltpu.VMEM((tokens // 4, width), bf),
            pltpu.VMEM((8, width), f32),
            pltpu.VMEM((1 + levels + finals, 8, width), f32),
            dma,
            dma((4,)), dma((2,)), dma((2, 2)), dma((3 + finals, SLOTS)), dma((3 + finals, SLOTS)),
            dma((levels - 1, SLOTS)), dma((levels - 1, SLOTS)), dma((1 + levels + finals,)), dma((1 + levels + finals,)),
        ],
        compiler_params=pltpu.CompilerParams(collective_id=1, has_side_effects=True, vmem_limit_bytes=62 * 2**20),
        cost_estimate=pl.CostEstimate(flops=100 * 10**9, bytes_accessed=100 * 2**20, transcendentals=0),
        name="reduce",
    )(*[g.reshape(rows // 2, 2, share, width) for g in (g_q, g_k, g_v, g_out)], normed, normed_t, grad, grad_t, x,
      w_in, w_back, b_in, base_out, base_dn, vec_in, gain, returned)


def body(block_input, lengths, norm_gain, norm_bias, w_qkv, w_attn_out, w_fc_in, b_fc_in, w_fc_out, b_fc_out, cotangent):
    f32, bf = jnp.float32, jnp.bfloat16
    rows, seqs = lax.axis_size("rows"), lax.axis_size("seq")
    inputs = block_input[0].astype(f32)
    tokens, width = inputs.shape
    own_lengths = lengths[0]
    count = own_lengths.shape[0]
    first = lax.axis_index("seq") * tokens
    index = first - tokens + jnp.arange(2 * tokens, dtype=jnp.int32)
    order = np.arange(count)
    ends = jnp.sum(jnp.where(order[None, :] <= order[:, None], own_lengths[None, :], 0), axis=1)
    begin = jnp.sum(jnp.where(ends[None, :] <= index[:, None], own_lengths[None, :], 0), axis=1)
    cosine, sine = rope_tables(index - begin)
    starts = (begin - first + tokens)[tokens:]
    lows = starts[::BQ] // BQ

    share, wide = width // rows, 4 * width // rows
    r = lax.axis_index("rows")
    place = lambda vector, lines: jnp.where(np.arange(lines * width).reshape(rows, -1) // (lines * share) == r,
                                            vector.astype(f32)[None, :], 0.0).reshape(lines, width)
    vec_own = jnp.concatenate([place(norm_gain, 1), place(norm_bias, 1), place(b_fc_out, 1), place(b_fc_in, 4),
                               jnp.zeros((1, width), f32)])
    grad_out = cotangent[0]
    (w_out_all, w_qkv_all, normed, normed_prior, turned_own, turned_prior, grad_turned, mixed, d_attended, prior_input,
     vectors) = gather_all(
        rows, seqs, w_attn_out, w_qkv, block_input[0], grad_out, vec_own, cosine, sine)
    w_fc_in, w_fc_out, vectors = lax.optimization_barrier((w_fc_in, w_fc_out, vectors))
    w_in_all = lax.all_gather(w_fc_in, "rows", axis=0, tiled=True)
    w_back_all = lax.all_gather(w_fc_out, "rows", axis=0, tiled=True)
    gain, bias, b_back_all = vectors[0], vectors[1], vectors[2]
    b_in_all = vectors[3:7].reshape(1, 4 * width)
    prior_unit, _ = layer_norm_stats(prior_input.astype(f32))
    attended, attended_turned, d_q, d_k, d_v = attention(lows, starts, cosine, sine, mixed, d_attended)

    d_normed_both = jnp.dot(d_k, w_qkv_all[:, width:2 * width].T, preferred_element_type=f32) + jnp.dot(
        d_v, w_qkv_all[:, 2 * width:].T, preferred_element_type=f32)
    d_prior = d_normed_both[:tokens]
    back = lax.ppermute(d_prior.astype(bf), "seq", [(i + 1, i) for i in range(seqs - 1)])
    vec_in = jnp.stack([jnp.sum(d_prior * prior_unit, axis=0), jnp.sum(d_prior, axis=0)])
    product = lambda turned, values: jnp.dot(turned, values, preferred_element_type=f32)
    grads = [product(turned_own, d_q).astype(bf),
             (product(turned_own, d_k[tokens:]) + product(turned_prior, d_k[:tokens])).astype(bf),
             (product(turned_own, d_v[tokens:]) + product(turned_prior, d_v[:tokens])).astype(bf)]
    grad_w_out = product(attended_turned, grad_out).astype(bf)
    base_dn = d_normed_both[tokens:] + jnp.dot(d_q, w_qkv_all[:, :width].T, preferred_element_type=f32)
    base_out = inputs + jnp.dot(attended, w_out_all, preferred_element_type=f32) + b_back_all

    g_qkv, g_out, g_in, g_back, vec, block_output, grad_input = reduce_all(
        rows, seqs, *grads, grad_w_out, normed, turned_own, grad_out, grad_turned, block_input[0], w_in_all, w_back_all,
        b_in_all, base_out, base_dn, vec_in, gain[None], back)

    own = lambda vector, size: lax.dynamic_slice_in_dim(vector, r * size, size)
    return (block_output[None], grad_input[None], own(vec[0], share), own(vec[1], share), g_qkv, g_out, g_in,
            own(vec[3:7].reshape(4 * width), wide), g_back, own(vec[2], share))


def solution(mesh):
    vector, matrix, tokens = P("rows"), P("rows", None), P("rows", "seq", None)
    in_specs = (tokens, matrix, vector, vector, matrix, matrix, matrix, vector, matrix, vector, tokens)
    out_specs = (tokens, tokens, vector, vector, matrix, matrix, matrix, vector, matrix, vector)
    return jax.shard_map(body, mesh=mesh, in_specs=in_specs, out_specs=out_specs, check_vma=False)
```

```python
import functools

import jax
import jax.numpy as jnp
import numpy as np
from jax import lax
from jax.experimental import pallas as pl
from jax.experimental.pallas import tpu as pltpu
from jax.sharding import PartitionSpec as P

HEADS = 16
HEAD = 64
ROT = 32
EPS = 1e-05
GELU_COEF = 0.7978845608028654
MESH = pl.DeviceIdType.MESH

NEG = -1e30
BQ = 256
PAIRS = 4

def dot_t(a, b):
    return lax.dot_general(a, b, (((1,), (1,)), ((), ())), preferred_element_type=jnp.float32)

def dot_n(a, b):
    return lax.dot_general(a, b, (((1,), (0,)), ((), ())), preferred_element_type=jnp.float32)

def dot_c(a, b):
    return lax.dot_general(a, b, (((0,), (0,)), ((), ())), preferred_element_type=jnp.float32)

def attention_kernel(pairs, tokens, lows, start_row, cos_ref, sin_ref, q_ref, k_ref, v_ref, do_ref,
                     out_ref, turned_ref, dq_ref, dk_ref, dv_ref, bias, scores, weights, k_turned, v_turned, dk_acc, dv_acc, out_acc, dq_acc, slope):
    bf, f32 = jnp.bfloat16, jnp.float32
    blocks = tokens // BQ
    span = blocks + 1
    heads = 2 * pairs
    even = lax.broadcasted_iota(jnp.int32, (BQ, 128), 1) < HEAD
    fold = lambda x, op: op(x.reshape(BQ // 8, 8, BQ), axis=0)

    @pl.when(pl.program_id(0) == 0)
    def _():
        for qb in range(blocks):
            start = start_row[:, qb * BQ:(qb + 1) * BQ]
            query = tokens + qb * BQ + lax.broadcasted_iota(jnp.int32, (BQ, BQ), 1)

            def fill(kb, _):
                key = kb * BQ + lax.broadcasted_iota(jnp.int32, (BQ, BQ), 0)
                bias[qb * span + kb - qb] = jnp.where((key >= start) & (key <= query), 0.0, NEG).astype(bf)
                return 0
            lax.fori_loop(lows[qb], blocks + qb + 1, fill, 0)

    def prepare(kb, _):
        rows = pl.ds(pl.multiple_of(kb * BQ, BQ), BQ)
        for p in range(pairs):
            cols = slice(p * 128, (p + 1) * 128)
            k_turned[p, :, rows] = k_ref[rows, cols].T
            v_turned[p, :, rows] = v_ref[rows, cols].T
        return 0
    lax.fori_loop(lows[0], 2 * blocks, prepare, 0)
    dk_acc[...] = jnp.zeros_like(dk_acc)
    dv_acc[...] = jnp.zeros_like(dv_acc)

    def one_q(qb, _):
        q_rows = pl.ds(pl.multiple_of(qb * BQ, BQ), BQ)
        own_rows = pl.ds(pl.multiple_of(tokens + qb * BQ, BQ), BQ)
        low, high = lows[qb], blocks + qb + 1
        q_h = []
        for p in range(pairs):
            q = q_ref[q_rows, p * 128:(p + 1) * 128]
            q_h += [jnp.where(even, q, 0), jnp.where(even, 0, q)]

        def score(kb, tops):
            rows = pl.ds(pl.multiple_of(kb * BQ, BQ), BQ)
            b = bias[qb * span + kb - qb].astype(f32)
            new = []
            for h in range(heads):
                s = dot_t(k_ref[rows, (h // 2) * 128:(h // 2 + 1) * 128], q_h[h]) + b
                scores[kb - qb, h] = s
                new.append(jnp.maximum(tops[h], fold(s, jnp.max)))
            return tuple(new)
        tops = lax.fori_loop(low, high, score, tuple(jnp.full((8, BQ), NEG, f32) for _ in range(heads)))
        tops = [jnp.max(t, axis=0, keepdims=True) for t in tops]
        out_acc[...] = jnp.zeros_like(out_acc)
        dq_acc[...] = jnp.zeros_like(dq_acc)

        def attend(kb, sums):
            rows = pl.ds(pl.multiple_of(kb * BQ, BQ), BQ)
            new = []
            for h in range(heads):
                e = jnp.exp(scores[kb - qb, h] - tops[h])
                new.append(sums[h] + fold(e, jnp.sum))
                e = e.astype(bf)
                weights[kb - qb, h] = e
            for h in range(heads):
                half = slice((h % 2) * HEAD, (h % 2 + 1) * HEAD)
                out_acc[h // 2, half, :] += dot_n(v_turned[h // 2, half, rows], weights[kb - qb, h])
            return tuple(new)
        sums = lax.fori_loop(low, high, attend, tuple(jnp.zeros((8, BQ), f32) for _ in range(heads)))

        do_h, deltas = [], []
        for p in range(pairs):
            cols = slice(p * 128, (p + 1) * 128)
            inverse = [1.0 / jnp.sum(sums[h], axis=0, keepdims=True) for h in (2 * p, 2 * p + 1)]
            inverse = jnp.concatenate([jnp.broadcast_to(v, (HEAD, BQ)) for v in inverse], axis=0)
            out = out_acc[p] * inverse
            out_ref[q_rows, cols] = out.T.astype(bf)
            turned_ref[cols, q_rows] = out.astype(bf)
            d_out = do_ref[q_rows, cols].astype(f32).T * inverse
            product = out * d_out
            deltas += [jnp.sum(product[:HEAD], axis=0, keepdims=True), jnp.sum(product[HEAD:], axis=0, keepdims=True)]
            d_out = d_out.T.astype(bf)
            do_h += [jnp.where(even, d_out, 0), jnp.where(even, 0, d_out)]

        def back(kb, _):
            rows = pl.ds(pl.multiple_of(kb * BQ, BQ), BQ)
            for p in range(pairs):
                v = v_ref[rows, p * 128:(p + 1) * 128]
                for h in (2 * p, 2 * p + 1):
                    d_prob = dot_t(v, do_h[h])
                    slope[h] = (weights[kb - qb, h].astype(f32) * (d_prob - deltas[h])).astype(bf)
            for p in range(pairs):
                cols = slice(p * 128, (p + 1) * 128)
                dv_acc[rows, cols] += dot_n(weights[kb - qb, 2 * p], do_h[2 * p]) + dot_n(weights[kb - qb, 2 * p + 1], do_h[2 * p + 1])
                dk_acc[rows, cols] += dot_n(slope[2 * p], q_h[2 * p]) + dot_n(slope[2 * p + 1], q_h[2 * p + 1])
            for h in range(heads):
                half = slice((h % 2) * HEAD, (h % 2 + 1) * HEAD)
                dq_acc[h // 2, half, :] += dot_n(k_turned[h // 2, half, rows], slope[h])
            return 0
        lax.fori_loop(low, high, back, 0)
        for p in range(pairs):
            dq_ref[q_rows, p * 128:(p + 1) * 128] = unrotate(
                dq_acc[p].T * 0.125, cos_ref[own_rows, :], sin_ref[own_rows, :]).astype(bf)
        return 0
    lax.fori_loop(0, blocks, one_q, 0)

    def finish(kb, _):
        rows = pl.ds(pl.multiple_of(kb * BQ, BQ), BQ)
        for p in range(pairs):
            cols = slice(p * 128, (p + 1) * 128)
            dk_ref[rows, cols] = unrotate(dk_acc[rows, cols], cos_ref[rows, :], sin_ref[rows, :]).astype(bf)
            dv_ref[rows, cols] = dv_acc[rows, cols].astype(bf)
        return 0
    lax.fori_loop(0, 2 * blocks, finish, 0)


def swap_pairs(x):
    odd = lax.broadcasted_iota(jnp.int32, x.shape, 1) % 2 == 1
    n = x.shape[1]
    return jnp.where(odd, pltpu.roll(x, 1, 1), pltpu.roll(x, n - 1, 1))

def rotate(x, cosine, sine):
    return x * cosine + swap_pairs(x) * sine

def unrotate(x, cosine, sine):
    return x * cosine - swap_pairs(x) * sine

def attention(lows, starts, cosine, sine, mixed, d_out):
    tokens, width = d_out.shape
    pairs = PAIRS
    wide = 128 * pairs
    groups = width // wide
    blocks = tokens // BQ
    whole = lambda shape: pl.BlockSpec(shape, lambda g, lows: (0,) * len(shape), pipeline_mode=pl.Buffered(1))
    own = pl.BlockSpec((tokens, wide), lambda g, lows: (0, g))
    both = pl.BlockSpec((2 * tokens, wide), lambda g, lows: (0, g))
    q_spec = pl.BlockSpec((tokens, wide), lambda g, lows: (1, g))
    k_spec = pl.BlockSpec((2 * tokens, wide), lambda g, lows: (0, groups + g))
    v_spec = pl.BlockSpec((2 * tokens, wide), lambda g, lows: (0, 2 * groups + g))
    bf, f32 = jnp.bfloat16, jnp.float32
    slots = blocks * (blocks + 1)
    one, two = jax.ShapeDtypeStruct((tokens, width), bf), jax.ShapeDtypeStruct((2 * tokens, width), bf)
    return pl.pallas_call(
        functools.partial(attention_kernel, pairs, tokens),
        out_shape=[one, jax.ShapeDtypeStruct((width, tokens), bf), one, two, two],
        grid_spec=pltpu.PrefetchScalarGridSpec(
            num_scalar_prefetch=1,
            grid=(groups,),
            in_specs=[whole((1, tokens)), whole((2 * tokens, 128)), whole((2 * tokens, 128)), q_spec, k_spec, v_spec, own],
            out_specs=[own, pl.BlockSpec((wide, tokens), lambda g, lows: (g, 0)), own, both, both],
            scratch_shapes=[pltpu.VMEM((slots, BQ, BQ), bf), pltpu.VMEM((blocks + 1, 2 * pairs, BQ, BQ), f32),
                            pltpu.VMEM((blocks + 1, 2 * pairs, BQ, BQ), bf), pltpu.VMEM((pairs, 128, 2 * tokens), bf),
                            pltpu.VMEM((pairs, 128, 2 * tokens), bf), pltpu.VMEM((2 * tokens, wide), f32),
                            pltpu.VMEM((2 * tokens, wide), f32), pltpu.VMEM((pairs, 128, BQ), f32),
                            pltpu.VMEM((pairs, 128, BQ), f32), pltpu.VMEM((2 * pairs, BQ, BQ), bf)],
        ),
        compiler_params=pltpu.CompilerParams(vmem_limit_bytes=62 * 2**20),
        cost_estimate=pl.CostEstimate(flops=60 * 10**9, bytes_accessed=30 * 2**20, transcendentals=0),
        name="attention",
    )(lows, starts[None, :], cosine, sine, mixed, mixed, mixed, d_out)


def layer_norm_stats(values):
    mean = jnp.mean(values, axis=1, keepdims=True)
    centered = values - mean
    spread = jnp.mean(centered * centered, axis=1, keepdims=True)
    scale = lax.rsqrt(spread + EPS)
    return centered * scale, scale


CHUNK = 256
AHEAD = 3


def gather_kernel(dims, w_out, w_qkv, x_hbm, grad, vec_own, lengths, freqs,
                  wout_all, wqkv_all, normed_own, normed_prior, turned_own, turned_prior, grad_turned, mixed_all, d_attended, prior_all, cos_all, sin_all, vec_all,
                  wbuf, own, prior, normed, turned, mixed, d_att, cos_ref, sin_ref, vec, vec_recv, in_sem, load_sem, out_sem, zsend, zrecv, ysend, yrecv,
                  csend, crecv, psend, precv, vsend, vrecv):
    rows, seqs, tokens, width = dims
    bf, f32 = jnp.bfloat16, jnp.float32
    levels = rows // 4
    r, s = lax.axis_index("rows"), lax.axis_index("seq")
    core, y, z = lax.rem(r, 2), lax.rem(r // 2, 2), r // 4
    core_id = {"rows": r + 1 - 2 * core}
    y_id = {"rows": r + 2 - 4 * y}
    z_of = lambda d: lax.rem(z + d, levels)
    z_id = lambda d: {"rows": z_of(d) * 4 + lax.rem(r, 4)}
    has_next, has_prior = s < seqs - 1, s > 0
    n_out, n_qkv = width // CHUNK, 3 * width // CHUNK
    total = n_out + n_qkv
    quarter = tokens // 4

    def load(k):
        source = w_out if k < n_out else w_qkv
        col = (k if k < n_out else k - n_out) * CHUNK
        return pltpu.make_async_copy(source.at[:, col:col + CHUNK], wbuf.at[k, z, y, core], load_sem.at[k])

    fetch = pltpu.make_async_copy(x_hbm, own, in_sem)
    fetch.start()
    for k in range(total):
        load(k).start()

    barrier = pltpu.get_barrier_semaphore()
    partners = [core_id, y_id] + [z_id(d) for d in range(1, levels)]
    for partner in partners:
        pl.semaphore_signal(barrier, inc=1, device_id=partner, device_id_type=MESH)

    @pl.when(has_next)
    def _():
        pl.semaphore_signal(barrier, inc=1, device_id={"seq": s + 1}, device_id_type=MESH)

    @pl.when(has_prior)
    def _():
        pl.semaphore_signal(barrier, inc=1, device_id={"seq": s - 1}, device_id_type=MESH)
    pl.semaphore_wait(barrier, len(partners) + jnp.where(has_next, 1, 0) + jnp.where(has_prior, 1, 0))

    def prior_copy(i):
        block = pl.ds(i * quarter, quarter)
        return pltpu.make_async_remote_copy(x_hbm.at[block], prior.at[block], psend.at[i], precv.at[i],
                                            device_id={"seq": jnp.minimum(s + 1, seqs - 1)}, device_id_type=MESH)

    def vec_copy(i, target):
        return pltpu.make_async_remote_copy(vec.at[i], vec_recv.at[i], vsend.at[i], vrecv.at[i],
                                            device_id=target, device_id_type=MESH)

    def z_vec(d):
        return pltpu.make_async_remote_copy(vec.at[0], vec_recv.at[1 + d], vsend.at[1 + d], vrecv.at[1 + d],
                                            device_id=z_id(d), device_id_type=MESH)

    def z_copy(k, d):
        mine = wbuf.at[k, z, y, core]
        return pltpu.make_async_remote_copy(mine, mine, zsend.at[k, d - 1], zrecv.at[k, d - 1],
                                            device_id=z_id(d), device_id_type=MESH)

    def z_landed(k, d):
        theirs = wbuf.at[k, z_of(levels - d), y, core]
        return pltpu.make_async_remote_copy(theirs, theirs, zsend.at[k, d - 1], zrecv.at[k, d - 1],
                                            device_id=z_id(d), device_id_type=MESH)

    def y_copy(k, side):
        part = wbuf.at[k, :, side, core]
        return pltpu.make_async_remote_copy(part, part, ysend.at[k], yrecv.at[k], device_id=y_id, device_id_type=MESH)

    def core_copy(k, side):
        part = wbuf.at[k, :, :, side]
        return pltpu.make_async_remote_copy(part, part, csend.at[k], crecv.at[k], device_id=core_id, device_id_type=MESH)

    vec[0] = vec_own[...]
    for d in range(1, levels):
        z_vec(d).start()

    @pl.when(has_next)
    def _():
        for i in range(2):
            prior_copy(i).start()

    @pl.when(jnp.logical_not(has_prior))
    def _():
        prior[...] = jnp.zeros_like(prior)

    def z_start(k):
        load(k).wait()
        for d in range(1, levels):
            z_copy(k, d).start()
    for k in range(AHEAD):
        z_start(k)

    swap = pltpu.make_async_remote_copy(vec.at[2], vec_recv.at[0], vsend.at[0], vrecv.at[0], device_id=core_id,
                                        device_id_type=MESH)

    def share_vectors(it):
        if it == 0:
            for d in range(1, levels):
                z_vec(d).wait()
            value = vec[0]
            for d in range(1, levels):
                value = value + vec_recv[1 + d]
            vec[1] = value
            vec_copy(1, y_id).start()
        if it == 1:
            vec_copy(1, y_id).wait()
            vec[2] = vec[1] + vec_recv[1]
            swap.start()
        if it == 2:
            swap.wait()
            vec_all[...] = vec[2] + vec_recv[0]

    def normalize(source, half, i):
        block = slice(i * quarter, (i + 1) * quarter)
        values = source[block, :].astype(f32)
        centered = values - jnp.mean(values, axis=1, keepdims=True)
        unit = centered * lax.rsqrt(jnp.mean(centered * centered, axis=1, keepdims=True) + EPS)
        normed[half, block, :] = (unit * vec_all[0:1, :] + vec_all[1:2, :]).astype(bf)

    def turn(source, place, i):
        block = slice(i * quarter, (i + 1) * quarter)
        turned[place, :, block] = source[block, :].T

    outs = []

    def send_out(src, dst):
        copy = pltpu.make_async_copy(src, dst, out_sem.at[len(outs)])
        copy.start()
        outs.append(copy)

    def multiply(half, j, parts):
        cols = slice(j * CHUNK, (j + 1) * CHUNK)
        tall = tokens // 2
        for i in parts:
            block = slice(i * tall, (i + 1) * tall)
            product = dot_n(normed[half, block, :], wbuf[n_out + j].reshape(width, CHUNK))
            if j * CHUNK < 2 * width:
                scale = 0.125 if j * CHUNK < width else 1.0
                place = slice(half * tokens + i * tall, half * tokens + (i + 1) * tall)
                cosine, sine = cos_ref[place, :] * scale, sin_ref[place, :] * scale
                for a in range(CHUNK // 128):
                    mixed[half, block, j * CHUNK + a * 128:j * CHUNK + (a + 1) * 128] = rotate(
                        product[:, a * 128:(a + 1) * 128], cosine, sine).astype(bf)
            else:
                mixed[half, block, cols] = product.astype(bf)
            send_out(mixed.at[half, block, cols], mixed_all.at[half, block, cols])

    def project_back():
        tall = tokens // 4

        def body(i, _):
            block = pl.ds(pl.multiple_of(i * tall, tall), tall)
            value = dot_t(grad[block, 0:CHUNK], wbuf[0].reshape(width, CHUNK))
            for k in range(1, n_out):
                value = value + dot_t(grad[block, k * CHUNK:(k + 1) * CHUNK], wbuf[k].reshape(width, CHUNK))
            d_att[block, :] = value.astype(bf)
            return 0
        lax.fori_loop(0, 4, body, 0)
        send_out(d_att, d_attended)

    def prior_landed(i):
        @pl.when(has_prior)
        def _():
            prior_copy(i).wait_recv()

    def prior_next(i):
        @pl.when(has_next)
        def _():
            prior_copy(i).wait_send()
            prior_copy(i + 2).start()

    def angles(i):
        block = slice(i * quarter, (i + 1) * quarter)
        index = (s - 1) * tokens + i * quarter + lax.broadcasted_iota(jnp.int32, (quarter, 128), 0)
        begin = jnp.zeros_like(index)
        end = jnp.int32(0)
        for j in range(lengths.shape[1]):
            end = end + lengths[0, j]
            begin = begin + jnp.where(end <= index, lengths[0, j], 0)
        angle = (index - begin).astype(f32) * freqs[0:1, :]
        cos_ref[block, :] = jnp.cos(angle)
        sin_ref[block, :] = jnp.sin(angle) * freqs[1:2, :]

    for it in range(total + 2):
        if it < total:
            for d in range(1, levels):
                z_landed(it, d).wait_recv()
            if it + AHEAD < total:
                z_start(it + AHEAD)
            y_copy(it, y).start()
        if 0 <= it - 1 < total:
            y_copy(it - 1, 1 - y).wait_recv()
            core_copy(it - 1, core).start()
        share_vectors(it)
        if it < 4:
            angles(2 * it)
            angles(2 * it + 1)
        if it == 4:
            send_out(cos_ref, cos_all)
            send_out(sin_ref, sin_all)
        if it == 3:
            fetch.wait()
        if 3 <= it <= 4:
            normalize(own, 1, 2 * it - 6)
            normalize(own, 1, 2 * it - 5)
        if it == 5:
            send_out(normed.at[1], normed_own)
        if 0 <= it - 2 < total:
            k = it - 2
            core_copy(k, 1 - core).wait_recv()
            if k < n_out:
                send_out(wbuf.at[k], wout_all.at[:, :, :, :, k * CHUNK:(k + 1) * CHUNK])
                if k == n_out - 1:
                    project_back()
            else:
                send_out(wbuf.at[k], wqkv_all.at[:, :, :, :, (k - n_out) * CHUNK:(k - n_out + 1) * CHUNK])
                multiply(1, k - n_out, (0, 1))
        if it < 4:
            turn(grad, 2, it)
        if it == 4:
            send_out(turned.at[2], grad_turned)
        if 8 <= it < 12:
            turn(normed.at[1], 1, it - 8)
        if it == 12:
            send_out(turned.at[1], turned_own)
        if it in (4, 8):
            prior_next(it // 4 - 1)
        if it in (5, 9, 13):
            i = it // 4 - 1
            prior_landed(i)
            normalize(prior, 0, i)
            turn(normed.at[0], 0, i)
        if it - 2 - n_out >= n_qkv // 3:
            multiply(0, it - 2 - n_out, (0,))

    prior_landed(3)
    normalize(prior, 0, 3)
    turn(normed.at[0], 0, 3)
    send_out(prior, prior_all)
    send_out(normed.at[0], normed_prior)
    send_out(turned.at[0], turned_prior)
    for j in range(n_qkv // 3, n_qkv):
        multiply(0, j, (1,))

    @pl.when(has_next)
    def _():
        for i in (2, 3):
            prior_copy(i).wait_send()
    for k in range(total):
        for d in range(1, levels):
            z_copy(k, d).wait_send()
        y_copy(k, y).wait_send()
        core_copy(k, core).wait_send()
    for copy in outs:
        copy.wait()


def rope_rows():
    lane = np.arange(128) % HEAD
    freqs = np.where(lane < ROT, 10000.0 ** (-2.0 * (lane // 2) / ROT), 0.0)
    sign = np.where(lane % 2 == 0, -1.0, 1.0)
    return np.concatenate([freqs[None], sign[None], np.zeros((6, 128))]).astype(np.float32)


def gather_all(rows, seqs, w_out, w_qkv, x, grad, vec_own, lengths):
    tokens, width = x.shape
    share, levels = width // rows, rows // 4
    bf, f32 = jnp.bfloat16, jnp.float32
    vmem, hbm = pl.BlockSpec(memory_space=pltpu.VMEM), pl.BlockSpec(memory_space=pl.ANY)
    dma = pltpu.SemaphoreType.DMA
    total = 4 * width // CHUNK
    shape = jax.ShapeDtypeStruct
    token, turned = shape((tokens, width), bf), shape((width, tokens), bf)
    wout_all, wqkv_all, normed, normed_prior, turned_own, turned_prior, grad_turned, mixed, d_att, prior, cosine, sine, vec = pl.pallas_call(
        functools.partial(gather_kernel, (rows, seqs, tokens, width)),
        out_shape=[shape((levels, 2, 2, share, width), bf), shape((levels, 2, 2, share, 3 * width), bf), token, token,
                   turned, turned, turned, shape((2, tokens, 3 * width), bf), token, token,
                   shape((2 * tokens, 128), f32), shape((2 * tokens, 128), f32), shape((8, width), f32)],
        in_specs=[hbm, hbm, hbm, vmem, vmem, pl.BlockSpec(memory_space=pltpu.SMEM), vmem],
        out_specs=[hbm] * 12 + [vmem],
        scratch_shapes=[
            pltpu.VMEM((total, levels, 2, 2, share, CHUNK), bf),
            pltpu.VMEM((tokens, width), bf), pltpu.VMEM((tokens, width), bf), pltpu.VMEM((2, tokens, width), bf), pltpu.VMEM((3, width, tokens), bf),
            pltpu.VMEM((2, tokens, 3 * width), bf), pltpu.VMEM((tokens, width), bf),
            pltpu.VMEM((2 * tokens, 128), f32), pltpu.VMEM((2 * tokens, 128), f32),
            pltpu.VMEM((3, 8, width), f32), pltpu.VMEM((1 + levels, 8, width), f32),
            dma, dma((total,)), dma((5 * total,)), dma((total, levels - 1)), dma((total, levels - 1)),
            dma((total,)), dma((total,)), dma((total,)), dma((total,)), dma((4,)), dma((4,)), dma((1 + levels,)), dma((1 + levels,)),
        ],
        compiler_params=pltpu.CompilerParams(collective_id=0, has_side_effects=True, vmem_limit_bytes=60 * 2**20),
        cost_estimate=pl.CostEstimate(flops=20 * 10**9, bytes_accessed=40 * 2**20, transcendentals=0),
        name="gather",
    )(w_out, w_qkv, x, grad, vec_own, lengths, rope_rows())
    return (wout_all.reshape(width, width), wqkv_all.reshape(width, 3 * width), normed, normed_prior, turned_own, turned_prior,
            grad_turned, mixed.reshape(2 * tokens, 3 * width), d_att, prior, cosine, sine, vec)


RING = 6
SLOTS = 6


def reduce_kernel(dims, g_q, g_k, g_v, g_out, normed, normed_t_hbm, grad, grad_t_hbm, x_hbm, w_in, w_back, b_in, base_out, base_dn,
                  vec_in, gain_in, returned, o_qkv, o_out, o_in, o_back, o_vec, block_hbm, input_hbm,
                  buf, core_recv, chip, x_recv, y_recv, part, z_recv, fin, fin_recv, res, acc_out, hidden, d_pre, win_buf, wback_buf,
                  normed_t, grad_t, x_ref, block_out, d_normed, came, vec, vec_recv, late_sem, done_sem, came_sem, load_sem, acc_sem, w_sem, send_sem, recv_sem, zsend_sem, zrecv_sem, vsend_sem, vrecv_sem):
    rows, seqs, q_rows, edge, tokens, width, ff = dims
    bf, f32 = jnp.bfloat16, jnp.float32
    levels = rows // 4
    region = q_rows - edge
    r, s = lax.axis_index("rows"), lax.axis_index("seq")
    core, y, z = lax.rem(r, 2), lax.rem(r // 2, 2), r // 4
    odd = lax.rem(s, 2)
    core_id = {"rows": r + 1 - 2 * core}
    y_id = {"rows": r + 2 - 4 * y}
    flip = lambda bit: {"seq": s + bit - 2 * bit * lax.rem(s // bit, 2)}
    z_of = lambda d: lax.rem(z + d, levels)
    z_id = lambda d: {"rows": z_of(d) * 4 + lax.rem(r, 4)}
    bits = []
    while 2 ** (len(bits) + 1) < seqs:
        bits.append(2 ** (len(bits) + 1))
    finals = bits + [1]

    barrier = pltpu.get_barrier_semaphore()
    partners = [core_id, y_id] + [z_id(d) for d in range(1, levels)] + [flip(b) for b in finals]
    for partner in partners:
        pl.semaphore_signal(barrier, inc=1, device_id=partner, device_id_type=MESH)
    pl.semaphore_wait(barrier, len(partners))

    piece = q_rows // 4
    n_qkv, n_out, n_in, n_back = 3 * width // 512, width // 512, ff // 512, width // 128
    n_first = n_qkv + n_out
    n_mlp = n_first + n_in
    assert n_first == n_in
    ready = lambda k: (k < n_mlp) & (lax.rem(k, 2) == 0)
    total = n_mlp + n_back
    own_rows = pl.ds(pl.multiple_of(odd * edge, edge), region)
    c_mine = pl.ds(pl.multiple_of(odd * (q_rows - edge), edge), edge)
    c_other = pl.ds(pl.multiple_of((1 - odd) * (q_rows - edge), edge), edge)

    def remote(src, dst, stage, slot, target):
        return pltpu.make_async_remote_copy(src, dst, send_sem.at[stage, slot], recv_sem.at[stage, slot],
                                            device_id=target, device_id_type=MESH)

    def core_copy(k):
        return remote(buf.at[lax.rem(k, RING), :, 1 - core], core_recv.at[lax.rem(k, SLOTS)], 0, lax.rem(k, SLOTS), core_id)

    def x_copy(k):
        t = lax.rem(k, SLOTS)
        return remote(chip.at[t, :, :, c_other], x_recv.at[t], 1, t, flip(1))

    def y_copy(k):
        t = lax.rem(k, SLOTS)
        return remote(chip.at[t, :, 1 - y, own_rows], y_recv.at[t], 2, t, y_id)

    def z_copy(k, d):
        t = lax.rem(k, SLOTS)
        return pltpu.make_async_remote_copy(part.at[t, z_of(d)], z_recv.at[t, d - 1], zsend_sem.at[d - 1, t],
                                            zrecv_sem.at[d - 1, t], device_id=z_id(d), device_id_type=MESH)

    def fin_copy(k, i):
        t = lax.rem(k, SLOTS)
        return remote(fin.at[t, i], fin_recv.at[t, i], 3 + i, t, flip(finals[i]))

    def load_copies(source, col, k):
        slot = lax.rem(k, RING)
        return [pltpu.make_async_copy(source.at[:, :, :, pl.ds(pl.multiple_of(col + 128 * j, 128), 128)],
                                      buf.at[slot, :, :, pl.ds(j * piece, piece)], load_sem.at[j]) for j in range(4)]

    def load(k):
        for i, source in enumerate((g_q, g_k, g_v, g_out)):
            @pl.when(ready(k) & (k // 2 >= i * n_out) & (k // 2 < (i + 1) * n_out))
            def _():
                for copy in load_copies(source, (k // 2 - i * n_out) * 512, k):
                    copy.start()

    def weights(j):
        t = lax.rem(j, 2)
        cols = pl.ds(pl.multiple_of(j * 512, 512), 512)
        return [pltpu.make_async_copy(w_in.at[:, cols], win_buf.at[t], w_sem.at[0, t]),
                pltpu.make_async_copy(w_back.at[cols, :], wback_buf.at[t], w_sem.at[1, t])]

    starts = [pltpu.make_async_copy(base_out, acc_out, acc_sem.at[0]), pltpu.make_async_copy(base_dn, d_normed, acc_sem.at[1])]
    late = [pltpu.make_async_copy(normed_t_hbm, normed_t, late_sem.at[0]), pltpu.make_async_copy(x_hbm, x_ref, late_sem.at[1]),
            pltpu.make_async_copy(grad_t_hbm, grad_t, late_sem.at[2])]
    for copy in weights(0) + starts + late:
        copy.start()
    load(0)

    def mlp_rows(j, i):
        t = lax.rem(j, 2)
        cols = pl.ds(pl.multiple_of(j * 512, 512), 512)
        tall = tokens // 2
        block = slice(i * tall, (i + 1) * tall)
        if i == 0:
            @pl.when(j == 0)
            def _():
                for copy in starts:
                    copy.wait()
            for copy in weights(j):
                copy.wait()

            @pl.when(j + 1 < n_in)
            def _():
                for copy in weights(j + 1):
                    copy.start()
        pre = dot_n(normed[block, :], win_buf[t]) + b_in[:, cols]
        up = dot_t(grad[block, :], wback_buf[t])
        square = pre * pre
        turn = jnp.tanh(pre * (GELU_COEF + (GELU_COEF * 0.044715) * square))
        half = 0.5 + 0.5 * turn
        hid = (pre * half).astype(bf)
        slope = half + (0.5 * pre) * (1.0 - turn * turn) * (GELU_COEF + (3 * 0.044715 * GELU_COEF) * square)
        down = (up * slope).astype(bf)
        hidden[block, cols] = hid
        d_pre[block, :] = down
        acc_out[block, :] += dot_n(hid, wback_buf[t])
        d_normed[block, :] += dot_t(down, win_buf[t])
        sums = jnp.sum(down.astype(f32), axis=0, keepdims=True)
        place = (pl.ds(3 + j // 2, 1), pl.ds(pl.multiple_of(lax.rem(j, 2) * 512, 512), 512))
        vec[place] = sums if i == 0 else vec[place] + sums

    def mlp_grads(j):
        @pl.when(j == 0)
        def _():
            late[0].wait()
        slot = lax.rem(2 * j + 1, RING)
        per = 8
        big = per * width // rows

        def grads_step(i, _):
            value = dot_n(normed_t[pl.ds(pl.multiple_of(i * big, big), big), :], d_pre[...]).astype(bf)
            for m in range(per):
                for a in range(4):
                    buf[slot, i * (per // 2) + m // 2, m % 2, a * piece:(a + 1) * piece, :] = (
                        value[m * piece:(m + 1) * piece, a * 128:(a + 1) * 128])
            return 0
        lax.fori_loop(0, rows // per, grads_step, 0)

    tall_end = tokens // 4

    def returned_copy(i):
        return pltpu.make_async_copy(returned.at[pl.ds(pl.multiple_of(i * tall_end, tall_end), tall_end)], came, came_sem)

    def done_copies(i):
        block = pl.ds(i * tall_end if isinstance(i, int) else pl.multiple_of(i * tall_end, tall_end), tall_end)
        return [pltpu.make_async_copy(block_out.at[block], block_hbm.at[block], done_sem.at[0, i]),
                pltpu.make_async_copy(d_normed.at[block], input_hbm.at[block], done_sem.at[1, i])]

    def finish_tokens(i):
        @pl.when(i == 0)
        def _():
            returned_copy(0).start()
            vec[0:2, :] = vec_in[...]
            vec[2:3, :] = jnp.zeros((1, width), f32)
            vec[7:8, :] = jnp.zeros((1, width), f32)
        returned_copy(i).wait()
        small = tall_end // 4

        def part(n, sums):
            gain, bias, back = sums
            block = pl.ds(pl.multiple_of(i * tall_end + n * small, small), small)
            block_out[block, :] = acc_out[block, :].astype(bf)
            values = x_ref[block, :].astype(f32)
            centered = values - jnp.mean(values, axis=1, keepdims=True)
            scale = lax.rsqrt(jnp.mean(centered * centered, axis=1, keepdims=True) + EPS)
            unit = centered * scale
            d = d_normed[block, :]
            g = grad[block, :].astype(f32)
            d_unit = (d + came[pl.ds(pl.multiple_of(n * small, small), small), :].astype(f32)) * gain_in[...]
            inner = jnp.mean(d_unit * unit, axis=1, keepdims=True)
            d_normed[block, :] = g + (d_unit - jnp.mean(d_unit, axis=1, keepdims=True) - unit * inner) * scale
            return (gain + jnp.sum(d * unit, axis=0, keepdims=True), bias + jnp.sum(d, axis=0, keepdims=True),
                    back + jnp.sum(g, axis=0, keepdims=True))
        sums = lax.fori_loop(0, 4, part, (vec[0:1, :], vec[1:2, :], vec[2:3, :]))
        for row in range(3):
            vec[row:row + 1, :] = sums[row]
        for copy in done_copies(i):
            copy.start()

        @pl.when(i < 3)
        def _():
            returned_copy(i + 1).start()

    def back_grads(j):
        value = dot_n(grad_t[pl.ds(pl.multiple_of(j * 128, 128), 128), :], hidden[...]).astype(bf)
        slot = lax.rem(n_mlp + j, RING)
        parts = q_rows // 128
        for d in range(rows):
            for a in range(parts):
                buf[slot, d // 2, d % 2, a * 128:(a + 1) * 128, :] = value[:, (d * parts + a) * 128:(d * parts + a + 1) * 128]

    def vec_copy(i, target):
        return pltpu.make_async_remote_copy(vec, vec_recv.at[i], vsend_sem.at[i], vrecv_sem.at[i],
                                            device_id=target, device_id_type=MESH)
    vec_stages = [[(0, core_id)], [(1, y_id)], [(2 + d - 1, z_id(d)) for d in range(1, levels)]]
    vec_stages += [[(1 + levels + i, flip(b))] for i, b in enumerate(finals)]

    def store(k):
        def place(out, col):
            for j in range(4):
                out[:, pl.ds(pl.multiple_of(col + 128 * j, 128), 128)] = res[j * piece:(j + 1) * piece, :]

        @pl.when(ready(k) & (k < 2 * n_qkv))
        def _():
            place(o_qkv, (k // 2) * 512)

        @pl.when(ready(k) & (k >= 2 * n_qkv))
        def _():
            place(o_out, (k // 2 - n_qkv) * 512)

        @pl.when((k < n_mlp) & (lax.rem(k, 2) == 1))
        def _():
            place(o_in, (k // 2) * 512)

        @pl.when(k >= n_mlp)
        def _():
            for a in range(q_rows // 128):
                o_back[a * 128:(a + 1) * 128, pl.ds(pl.multiple_of((k - n_mlp) * 128, 128), 128)] = (
                    res[a * 128:(a + 1) * 128, :].T)

    def stage(lag, it, body):
        k = it - lag

        @pl.when((k >= 0) & (k < total))
        def _():
            body(k, lax.rem(k, SLOTS))

    def send_first(k, t):
        @pl.when(ready(k))
        def _():
            for copy in load_copies(g_q, 0, k):
                copy.wait()
        load(k + 1)
        core_copy(k).start()

    def core_add(k, t):
        core_copy(k).wait()
        slot = lax.rem(k, RING)
        for i in range(rows // 2):
            chip[t, i // 2, i % 2] = buf[slot, i, core] + core_recv[t, i]
        x_copy(k).start()

    def x_add(k, t):
        x_copy(k).wait()
        for i in range(rows // 2):
            chip[t, i // 2, i % 2, c_mine] = chip[t, i // 2, i % 2, c_mine] + x_recv[t, i // 2, i % 2]
        y_copy(k).start()

    def y_add(k, t):
        y_copy(k).wait()
        for i in range(levels):
            part[t, i] = chip[t, i, y, own_rows] + y_recv[t, i]
        for d in range(1, levels):
            z_copy(k, d).start()

    def z_add(k, t):
        for d in range(1, levels):
            z_copy(k, d).wait()
        value = part[t, z].astype(f32)
        for d in range(1, levels):
            value = value + z_recv[t, d - 1].astype(f32)
        fin[t, 0] = value.astype(bf)
        fin_copy(k, 0).start()

    def fin_add(i):
        def body(k, t):
            fin_copy(k, i).wait()
            fin[t, i + 1] = fin[t, i] + fin_recv[t, i]
            fin_copy(k, i + 1).start()
        return body

    def last(k, t):
        i = len(finals) - 1
        fin_copy(k, i).wait()
        middle = q_rows - 2 * edge
        at = lambda start, size: pl.ds(pl.multiple_of(start, edge), size)
        res[c_mine, :] = fin[t, i, at(odd * middle, edge)].astype(f32)
        res[c_other, :] = fin_recv[t, i, at((1 - odd) * middle, edge)].astype(f32)
        res[edge:q_rows - edge, :] = (fin[t, i, at((1 - odd) * edge, middle)].astype(f32)
                                      + fin_recv[t, i, at(odd * edge, middle)].astype(f32))
        store(k)

    pipeline = [send_first, core_add, x_add, y_add, z_add] + [fin_add(i) for i in range(len(bits))] + [last]

    def step(it, _):
        for lag, body in enumerate(pipeline):
            stage(2 * lag, it, body)

        @pl.when((it < n_mlp) & (lax.rem(it, 2) == 0))
        def _():
            mlp_rows(it // 2, 1)
            mlp_grads(it // 2)

        @pl.when((it < n_mlp - 1) & (lax.rem(it, 2) == 1))
        def _():
            mlp_rows(it // 2 + 1, 0)

        @pl.when(it == n_mlp - 1)
        def _():
            for copy in late[1:]:
                copy.wait()

        @pl.when((it >= n_mlp - 1) & (it < n_mlp + 3))
        def _():
            finish_tokens(it - (n_mlp - 1))

        @pl.when(it == n_mlp + 2)
        def _():
            for i, target in vec_stages[0]:
                vec_copy(i, target).start()
        for number, stages in enumerate(vec_stages):
            @pl.when(it == n_mlp + 4 + 2 * number)
            def _():
                for i, target in stages:
                    vec_copy(i, target).wait()
                value = vec[...]
                for i, target in stages:
                    value = value + vec_recv[i]
                if number + 1 < len(vec_stages):
                    vec[...] = value
                    for i, target in vec_stages[number + 1]:
                        vec_copy(i, target).start()
                else:
                    o_vec[...] = value

        @pl.when((it >= n_mlp - 1) & (it < total - 1))
        def _():
            back_grads(it - (n_mlp - 1))
        return 0
    mlp_rows(jnp.int32(0), 0)
    lax.fori_loop(0, total + 2 * len(pipeline) - 2, step, 0)
    for i in range(4):
        for copy in done_copies(i):
            copy.wait()


def reduce_all(rows, seqs, g_q, g_k, g_v, g_out, normed, normed_t, grad, grad_t, x, w_in, w_back, b_in, base_out, base_dn, vec_in, gain,
               returned):
    tokens, width = normed.shape
    ff = w_in.shape[1]
    share = width // rows
    q_rows = 4 * share
    edge = q_rows // 4
    levels = rows // 4
    region = q_rows - edge
    finals = max(1, (seqs - 1).bit_length())
    bf, f32 = jnp.bfloat16, jnp.float32
    vmem, hbm = pl.BlockSpec(memory_space=pltpu.VMEM), pl.BlockSpec(memory_space=pl.ANY)
    dma = pltpu.SemaphoreType.DMA
    return pl.pallas_call(
        functools.partial(reduce_kernel, (rows, seqs, q_rows, edge, tokens, width, ff)),
        out_shape=[jax.ShapeDtypeStruct((share, 3 * width), f32), jax.ShapeDtypeStruct((share, width), f32),
                   jax.ShapeDtypeStruct((share, ff), f32), jax.ShapeDtypeStruct((ff // rows, width), f32),
                   jax.ShapeDtypeStruct((8, width), f32), jax.ShapeDtypeStruct((tokens, width), bf),
                   jax.ShapeDtypeStruct((tokens, width), f32)],
        in_specs=[hbm, hbm, hbm, hbm, vmem, hbm, vmem, hbm, hbm, hbm, hbm, vmem, hbm, hbm, vmem, vmem, hbm],
        out_specs=[vmem] * 5 + [hbm] * 2,
        scratch_shapes=[
            pltpu.VMEM((RING, rows // 2, 2, q_rows, 128), bf),
            pltpu.VMEM((SLOTS, rows // 2, q_rows, 128), bf),
            pltpu.VMEM((SLOTS, levels, 2, q_rows, 128), bf),
            pltpu.VMEM((SLOTS, levels, 2, edge, 128), bf),
            pltpu.VMEM((SLOTS, levels, region, 128), bf),
            pltpu.VMEM((SLOTS, levels, region, 128), bf),
            pltpu.VMEM((SLOTS, levels - 1, region, 128), bf),
            pltpu.VMEM((SLOTS, finals, region, 128), bf),
            pltpu.VMEM((SLOTS, finals, region, 128), bf),
            pltpu.VMEM((q_rows, 128), f32),
            pltpu.VMEM((tokens, width), f32),
            pltpu.VMEM((tokens, ff), bf),
            pltpu.VMEM((tokens, 512), bf),
            pltpu.VMEM((2, width, 512), bf),
            pltpu.VMEM((2, 512, width), bf),
            pltpu.VMEM((width, tokens), bf),
            pltpu.VMEM((width, tokens), bf),
            pltpu.VMEM((tokens, width), bf),
            pltpu.VMEM((tokens, width), bf),
            pltpu.VMEM((tokens, width), f32),
            pltpu.VMEM((tokens // 4, width), bf),
            pltpu.VMEM((8, width), f32),
            pltpu.VMEM((1 + levels + finals, 8, width), f32),
            dma((3,)), dma((2, 4)), dma,
            dma((4,)), dma((2,)), dma((2, 2)), dma((3 + finals, SLOTS)), dma((3 + finals, SLOTS)),
            dma((levels - 1, SLOTS)), dma((levels - 1, SLOTS)), dma((1 + levels + finals,)), dma((1 + levels + finals,)),
        ],
        compiler_params=pltpu.CompilerParams(collective_id=1, has_side_effects=True, vmem_limit_bytes=62 * 2**20),
        cost_estimate=pl.CostEstimate(flops=100 * 10**9, bytes_accessed=100 * 2**20, transcendentals=0),
        name="reduce",
    )(*[g.reshape(rows // 2, 2, share, width) for g in (g_q, g_k, g_v, g_out)], normed, normed_t, grad, grad_t, x,
      w_in, w_back, b_in, base_out, base_dn, vec_in, gain, returned)


def body(block_input, lengths, norm_gain, norm_bias, w_qkv, w_attn_out, w_fc_in, b_fc_in, w_fc_out, b_fc_out, cotangent):
    f32, bf = jnp.float32, jnp.bfloat16
    rows, seqs = lax.axis_size("rows"), lax.axis_size("seq")
    inputs = block_input[0].astype(f32)
    tokens, width = inputs.shape
    own_lengths = lengths[0]
    count = own_lengths.shape[0]
    first = lax.axis_index("seq") * tokens
    index = first + jnp.arange(tokens, dtype=jnp.int32)
    order = np.arange(count)
    ends = jnp.sum(jnp.where(order[None, :] <= order[:, None], own_lengths[None, :], 0), axis=1)
    begin = jnp.sum(jnp.where(ends[None, :] <= index[:, None], own_lengths[None, :], 0), axis=1)
    starts = begin - first + tokens
    lows = starts[::BQ] // BQ

    share, wide = width // rows, 4 * width // rows
    r = lax.axis_index("rows")
    place = lambda vector, lines: jnp.where(np.arange(lines * width).reshape(rows, -1) // (lines * share) == r,
                                            vector.astype(f32)[None, :], 0.0).reshape(lines, width)
    vec_own = jnp.concatenate([place(norm_gain, 1), place(norm_bias, 1), place(b_fc_out, 1), place(b_fc_in, 4),
                               jnp.zeros((1, width), f32)])
    grad_out = cotangent[0]
    (w_out_all, w_qkv_all, normed, normed_prior, turned_own, turned_prior, grad_turned, mixed, d_attended, prior_input,
     cosine, sine, vectors) = gather_all(
        rows, seqs, w_attn_out, w_qkv, block_input[0], grad_out, vec_own, lengths)
    w_fc_in, w_fc_out, vectors = lax.optimization_barrier((w_fc_in, w_fc_out, vectors))
    w_in_all = lax.all_gather(w_fc_in, "rows", axis=0, tiled=True)
    w_back_all = lax.all_gather(w_fc_out, "rows", axis=0, tiled=True)
    gain, bias, b_back_all = vectors[0], vectors[1], vectors[2]
    b_in_all = vectors[3:7].reshape(1, 4 * width)
    prior_unit, _ = layer_norm_stats(prior_input.astype(f32))
    attended, attended_turned, d_q, d_k, d_v = attention(lows, starts, cosine, sine, mixed, d_attended)

    d_normed_both = jnp.dot(d_k, w_qkv_all[:, width:2 * width].T, preferred_element_type=f32) + jnp.dot(
        d_v, w_qkv_all[:, 2 * width:].T, preferred_element_type=f32)
    d_prior = d_normed_both[:tokens]
    back = lax.ppermute(d_prior.astype(bf), "seq", [(i + 1, i) for i in range(seqs - 1)])
    vec_in = jnp.stack([jnp.sum(d_prior * prior_unit, axis=0), jnp.sum(d_prior, axis=0)])
    product = lambda turned, values: jnp.dot(turned, values, preferred_element_type=f32)
    grads = [product(turned_own, d_q).astype(bf),
             (product(turned_own, d_k[tokens:]) + product(turned_prior, d_k[:tokens])).astype(bf),
             (product(turned_own, d_v[tokens:]) + product(turned_prior, d_v[:tokens])).astype(bf)]
    grad_w_out = product(attended_turned, grad_out).astype(bf)
    base_dn = d_normed_both[tokens:] + jnp.dot(d_q, w_qkv_all[:, :width].T, preferred_element_type=f32)
    base_out = inputs + jnp.dot(attended, w_out_all, preferred_element_type=f32) + b_back_all

    g_qkv, g_out, g_in, g_back, vec, block_output, grad_input = reduce_all(
        rows, seqs, *grads, grad_w_out, normed, turned_own, grad_out, grad_turned, block_input[0], w_in_all, w_back_all,
        b_in_all, base_out, base_dn, vec_in, gain[None], back)

    own = lambda vector, size: lax.dynamic_slice_in_dim(vector, r * size, size)
    return (block_output[None], grad_input[None], own(vec[0], share), own(vec[1], share), g_qkv, g_out, g_in,
            own(vec[3:7].reshape(4 * width), wide), g_back, own(vec[2], share))


def solution(mesh):
    vector, matrix, tokens = P("rows"), P("rows", None), P("rows", "seq", None)
    in_specs = (tokens, matrix, vector, vector, matrix, matrix, matrix, vector, matrix, vector, tokens)
    out_specs = (tokens, tokens, vector, vector, matrix, matrix, matrix, vector, matrix, vector)
    return jax.shard_map(body, mesh=mesh, in_specs=in_specs, out_specs=out_specs, check_vma=False)
```

```python
import functools

import jax
import jax.numpy as jnp
import numpy as np
from jax import lax
from jax.experimental import pallas as pl
from jax.experimental.pallas import tpu as pltpu
from jax.sharding import PartitionSpec as P

HEADS = 16
HEAD = 64
ROT = 32
EPS = 1e-05
GELU_COEF = 0.7978845608028654
MESH = pl.DeviceIdType.MESH

NEG = -1e30
BQ = 256
PAIRS = 4

def dot_t(a, b):
    return lax.dot_general(a, b, (((1,), (1,)), ((), ())), preferred_element_type=jnp.float32)

def dot_n(a, b):
    return lax.dot_general(a, b, (((1,), (0,)), ((), ())), preferred_element_type=jnp.float32)

def dot_c(a, b):
    return lax.dot_general(a, b, (((0,), (0,)), ((), ())), preferred_element_type=jnp.float32)

def attention_kernel(pairs, tokens, lows, start_row, cos_ref, sin_ref, q_ref, k_ref, v_ref, do_ref,
                     out_ref, turned_ref, dq_ref, dk_ref, dv_ref, bias, scores, weights, k_turned, v_turned, dk_acc, dv_acc, out_acc, dq_acc, slope):
    bf, f32 = jnp.bfloat16, jnp.float32
    blocks = tokens // BQ
    span = blocks + 1
    heads = 2 * pairs
    even = lax.broadcasted_iota(jnp.int32, (BQ, 128), 1) < HEAD
    fold = lambda x, op: op(x.reshape(BQ // 8, 8, BQ), axis=0)

    @pl.when(pl.program_id(0) == 0)
    def _():
        for qb in range(blocks):
            start = start_row[:, qb * BQ:(qb + 1) * BQ]
            query = tokens + qb * BQ + lax.broadcasted_iota(jnp.int32, (BQ, BQ), 1)

            def fill(kb, _):
                key = kb * BQ + lax.broadcasted_iota(jnp.int32, (BQ, BQ), 0)
                bias[qb * span + kb - qb] = jnp.where((key >= start) & (key <= query), 0.0, NEG).astype(bf)
                return 0
            lax.fori_loop(lows[qb], blocks + qb + 1, fill, 0)

    def prepare(kb, _):
        rows = pl.ds(pl.multiple_of(kb * BQ, BQ), BQ)
        for p in range(pairs):
            cols = slice(p * 128, (p + 1) * 128)
            k_turned[p, :, rows] = k_ref[rows, cols].T
            v_turned[p, :, rows] = v_ref[rows, cols].T
        return 0
    lax.fori_loop(lows[0], 2 * blocks, prepare, 0)
    dk_acc[...] = jnp.zeros_like(dk_acc)
    dv_acc[...] = jnp.zeros_like(dv_acc)

    def one_q(qb, _):
        q_rows = pl.ds(pl.multiple_of(qb * BQ, BQ), BQ)
        own_rows = pl.ds(pl.multiple_of(tokens + qb * BQ, BQ), BQ)
        low, high = lows[qb], blocks + qb + 1
        q_h = []
        for p in range(pairs):
            q = q_ref[q_rows, p * 128:(p + 1) * 128]
            q_h += [jnp.where(even, q, 0), jnp.where(even, 0, q)]

        def score(kb, tops):
            rows = pl.ds(pl.multiple_of(kb * BQ, BQ), BQ)
            b = bias[qb * span + kb - qb].astype(f32)
            new = []
            for h in range(heads):
                s = dot_t(k_ref[rows, (h // 2) * 128:(h // 2 + 1) * 128], q_h[h]) + b
                scores[kb - qb, h] = s
                new.append(jnp.maximum(tops[h], fold(s, jnp.max)))
            return tuple(new)
        tops = lax.fori_loop(low, high, score, tuple(jnp.full((8, BQ), NEG, f32) for _ in range(heads)))
        tops = [jnp.max(t, axis=0, keepdims=True) for t in tops]
        out_acc[...] = jnp.zeros_like(out_acc)
        dq_acc[...] = jnp.zeros_like(dq_acc)

        def attend(kb, sums):
            rows = pl.ds(pl.multiple_of(kb * BQ, BQ), BQ)
            new = []
            for h in range(heads):
                e = jnp.exp(scores[kb - qb, h] - tops[h])
                new.append(sums[h] + fold(e, jnp.sum))
                e = e.astype(bf)
                weights[kb - qb, h] = e
            for h in range(heads):
                half = slice((h % 2) * HEAD, (h % 2 + 1) * HEAD)
                out_acc[h // 2, half, :] += dot_n(v_turned[h // 2, half, rows], weights[kb - qb, h])
            return tuple(new)
        sums = lax.fori_loop(low, high, attend, tuple(jnp.zeros((8, BQ), f32) for _ in range(heads)))

        do_h, deltas = [], []
        for p in range(pairs):
            cols = slice(p * 128, (p + 1) * 128)
            inverse = [1.0 / jnp.sum(sums[h], axis=0, keepdims=True) for h in (2 * p, 2 * p + 1)]
            inverse = jnp.concatenate([jnp.broadcast_to(v, (HEAD, BQ)) for v in inverse], axis=0)
            out = out_acc[p] * inverse
            out_ref[q_rows, cols] = out.T.astype(bf)
            turned_ref[cols, q_rows] = out.astype(bf)
            d_out = do_ref[q_rows, cols].astype(f32).T * inverse
            product = out * d_out
            deltas += [jnp.sum(product[:HEAD], axis=0, keepdims=True), jnp.sum(product[HEAD:], axis=0, keepdims=True)]
            d_out = d_out.T.astype(bf)
            do_h += [jnp.where(even, d_out, 0), jnp.where(even, 0, d_out)]

        def back(kb, _):
            rows = pl.ds(pl.multiple_of(kb * BQ, BQ), BQ)
            for p in range(pairs):
                v = v_ref[rows, p * 128:(p + 1) * 128]
                for h in (2 * p, 2 * p + 1):
                    d_prob = dot_t(v, do_h[h])
                    slope[h] = (weights[kb - qb, h].astype(f32) * (d_prob - deltas[h])).astype(bf)
            for p in range(pairs):
                cols = slice(p * 128, (p + 1) * 128)
                dv_acc[rows, cols] += dot_n(weights[kb - qb, 2 * p], do_h[2 * p]) + dot_n(weights[kb - qb, 2 * p + 1], do_h[2 * p + 1])
                dk_acc[rows, cols] += dot_n(slope[2 * p], q_h[2 * p]) + dot_n(slope[2 * p + 1], q_h[2 * p + 1])
            for h in range(heads):
                half = slice((h % 2) * HEAD, (h % 2 + 1) * HEAD)
                dq_acc[h // 2, half, :] += dot_n(k_turned[h // 2, half, rows], slope[h])
            return 0
        lax.fori_loop(low, high, back, 0)
        for p in range(pairs):
            dq_ref[q_rows, p * 128:(p + 1) * 128] = unrotate(
                dq_acc[p].T * 0.125, cos_ref[own_rows, :], sin_ref[own_rows, :]).astype(bf)
        return 0
    lax.fori_loop(0, blocks, one_q, 0)

    def finish(kb, _):
        rows = pl.ds(pl.multiple_of(kb * BQ, BQ), BQ)
        for p in range(pairs):
            cols = slice(p * 128, (p + 1) * 128)
            dk_ref[rows, cols] = unrotate(dk_acc[rows, cols], cos_ref[rows, :], sin_ref[rows, :]).astype(bf)
            dv_ref[rows, cols] = dv_acc[rows, cols].astype(bf)
        return 0
    lax.fori_loop(0, 2 * blocks, finish, 0)


def swap_pairs(x):
    odd = lax.broadcasted_iota(jnp.int32, x.shape, 1) % 2 == 1
    n = x.shape[1]
    return jnp.where(odd, pltpu.roll(x, 1, 1), pltpu.roll(x, n - 1, 1))

def rotate(x, cosine, sine):
    return x * cosine + swap_pairs(x) * sine

def unrotate(x, cosine, sine):
    return x * cosine - swap_pairs(x) * sine

def attention(lows, starts, cosine, sine, mixed, d_out):
    tokens, width = d_out.shape
    pairs = PAIRS
    wide = 128 * pairs
    groups = width // wide
    blocks = tokens // BQ
    whole = lambda shape: pl.BlockSpec(shape, lambda g, lows: (0,) * len(shape), pipeline_mode=pl.Buffered(1))
    own = pl.BlockSpec((tokens, wide), lambda g, lows: (0, g))
    both = pl.BlockSpec((2 * tokens, wide), lambda g, lows: (0, g))
    q_spec = pl.BlockSpec((tokens, wide), lambda g, lows: (1, g))
    k_spec = pl.BlockSpec((2 * tokens, wide), lambda g, lows: (0, groups + g))
    v_spec = pl.BlockSpec((2 * tokens, wide), lambda g, lows: (0, 2 * groups + g))
    bf, f32 = jnp.bfloat16, jnp.float32
    slots = blocks * (blocks + 1)
    one, two = jax.ShapeDtypeStruct((tokens, width), bf), jax.ShapeDtypeStruct((2 * tokens, width), bf)
    return pl.pallas_call(
        functools.partial(attention_kernel, pairs, tokens),
        out_shape=[one, jax.ShapeDtypeStruct((width, tokens), bf), one, two, two],
        grid_spec=pltpu.PrefetchScalarGridSpec(
            num_scalar_prefetch=1,
            grid=(groups,),
            in_specs=[whole((1, tokens)), whole((2 * tokens, 128)), whole((2 * tokens, 128)), q_spec, k_spec, v_spec, own],
            out_specs=[own, pl.BlockSpec((wide, tokens), lambda g, lows: (g, 0)), own, both, both],
            scratch_shapes=[pltpu.VMEM((slots, BQ, BQ), bf), pltpu.VMEM((blocks + 1, 2 * pairs, BQ, BQ), f32),
                            pltpu.VMEM((blocks + 1, 2 * pairs, BQ, BQ), bf), pltpu.VMEM((pairs, 128, 2 * tokens), bf),
                            pltpu.VMEM((pairs, 128, 2 * tokens), bf), pltpu.VMEM((2 * tokens, wide), f32),
                            pltpu.VMEM((2 * tokens, wide), f32), pltpu.VMEM((pairs, 128, BQ), f32),
                            pltpu.VMEM((pairs, 128, BQ), f32), pltpu.VMEM((2 * pairs, BQ, BQ), bf)],
        ),
        compiler_params=pltpu.CompilerParams(vmem_limit_bytes=62 * 2**20),
        cost_estimate=pl.CostEstimate(flops=60 * 10**9, bytes_accessed=30 * 2**20, transcendentals=0),
        name="attention",
    )(lows, starts[None, :], cosine, sine, mixed, mixed, mixed, d_out)


def layer_norm_stats(values):
    mean = jnp.mean(values, axis=1, keepdims=True)
    centered = values - mean
    spread = jnp.mean(centered * centered, axis=1, keepdims=True)
    scale = lax.rsqrt(spread + EPS)
    return centered * scale, scale


CHUNK = 256
AHEAD = 3


def gather_kernel(dims, w_out, w_qkv, x_hbm, grad, gain_own, bias_own, b_out_own, b_in_own, lengths, freqs,
                  wout_all, wqkv_all, normed_own, normed_prior, turned_own, turned_prior, grad_turned, mixed_all, d_attended, prior_all, cos_all, sin_all, vec_all,
                  wbuf, own, prior, normed, turned, mixed, d_att, cos_ref, sin_ref, vec, vec_recv, in_sem, load_sem, out_sem, zsend, zrecv, ysend, yrecv,
                  csend, crecv, psend, precv, vsend, vrecv):
    rows, seqs, tokens, width = dims
    bf, f32 = jnp.bfloat16, jnp.float32
    levels = rows // 4
    r, s = lax.axis_index("rows"), lax.axis_index("seq")
    core, y, z = lax.rem(r, 2), lax.rem(r // 2, 2), r // 4
    core_id = {"rows": r + 1 - 2 * core}
    y_id = {"rows": r + 2 - 4 * y}
    z_of = lambda d: lax.rem(z + d, levels)
    z_id = lambda d: {"rows": z_of(d) * 4 + lax.rem(r, 4)}
    has_next, has_prior = s < seqs - 1, s > 0
    n_out, n_qkv = width // CHUNK, 3 * width // CHUNK
    total = n_out + n_qkv
    quarter = tokens // 4

    def load(k):
        source = w_out if k < n_out else w_qkv
        col = (k if k < n_out else k - n_out) * CHUNK
        return pltpu.make_async_copy(source.at[:, col:col + CHUNK], wbuf.at[k, z, y, core], load_sem.at[k])

    fetch = pltpu.make_async_copy(x_hbm, own, in_sem)
    fetch.start()
    for k in range(total):
        load(k).start()

    barrier = pltpu.get_barrier_semaphore()
    partners = [core_id, y_id] + [z_id(d) for d in range(1, levels)]
    for partner in partners:
        pl.semaphore_signal(barrier, inc=1, device_id=partner, device_id_type=MESH)

    @pl.when(has_next)
    def _():
        pl.semaphore_signal(barrier, inc=1, device_id={"seq": s + 1}, device_id_type=MESH)

    @pl.when(has_prior)
    def _():
        pl.semaphore_signal(barrier, inc=1, device_id={"seq": s - 1}, device_id_type=MESH)
    pl.semaphore_wait(barrier, len(partners) + jnp.where(has_next, 1, 0) + jnp.where(has_prior, 1, 0))

    def prior_copy(i):
        block = pl.ds(i * quarter, quarter)
        return pltpu.make_async_remote_copy(x_hbm.at[block], prior.at[block], psend.at[i], precv.at[i],
                                            device_id={"seq": jnp.minimum(s + 1, seqs - 1)}, device_id_type=MESH)

    def vec_copy(i, target):
        return pltpu.make_async_remote_copy(vec.at[i], vec_recv.at[i], vsend.at[i], vrecv.at[i],
                                            device_id=target, device_id_type=MESH)

    def z_vec(d):
        return pltpu.make_async_remote_copy(vec.at[0], vec_recv.at[1 + d], vsend.at[1 + d], vrecv.at[1 + d],
                                            device_id=z_id(d), device_id_type=MESH)

    def z_copy(k, d):
        mine = wbuf.at[k, z, y, core]
        return pltpu.make_async_remote_copy(mine, mine, zsend.at[k, d - 1], zrecv.at[k, d - 1],
                                            device_id=z_id(d), device_id_type=MESH)

    def z_landed(k, d):
        theirs = wbuf.at[k, z_of(levels - d), y, core]
        return pltpu.make_async_remote_copy(theirs, theirs, zsend.at[k, d - 1], zrecv.at[k, d - 1],
                                            device_id=z_id(d), device_id_type=MESH)

    def y_copy(k, side):
        part = wbuf.at[k, :, side, core]
        return pltpu.make_async_remote_copy(part, part, ysend.at[k], yrecv.at[k], device_id=y_id, device_id_type=MESH)

    def core_copy(k, side):
        part = wbuf.at[k, :, :, side]
        return pltpu.make_async_remote_copy(part, part, csend.at[k], crecv.at[k], device_id=core_id, device_id_type=MESH)

    vec[0] = jnp.zeros((8, width), f32)
    for line, own_ref in ((0, gain_own), (1, bias_own), (2, b_out_own), (3, b_in_own)):
        size = own_ref.shape[1]
        lane = lax.broadcasted_iota(jnp.int32, (size, width), 1)
        hot = jnp.where(lax.rem(lane, size) == lax.broadcasted_iota(jnp.int32, (size, width), 0), 1.0, 0.0).astype(bf)
        value = dot_n(jnp.broadcast_to(own_ref[...], (16, size)), hot)[0:1, :]
        inside = lane[0:1, :] // size == lax.rem(r, width // size)
        vec[0, pl.ds(line + r * size // width, 1), :] = jnp.where(inside, value, 0.0)
    for d in range(1, levels):
        z_vec(d).start()

    @pl.when(has_next)
    def _():
        for i in range(2):
            prior_copy(i).start()

    @pl.when(jnp.logical_not(has_prior))
    def _():
        prior[...] = jnp.zeros_like(prior)

    def z_start(k):
        load(k).wait()
        for d in range(1, levels):
            z_copy(k, d).start()
    for k in range(AHEAD):
        z_start(k)

    swap = pltpu.make_async_remote_copy(vec.at[2], vec_recv.at[0], vsend.at[0], vrecv.at[0], device_id=core_id,
                                        device_id_type=MESH)

    def share_vectors(it):
        if it == 0:
            for d in range(1, levels):
                z_vec(d).wait()
            value = vec[0]
            for d in range(1, levels):
                value = value + vec_recv[1 + d]
            vec[1] = value
            vec_copy(1, y_id).start()
        if it == 1:
            vec_copy(1, y_id).wait()
            vec[2] = vec[1] + vec_recv[1]
            swap.start()
        if it == 2:
            swap.wait()
            vec_all[...] = vec[2] + vec_recv[0]

    def normalize(source, half, i):
        block = slice(i * quarter, (i + 1) * quarter)
        values = source[block, :].astype(f32)
        centered = values - jnp.mean(values, axis=1, keepdims=True)
        unit = centered * lax.rsqrt(jnp.mean(centered * centered, axis=1, keepdims=True) + EPS)
        normed[half, block, :] = (unit * vec_all[0:1, :] + vec_all[1:2, :]).astype(bf)

    def turn(source, place, i):
        block = slice(i * quarter, (i + 1) * quarter)
        turned[place, :, block] = source[block, :].T

    outs = []

    def send_out(src, dst):
        copy = pltpu.make_async_copy(src, dst, out_sem.at[len(outs)])
        copy.start()
        outs.append(copy)

    def multiply(half, j, parts):
        cols = slice(j * CHUNK, (j + 1) * CHUNK)
        tall = tokens // 2
        for i in parts:
            block = slice(i * tall, (i + 1) * tall)
            product = dot_n(normed[half, block, :], wbuf[n_out + j].reshape(width, CHUNK))
            if j * CHUNK < 2 * width:
                scale = 0.125 if j * CHUNK < width else 1.0
                place = slice(half * tokens + i * tall, half * tokens + (i + 1) * tall)
                cosine, sine = cos_ref[place, :] * scale, sin_ref[place, :] * scale
                for a in range(CHUNK // 128):
                    mixed[half, block, j * CHUNK + a * 128:j * CHUNK + (a + 1) * 128] = rotate(
                        product[:, a * 128:(a + 1) * 128], cosine, sine).astype(bf)
            else:
                mixed[half, block, cols] = product.astype(bf)
            send_out(mixed.at[half, block, cols], mixed_all.at[half, block, cols])

    def project_back():
        tall = tokens // 4

        def body(i, _):
            block = pl.ds(pl.multiple_of(i * tall, tall), tall)
            value = dot_t(grad[block, 0:CHUNK], wbuf[0].reshape(width, CHUNK))
            for k in range(1, n_out):
                value = value + dot_t(grad[block, k * CHUNK:(k + 1) * CHUNK], wbuf[k].reshape(width, CHUNK))
            d_att[block, :] = value.astype(bf)
            return 0
        lax.fori_loop(0, 4, body, 0)
        send_out(d_att, d_attended)

    def prior_landed(i):
        @pl.when(has_prior)
        def _():
            prior_copy(i).wait_recv()

    def prior_next(i):
        @pl.when(has_next)
        def _():
            prior_copy(i).wait_send()
            prior_copy(i + 2).start()

    def angles(i):
        block = slice(i * quarter, (i + 1) * quarter)
        index = (s - 1) * tokens + i * quarter + lax.broadcasted_iota(jnp.int32, (quarter, 128), 0)
        begin = jnp.zeros_like(index)
        end = jnp.int32(0)
        for j in range(lengths.shape[1]):
            end = end + lengths[0, j]
            begin = begin + jnp.where(end <= index, lengths[0, j], 0)
        angle = (index - begin).astype(f32) * freqs[0:1, :]
        cos_ref[block, :] = jnp.cos(angle)
        sin_ref[block, :] = jnp.sin(angle) * freqs[1:2, :]

    for it in range(total + 2):
        if it < total:
            for d in range(1, levels):
                z_landed(it, d).wait_recv()
            if it + AHEAD < total:
                z_start(it + AHEAD)
            y_copy(it, y).start()
        if 0 <= it - 1 < total:
            y_copy(it - 1, 1 - y).wait_recv()
            core_copy(it - 1, core).start()
        share_vectors(it)
        if it < 4:
            angles(2 * it)
            angles(2 * it + 1)
        if it == 4:
            send_out(cos_ref, cos_all)
            send_out(sin_ref, sin_all)
        if it == 3:
            fetch.wait()
        if 3 <= it <= 4:
            normalize(own, 1, 2 * it - 6)
            normalize(own, 1, 2 * it - 5)
        if it == 5:
            send_out(normed.at[1], normed_own)
        if 0 <= it - 2 < total:
            k = it - 2
            core_copy(k, 1 - core).wait_recv()
            if k < n_out:
                send_out(wbuf.at[k], wout_all.at[:, :, :, :, k * CHUNK:(k + 1) * CHUNK])
                if k == n_out - 1:
                    project_back()
            else:
                send_out(wbuf.at[k], wqkv_all.at[:, :, :, :, (k - n_out) * CHUNK:(k - n_out + 1) * CHUNK])
                multiply(1, k - n_out, (0, 1))
        if it < 4:
            turn(grad, 2, it)
        if it == 4:
            send_out(turned.at[2], grad_turned)
        if 8 <= it < 12:
            turn(normed.at[1], 1, it - 8)
        if it == 12:
            send_out(turned.at[1], turned_own)
        if it in (4, 8):
            prior_next(it // 4 - 1)
        if it in (5, 9, 13):
            i = it // 4 - 1
            prior_landed(i)
            normalize(prior, 0, i)
            turn(normed.at[0], 0, i)
        if it - 2 - n_out >= n_qkv // 3:
            multiply(0, it - 2 - n_out, (0,))

    prior_landed(3)
    normalize(prior, 0, 3)
    turn(normed.at[0], 0, 3)
    send_out(prior, prior_all)
    send_out(normed.at[0], normed_prior)
    send_out(turned.at[0], turned_prior)
    for j in range(n_qkv // 3, n_qkv):
        multiply(0, j, (1,))

    @pl.when(has_next)
    def _():
        for i in (2, 3):
            prior_copy(i).wait_send()
    for k in range(total):
        for d in range(1, levels):
            z_copy(k, d).wait_send()
        y_copy(k, y).wait_send()
        core_copy(k, core).wait_send()
    for copy in outs:
        copy.wait()


def rope_rows():
    lane = np.arange(128) % HEAD
    freqs = np.where(lane < ROT, 10000.0 ** (-2.0 * (lane // 2) / ROT), 0.0)
    sign = np.where(lane % 2 == 0, -1.0, 1.0)
    return np.concatenate([freqs[None], sign[None], np.zeros((6, 128))]).astype(np.float32)


def gather_all(rows, seqs, w_out, w_qkv, x, grad, vectors, lengths):
    tokens, width = x.shape
    share, levels = width // rows, rows // 4
    bf, f32 = jnp.bfloat16, jnp.float32
    vmem, hbm = pl.BlockSpec(memory_space=pltpu.VMEM), pl.BlockSpec(memory_space=pl.ANY)
    dma = pltpu.SemaphoreType.DMA
    total = 4 * width // CHUNK
    shape = jax.ShapeDtypeStruct
    token, turned = shape((tokens, width), bf), shape((width, tokens), bf)
    wout_all, wqkv_all, normed, normed_prior, turned_own, turned_prior, grad_turned, mixed, d_att, prior, cosine, sine, vec = pl.pallas_call(
        functools.partial(gather_kernel, (rows, seqs, tokens, width)),
        out_shape=[shape((levels, 2, 2, share, width), bf), shape((levels, 2, 2, share, 3 * width), bf), token, token,
                   turned, turned, turned, shape((2, tokens, 3 * width), bf), token, token,
                   shape((2 * tokens, 128), f32), shape((2 * tokens, 128), f32), shape((8, width), f32)],
        in_specs=[hbm, hbm, hbm, vmem, vmem, vmem, vmem, vmem, pl.BlockSpec(memory_space=pltpu.SMEM), vmem],
        out_specs=[hbm] * 12 + [vmem],
        scratch_shapes=[
            pltpu.VMEM((total, levels, 2, 2, share, CHUNK), bf),
            pltpu.VMEM((tokens, width), bf), pltpu.VMEM((tokens, width), bf), pltpu.VMEM((2, tokens, width), bf), pltpu.VMEM((3, width, tokens), bf),
            pltpu.VMEM((2, tokens, 3 * width), bf), pltpu.VMEM((tokens, width), bf),
            pltpu.VMEM((2 * tokens, 128), f32), pltpu.VMEM((2 * tokens, 128), f32),
            pltpu.VMEM((3, 8, width), f32), pltpu.VMEM((1 + levels, 8, width), f32),
            dma, dma((total,)), dma((5 * total,)), dma((total, levels - 1)), dma((total, levels - 1)),
            dma((total,)), dma((total,)), dma((total,)), dma((total,)), dma((4,)), dma((4,)), dma((1 + levels,)), dma((1 + levels,)),
        ],
        compiler_params=pltpu.CompilerParams(collective_id=0, has_side_effects=True, vmem_limit_bytes=60 * 2**20),
        cost_estimate=pl.CostEstimate(flops=20 * 10**9, bytes_accessed=40 * 2**20, transcendentals=0),
        name="gather",
    )(w_out, w_qkv, x, grad, *[v[None] for v in vectors], lengths, rope_rows())
    return (wout_all.reshape(width, width), wqkv_all.reshape(width, 3 * width), normed, normed_prior, turned_own, turned_prior,
            grad_turned, mixed.reshape(2 * tokens, 3 * width), d_att, prior, cosine, sine, vec)


RING = 6
SLOTS = 6


def reduce_kernel(dims, g_q, g_k, g_v, g_out, normed, normed_t_hbm, grad, grad_t_hbm, x_hbm, w_in, w_back, b_in, base_out, base_dn,
                  vec_in, gain_in, returned, o_qkv, o_out, o_in, o_back, o_vec, block_hbm, input_hbm,
                  buf, core_recv, chip, x_recv, y_recv, part, z_recv, fin, fin_recv, res, acc_out, hidden, d_pre, win_buf, wback_buf,
                  normed_t, grad_t, x_ref, block_out, d_normed, came, vec, vec_recv, late_sem, done_sem, came_sem, load_sem, acc_sem, w_sem, send_sem, recv_sem, zsend_sem, zrecv_sem, vsend_sem, vrecv_sem):
    rows, seqs, q_rows, edge, tokens, width, ff = dims
    bf, f32 = jnp.bfloat16, jnp.float32
    levels = rows // 4
    region = q_rows - edge
    r, s = lax.axis_index("rows"), lax.axis_index("seq")
    core, y, z = lax.rem(r, 2), lax.rem(r // 2, 2), r // 4
    odd = lax.rem(s, 2)
    core_id = {"rows": r + 1 - 2 * core}
    y_id = {"rows": r + 2 - 4 * y}
    flip = lambda bit: {"seq": s + bit - 2 * bit * lax.rem(s // bit, 2)}
    z_of = lambda d: lax.rem(z + d, levels)
    z_id = lambda d: {"rows": z_of(d) * 4 + lax.rem(r, 4)}
    bits = []
    while 2 ** (len(bits) + 1) < seqs:
        bits.append(2 ** (len(bits) + 1))
    finals = bits + [1]

    barrier = pltpu.get_barrier_semaphore()
    partners = [core_id, y_id] + [z_id(d) for d in range(1, levels)] + [flip(b) for b in finals]
    for partner in partners:
        pl.semaphore_signal(barrier, inc=1, device_id=partner, device_id_type=MESH)
    pl.semaphore_wait(barrier, len(partners))

    piece = q_rows // 4
    n_qkv, n_out, n_in, n_back = 3 * width // 512, width // 512, ff // 512, width // 128
    n_first = n_qkv + n_out
    n_mlp = n_first + n_in
    assert n_first == n_in
    ready = lambda k: (k < n_mlp) & (lax.rem(k, 2) == 0)
    total = n_mlp + n_back
    own_rows = pl.ds(pl.multiple_of(odd * edge, edge), region)
    c_mine = pl.ds(pl.multiple_of(odd * (q_rows - edge), edge), edge)
    c_other = pl.ds(pl.multiple_of((1 - odd) * (q_rows - edge), edge), edge)

    def remote(src, dst, stage, slot, target):
        return pltpu.make_async_remote_copy(src, dst, send_sem.at[stage, slot], recv_sem.at[stage, slot],
                                            device_id=target, device_id_type=MESH)

    def core_copy(k):
        return remote(buf.at[lax.rem(k, RING), :, 1 - core], core_recv.at[lax.rem(k, SLOTS)], 0, lax.rem(k, SLOTS), core_id)

    def x_copy(k):
        t = lax.rem(k, SLOTS)
        return remote(chip.at[t, :, :, c_other], x_recv.at[t], 1, t, flip(1))

    def y_copy(k):
        t = lax.rem(k, SLOTS)
        return remote(chip.at[t, :, 1 - y, own_rows], y_recv.at[t], 2, t, y_id)

    def z_copy(k, d):
        t = lax.rem(k, SLOTS)
        return pltpu.make_async_remote_copy(part.at[t, z_of(d)], z_recv.at[t, d - 1], zsend_sem.at[d - 1, t],
                                            zrecv_sem.at[d - 1, t], device_id=z_id(d), device_id_type=MESH)

    def fin_copy(k, i):
        t = lax.rem(k, SLOTS)
        return remote(fin.at[t, i], fin_recv.at[t, i], 3 + i, t, flip(finals[i]))

    def load_copies(source, col, k):
        slot = lax.rem(k, RING)
        return [pltpu.make_async_copy(source.at[:, :, :, pl.ds(pl.multiple_of(col + 128 * j, 128), 128)],
                                      buf.at[slot, :, :, pl.ds(j * piece, piece)], load_sem.at[j]) for j in range(4)]

    def load(k):
        for i, source in enumerate((g_q, g_k, g_v, g_out)):
            @pl.when(ready(k) & (k // 2 >= i * n_out) & (k // 2 < (i + 1) * n_out))
            def _():
                for copy in load_copies(source, (k // 2 - i * n_out) * 512, k):
                    copy.start()

    def weights(j):
        t = lax.rem(j, 2)
        cols = pl.ds(pl.multiple_of(j * 512, 512), 512)
        return [pltpu.make_async_copy(w_in.at[:, cols], win_buf.at[t], w_sem.at[0, t]),
                pltpu.make_async_copy(w_back.at[cols, :], wback_buf.at[t], w_sem.at[1, t])]

    starts = [pltpu.make_async_copy(base_out, acc_out, acc_sem.at[0]), pltpu.make_async_copy(base_dn, d_normed, acc_sem.at[1])]
    late = [pltpu.make_async_copy(normed_t_hbm, normed_t, late_sem.at[0]), pltpu.make_async_copy(x_hbm, x_ref, late_sem.at[1]),
            pltpu.make_async_copy(grad_t_hbm, grad_t, late_sem.at[2])]
    for copy in weights(0) + starts + late:
        copy.start()
    load(0)

    def mlp_rows(j, i):
        t = lax.rem(j, 2)
        cols = pl.ds(pl.multiple_of(j * 512, 512), 512)
        tall = tokens // 2
        block = slice(i * tall, (i + 1) * tall)
        if i == 0:
            @pl.when(j == 0)
            def _():
                for copy in starts:
                    copy.wait()
            for copy in weights(j):
                copy.wait()

            @pl.when(j + 1 < n_in)
            def _():
                for copy in weights(j + 1):
                    copy.start()
        pre = dot_n(normed[block, :], win_buf[t]) + b_in[:, cols]
        up = dot_t(grad[block, :], wback_buf[t])
        square = pre * pre
        turn = jnp.tanh(pre * (GELU_COEF + (GELU_COEF * 0.044715) * square))
        half = 0.5 + 0.5 * turn
        hid = (pre * half).astype(bf)
        slope = half + (0.5 * pre) * (1.0 - turn * turn) * (GELU_COEF + (3 * 0.044715 * GELU_COEF) * square)
        down = (up * slope).astype(bf)
        hidden[block, cols] = hid
        d_pre[block, :] = down
        acc_out[block, :] += dot_n(hid, wback_buf[t])
        d_normed[block, :] += dot_t(down, win_buf[t])
        sums = jnp.sum(down.astype(f32), axis=0, keepdims=True)
        place = (pl.ds(3 + j // 2, 1), pl.ds(pl.multiple_of(lax.rem(j, 2) * 512, 512), 512))
        vec[place] = sums if i == 0 else vec[place] + sums

    def mlp_grads(j):
        @pl.when(j == 0)
        def _():
            late[0].wait()
        slot = lax.rem(2 * j + 1, RING)
        per = 8
        big = per * width // rows

        def grads_step(i, _):
            value = dot_n(normed_t[pl.ds(pl.multiple_of(i * big, big), big), :], d_pre[...]).astype(bf)
            for m in range(per):
                for a in range(4):
                    buf[slot, i * (per // 2) + m // 2, m % 2, a * piece:(a + 1) * piece, :] = (
                        value[m * piece:(m + 1) * piece, a * 128:(a + 1) * 128])
            return 0
        lax.fori_loop(0, rows // per, grads_step, 0)

    tall_end = tokens // 4

    def returned_copy(i):
        return pltpu.make_async_copy(returned.at[pl.ds(pl.multiple_of(i * tall_end, tall_end), tall_end)], came, came_sem)

    def done_copies(i):
        block = pl.ds(i * tall_end if isinstance(i, int) else pl.multiple_of(i * tall_end, tall_end), tall_end)
        return [pltpu.make_async_copy(block_out.at[block], block_hbm.at[block], done_sem.at[0, i]),
                pltpu.make_async_copy(d_normed.at[block], input_hbm.at[block], done_sem.at[1, i])]

    def finish_tokens(i):
        @pl.when(i == 0)
        def _():
            returned_copy(0).start()
            vec[0:2, :] = vec_in[...]
            vec[2:3, :] = jnp.zeros((1, width), f32)
            vec[7:8, :] = jnp.zeros((1, width), f32)
        returned_copy(i).wait()
        small = tall_end // 4

        def part(n, sums):
            gain, bias, back = sums
            block = pl.ds(pl.multiple_of(i * tall_end + n * small, small), small)
            block_out[block, :] = acc_out[block, :].astype(bf)
            values = x_ref[block, :].astype(f32)
            centered = values - jnp.mean(values, axis=1, keepdims=True)
            scale = lax.rsqrt(jnp.mean(centered * centered, axis=1, keepdims=True) + EPS)
            unit = centered * scale
            d = d_normed[block, :]
            g = grad[block, :].astype(f32)
            d_unit = (d + came[pl.ds(pl.multiple_of(n * small, small), small), :].astype(f32)) * gain_in[...]
            inner = jnp.mean(d_unit * unit, axis=1, keepdims=True)
            d_normed[block, :] = g + (d_unit - jnp.mean(d_unit, axis=1, keepdims=True) - unit * inner) * scale
            return (gain + jnp.sum(d * unit, axis=0, keepdims=True), bias + jnp.sum(d, axis=0, keepdims=True),
                    back + jnp.sum(g, axis=0, keepdims=True))
        sums = lax.fori_loop(0, 4, part, (vec[0:1, :], vec[1:2, :], vec[2:3, :]))
        for row in range(3):
            vec[row:row + 1, :] = sums[row]
        for copy in done_copies(i):
            copy.start()

        @pl.when(i < 3)
        def _():
            returned_copy(i + 1).start()

    def back_grads(j):
        value = dot_n(grad_t[pl.ds(pl.multiple_of(j * 128, 128), 128), :], hidden[...]).astype(bf)
        slot = lax.rem(n_mlp + j, RING)
        parts = q_rows // 128
        for d in range(rows):
            for a in range(parts):
                buf[slot, d // 2, d % 2, a * 128:(a + 1) * 128, :] = value[:, (d * parts + a) * 128:(d * parts + a + 1) * 128]

    def vec_copy(i, target):
        return pltpu.make_async_remote_copy(vec, vec_recv.at[i], vsend_sem.at[i], vrecv_sem.at[i],
                                            device_id=target, device_id_type=MESH)
    vec_stages = [[(0, core_id)], [(1, y_id)], [(2 + d - 1, z_id(d)) for d in range(1, levels)]]
    vec_stages += [[(1 + levels + i, flip(b))] for i, b in enumerate(finals)]

    def store(k):
        def place(out, col):
            for j in range(4):
                out[:, pl.ds(pl.multiple_of(col + 128 * j, 128), 128)] = res[j * piece:(j + 1) * piece, :]

        @pl.when(ready(k) & (k < 2 * n_qkv))
        def _():
            place(o_qkv, (k // 2) * 512)

        @pl.when(ready(k) & (k >= 2 * n_qkv))
        def _():
            place(o_out, (k // 2 - n_qkv) * 512)

        @pl.when((k < n_mlp) & (lax.rem(k, 2) == 1))
        def _():
            place(o_in, (k // 2) * 512)

        @pl.when(k >= n_mlp)
        def _():
            for a in range(q_rows // 128):
                o_back[a * 128:(a + 1) * 128, pl.ds(pl.multiple_of((k - n_mlp) * 128, 128), 128)] = (
                    res[a * 128:(a + 1) * 128, :].T)

    def stage(lag, it, body):
        k = it - lag

        @pl.when((k >= 0) & (k < total))
        def _():
            body(k, lax.rem(k, SLOTS))

    def send_first(k, t):
        @pl.when(ready(k))
        def _():
            for copy in load_copies(g_q, 0, k):
                copy.wait()
        load(k + 1)
        core_copy(k).start()

    def core_add(k, t):
        core_copy(k).wait()
        slot = lax.rem(k, RING)
        for i in range(rows // 2):
            chip[t, i // 2, i % 2] = buf[slot, i, core] + core_recv[t, i]
        x_copy(k).start()

    def x_add(k, t):
        x_copy(k).wait()
        for i in range(rows // 2):
            chip[t, i // 2, i % 2, c_mine] = chip[t, i // 2, i % 2, c_mine] + x_recv[t, i // 2, i % 2]
        y_copy(k).start()

    def y_add(k, t):
        y_copy(k).wait()
        for i in range(levels):
            part[t, i] = chip[t, i, y, own_rows] + y_recv[t, i]
        for d in range(1, levels):
            z_copy(k, d).start()

    def z_add(k, t):
        for d in range(1, levels):
            z_copy(k, d).wait()
        value = part[t, z].astype(f32)
        for d in range(1, levels):
            value = value + z_recv[t, d - 1].astype(f32)
        fin[t, 0] = value.astype(bf)
        fin_copy(k, 0).start()

    def fin_add(i):
        def body(k, t):
            fin_copy(k, i).wait()
            fin[t, i + 1] = fin[t, i] + fin_recv[t, i]
            fin_copy(k, i + 1).start()
        return body

    def last(k, t):
        i = len(finals) - 1
        fin_copy(k, i).wait()
        middle = q_rows - 2 * edge
        at = lambda start, size: pl.ds(pl.multiple_of(start, edge), size)
        res[c_mine, :] = fin[t, i, at(odd * middle, edge)].astype(f32)
        res[c_other, :] = fin_recv[t, i, at((1 - odd) * middle, edge)].astype(f32)
        res[edge:q_rows - edge, :] = (fin[t, i, at((1 - odd) * edge, middle)].astype(f32)
                                      + fin_recv[t, i, at(odd * edge, middle)].astype(f32))
        store(k)

    pipeline = [send_first, core_add, x_add, y_add, z_add] + [fin_add(i) for i in range(len(bits))] + [last]

    def step(it, _):
        for lag, body in enumerate(pipeline):
            stage(2 * lag, it, body)

        @pl.when((it < n_mlp) & (lax.rem(it, 2) == 0))
        def _():
            mlp_rows(it // 2, 1)
            mlp_grads(it // 2)

        @pl.when((it < n_mlp - 1) & (lax.rem(it, 2) == 1))
        def _():
            mlp_rows(it // 2 + 1, 0)

        @pl.when(it == n_mlp - 1)
        def _():
            for copy in late[1:]:
                copy.wait()

        @pl.when((it >= n_mlp - 1) & (it < n_mlp + 3))
        def _():
            finish_tokens(it - (n_mlp - 1))

        @pl.when(it == n_mlp + 2)
        def _():
            for i, target in vec_stages[0]:
                vec_copy(i, target).start()
        for number, stages in enumerate(vec_stages):
            @pl.when(it == n_mlp + 4 + 2 * number)
            def _():
                for i, target in stages:
                    vec_copy(i, target).wait()
                value = vec[...]
                for i, target in stages:
                    value = value + vec_recv[i]
                if number + 1 < len(vec_stages):
                    vec[...] = value
                    for i, target in vec_stages[number + 1]:
                        vec_copy(i, target).start()
                else:
                    o_vec[...] = value

        @pl.when((it >= n_mlp - 1) & (it < total - 1))
        def _():
            back_grads(it - (n_mlp - 1))
        return 0
    mlp_rows(jnp.int32(0), 0)
    lax.fori_loop(0, total + 2 * len(pipeline) - 2, step, 0)
    for i in range(4):
        for copy in done_copies(i):
            copy.wait()


def reduce_all(rows, seqs, g_q, g_k, g_v, g_out, normed, normed_t, grad, grad_t, x, w_in, w_back, b_in, base_out, base_dn, vec_in, gain,
               returned):
    tokens, width = normed.shape
    ff = w_in.shape[1]
    share = width // rows
    q_rows = 4 * share
    edge = q_rows // 4
    levels = rows // 4
    region = q_rows - edge
    finals = max(1, (seqs - 1).bit_length())
    bf, f32 = jnp.bfloat16, jnp.float32
    vmem, hbm = pl.BlockSpec(memory_space=pltpu.VMEM), pl.BlockSpec(memory_space=pl.ANY)
    dma = pltpu.SemaphoreType.DMA
    return pl.pallas_call(
        functools.partial(reduce_kernel, (rows, seqs, q_rows, edge, tokens, width, ff)),
        out_shape=[jax.ShapeDtypeStruct((share, 3 * width), f32), jax.ShapeDtypeStruct((share, width), f32),
                   jax.ShapeDtypeStruct((share, ff), f32), jax.ShapeDtypeStruct((ff // rows, width), f32),
                   jax.ShapeDtypeStruct((8, width), f32), jax.ShapeDtypeStruct((tokens, width), bf),
                   jax.ShapeDtypeStruct((tokens, width), f32)],
        in_specs=[hbm, hbm, hbm, hbm, vmem, hbm, vmem, hbm, hbm, hbm, hbm, vmem, hbm, hbm, vmem, vmem, hbm],
        out_specs=[vmem] * 5 + [hbm] * 2,
        scratch_shapes=[
            pltpu.VMEM((RING, rows // 2, 2, q_rows, 128), bf),
            pltpu.VMEM((SLOTS, rows // 2, q_rows, 128), bf),
            pltpu.VMEM((SLOTS, levels, 2, q_rows, 128), bf),
            pltpu.VMEM((SLOTS, levels, 2, edge, 128), bf),
            pltpu.VMEM((SLOTS, levels, region, 128), bf),
            pltpu.VMEM((SLOTS, levels, region, 128), bf),
            pltpu.VMEM((SLOTS, levels - 1, region, 128), bf),
            pltpu.VMEM((SLOTS, finals, region, 128), bf),
            pltpu.VMEM((SLOTS, finals, region, 128), bf),
            pltpu.VMEM((q_rows, 128), f32),
            pltpu.VMEM((tokens, width), f32),
            pltpu.VMEM((tokens, ff), bf),
            pltpu.VMEM((tokens, 512), bf),
            pltpu.VMEM((2, width, 512), bf),
            pltpu.VMEM((2, 512, width), bf),
            pltpu.VMEM((width, tokens), bf),
            pltpu.VMEM((width, tokens), bf),
            pltpu.VMEM((tokens, width), bf),
            pltpu.VMEM((tokens, width), bf),
            pltpu.VMEM((tokens, width), f32),
            pltpu.VMEM((tokens // 4, width), bf),
            pltpu.VMEM((8, width), f32),
            pltpu.VMEM((1 + levels + finals, 8, width), f32),
            dma((3,)), dma((2, 4)), dma,
            dma((4,)), dma((2,)), dma((2, 2)), dma((3 + finals, SLOTS)), dma((3 + finals, SLOTS)),
            dma((levels - 1, SLOTS)), dma((levels - 1, SLOTS)), dma((1 + levels + finals,)), dma((1 + levels + finals,)),
        ],
        compiler_params=pltpu.CompilerParams(collective_id=1, has_side_effects=True, vmem_limit_bytes=62 * 2**20),
        cost_estimate=pl.CostEstimate(flops=100 * 10**9, bytes_accessed=100 * 2**20, transcendentals=0),
        name="reduce",
    )(*[g.reshape(rows // 2, 2, share, width) for g in (g_q, g_k, g_v, g_out)], normed, normed_t, grad, grad_t, x,
      w_in, w_back, b_in, base_out, base_dn, vec_in, gain, returned)


def body(block_input, lengths, norm_gain, norm_bias, w_qkv, w_attn_out, w_fc_in, b_fc_in, w_fc_out, b_fc_out, cotangent):
    f32, bf = jnp.float32, jnp.bfloat16
    rows, seqs = lax.axis_size("rows"), lax.axis_size("seq")
    inputs = block_input[0].astype(f32)
    tokens, width = inputs.shape
    own_lengths = lengths[0]
    count = own_lengths.shape[0]
    first = lax.axis_index("seq") * tokens
    index = first + jnp.arange(tokens, dtype=jnp.int32)
    order = np.arange(count)
    ends = jnp.sum(jnp.where(order[None, :] <= order[:, None], own_lengths[None, :], 0), axis=1)
    begin = jnp.sum(jnp.where(ends[None, :] <= index[:, None], own_lengths[None, :], 0), axis=1)
    starts = begin - first + tokens
    lows = starts[::BQ] // BQ

    share, wide = width // rows, 4 * width // rows
    r = lax.axis_index("rows")
    grad_out = cotangent[0]
    (w_out_all, w_qkv_all, normed, normed_prior, turned_own, turned_prior, grad_turned, mixed, d_attended, prior_input,
     cosine, sine, vectors) = gather_all(
        rows, seqs, w_attn_out, w_qkv, block_input[0], grad_out, (norm_gain, norm_bias, b_fc_out, b_fc_in), lengths)
    w_fc_in, w_fc_out, vectors = lax.optimization_barrier((w_fc_in, w_fc_out, vectors))
    w_in_all = lax.all_gather(w_fc_in, "rows", axis=0, tiled=True)
    w_back_all = lax.all_gather(w_fc_out, "rows", axis=0, tiled=True)
    gain, bias, b_back_all = vectors[0], vectors[1], vectors[2]
    b_in_all = vectors[3:7].reshape(1, 4 * width)
    prior_unit, _ = layer_norm_stats(prior_input.astype(f32))
    attended, attended_turned, d_q, d_k, d_v = attention(lows, starts, cosine, sine, mixed, d_attended)

    w_k, w_v = w_qkv_all[:, width:2 * width].T, w_qkv_all[:, 2 * width:].T
    d_prior = jnp.dot(d_k[:tokens], w_k, preferred_element_type=f32) + jnp.dot(d_v[:tokens], w_v, preferred_element_type=f32)
    back = lax.ppermute(d_prior.astype(bf), "seq", [(i + 1, i) for i in range(seqs - 1)])
    vec_in = jnp.stack([jnp.sum(d_prior * prior_unit, axis=0), jnp.sum(d_prior, axis=0)])
    product = lambda turned, values: jnp.dot(turned, values, preferred_element_type=f32)
    grads = [product(turned_own, d_q).astype(bf),
             (product(turned_own, d_k[tokens:]) + product(turned_prior, d_k[:tokens])).astype(bf),
             (product(turned_own, d_v[tokens:]) + product(turned_prior, d_v[:tokens])).astype(bf)]
    grad_w_out = product(attended_turned, grad_out).astype(bf)
    base_dn = (jnp.dot(d_k[tokens:], w_k, preferred_element_type=f32) + jnp.dot(d_v[tokens:], w_v, preferred_element_type=f32)
               + jnp.dot(d_q, w_qkv_all[:, :width].T, preferred_element_type=f32))
    base_out = inputs + jnp.dot(attended, w_out_all, preferred_element_type=f32) + b_back_all

    g_qkv, g_out, g_in, g_back, vec, block_output, grad_input = reduce_all(
        rows, seqs, *grads, grad_w_out, normed, turned_own, grad_out, grad_turned, block_input[0], w_in_all, w_back_all,
        b_in_all, base_out, base_dn, vec_in, gain[None], back)

    own = lambda vector, size: lax.dynamic_slice_in_dim(vector, r * size, size)
    return (block_output[None], grad_input[None], own(vec[0], share), own(vec[1], share), g_qkv, g_out, g_in,
            own(vec[3:7].reshape(4 * width), wide), g_back, own(vec[2], share))


def solution(mesh):
    vector, matrix, tokens = P("rows"), P("rows", None), P("rows", "seq", None)
    in_specs = (tokens, matrix, vector, vector, matrix, matrix, matrix, vector, matrix, vector, tokens)
    out_specs = (tokens, tokens, vector, vector, matrix, matrix, matrix, vector, matrix, vector)
    return jax.shard_map(body, mesh=mesh, in_specs=in_specs, out_specs=out_specs, check_vma=False)
```
